32 devices in a mesh: ha: 2 (over y), wa: 4 (over z), hd: 4 (over x, core).
Axes of the slice: x: 2, y: 2, z: 4, core: 2. Of those that a mesh axis runs over, the one named last changes fastest.
Arguments:
- q_raw: bfloat16 [2, 4, 128, 2560], P('ha', 'wa', None, 'hd')
- k_raw: bfloat16 [2, 4, 128, 2560], P('ha', 'wa', None, 'hd')
- values: bfloat16 [2, 4, 128, 2560], P('ha', 'wa', None, 'hd')
- upstream: bfloat16 [2, 4, 128, 2560], P('ha', 'wa', None, 'hd'), may hold values from -384 to 384
- outputs: bfloat16 [2, 4, 128, 2560], P('ha', 'wa', None, 'hd')
- logsumexp: float32 [2, 4, 20, 128], P('ha', 'wa', 'hd'), may hold values from 7.5 to 9.5
- gain_q: bfloat16 [2560], P('hd'), may hold values from 0.25 to 1.75
- gain_k: bfloat16 [2560], P('hd'), may hold values from 0.25 to 1.75
- far_list: int32 [2, 4, 12], P('ha'), may hold values from -1 to 15, as said below
Outputs:
- dq_raw: bfloat16 [2, 4, 128, 2560], P('ha', 'wa', None, 'hd')
- dk_raw: bfloat16 [2, 4, 128, 2560], P('ha', 'wa', None, 'hd')
- dv: bfloat16 [2, 4, 128, 2560], P('ha', 'wa', None, 'hd')
The draws below stay inside these ranges and needn't reach their ends.
Inputs may be any that keep to these rules, and one draw needn't show every extreme that they name: far_list[r, c, f] is -1 (an empty slot) or names key unit u of tile (r, u // 4); the named tiles lie two or more columns away from c, and each is named at most once in far_list[r, c].
All inputs are finite; a program needn't handle non-finite values.
Results may differ from the reference program's by a relative error of at most 0.0015.
The reference program's roundings to bfloat16 on the way (of `dscore`, `weight_low`, `dq_norm` and `dk_norm`) count: a program that leaves them out, or rounds other values in their place, can miss the bound.
Values may be sent and summed in bfloat16 or wider, within the bound.
A program may use at most 64 MiB of HBM per device.

```python
import math
import jax
import jax.numpy as jnp
from jax import lax

HEADS = 20
HEAD = 128
TOK_DEV = 128
UNITS = 4
FAR = 12
TROWS = 2
TCOLS = 4
HW = 2560
KB = 32


def ramp_draw(key):
    shape = (TROWS, TCOLS, TOK_DEV, HW)
    head_place = (jnp.arange(HW) // HEAD).astype(jnp.float32) / max(HEADS - 1, 1)
    parts = jax.random.split(key, 1)
    base = jax.random.normal(parts[0], shape, jnp.float32)
    ramp = jnp.exp(0.5 * math.log(3.0) * head_place)
    return (base * ramp).astype(jnp.bfloat16)


def draw_q_raw(key, part):
    return ramp_draw(jax.random.fold_in(key, 101))


def draw_k_raw(key, part):
    return ramp_draw(jax.random.fold_in(key, 202))


def channel_mean(key):
    return jax.random.normal(jax.random.fold_in(key, 303), (HW,), jnp.float32)


def noise_draw(key):
    shape = (TROWS, TCOLS, TOK_DEV, HW)
    return jax.random.normal(key, shape, jnp.float32)


def draw_values(key, part):
    return (channel_mean(key) + noise_draw(jax.random.fold_in(key, 404))).astype(jnp.bfloat16)


def draw_outputs(key, part):
    return (channel_mean(key) + 0.15 * noise_draw(jax.random.fold_in(key, 505))).astype(jnp.bfloat16)


def draw_far_list(key, part):
    parts = jax.random.split(jax.random.fold_in(key, 606), 4)
    owners = jnp.arange(TCOLS, dtype=jnp.int32)
    column = owners[None, :, None]
    peer = owners[None, None, :]
    popularity = jax.random.randint(parts[0], (TROWS, 1, TCOLS), 0, TCOLS)
    jitter = jax.random.randint(parts[1], (TROWS, TCOLS, TCOLS), 0, TCOLS)
    score = 2 * popularity + jitter
    eligible = jnp.abs(peer - column) >= 2
    score = jnp.where(eligible, score, 4 * TCOLS)
    forced = (column == 0) & (peer == TCOLS - 1)
    score = jnp.where(forced, -1, score)
    ranked = jnp.argsort(score * TCOLS + peer, axis=-1, stable=True).astype(jnp.int32)
    filler = jnp.zeros((TROWS, TCOLS, FAR), jnp.int32)
    ranked = jnp.concatenate([ranked, filler], axis=-1)[..., :FAR]
    available = jnp.broadcast_to(jnp.sum(eligible, axis=-1).astype(jnp.int32), (TROWS, TCOLS))
    wanted = jax.random.randint(parts[2], (TROWS, TCOLS), max(FAR - 2, 1), FAR + 1)
    wanted = jnp.where(owners[None, :] == 1, max(FAR - 2, 1), wanted)
    count = jnp.minimum(wanted, available)
    slot = jnp.arange(FAR, dtype=jnp.int32)
    unit = jax.random.randint(parts[3], (TROWS, TCOLS, FAR), 0, UNITS)
    unit = jnp.where((owners[None, :, None] == 0) & (slot[None, None, :] == 0), UNITS - 1, unit)
    return jnp.where(slot[None, None, :] < count[..., None], ranked * UNITS + unit, -1).astype(jnp.int32)


def shard_levels(own_key, extent, pieces, smallest, high):
    def one(position, blocks):
        draws = jax.random.uniform(jax.random.fold_in(jax.random.fold_in(own_key, 6), position), (blocks,), jnp.float32, smallest / len(pieces), high / len(pieces))
        return jnp.repeat(jnp.exp(draws), extent[position] // blocks).reshape((-1,) + (1,) * (len(extent) - position - 1))

    loudness = one(*pieces[0])
    for cut in pieces[1:]:
        loudness = loudness * one(*cut)
    return loudness


def bell_draw(key, extent, deviation, most, pieces=(), kind=jnp.bfloat16):
    result = jax.random.normal(key, extent, jnp.float32) * deviation
    if len(pieces) > 0:
        result = shard_levels(key, extent, pieces, -0.22, 0.18) * result
    return jnp.clip(result, min=-most, max=most).astype(kind)


def setup_inputs(seed: int = 0) -> dict:
    streams_of = jax.random.split(jax.random.key(seed), 10)
    return {
        "q_raw": draw_q_raw(jax.random.fold_in(streams_of[9], 71), 0),
        "k_raw": draw_k_raw(jax.random.fold_in(streams_of[9], 71), 0),
        "values": draw_values(jax.random.fold_in(streams_of[9], 71), 0),
        "upstream": bell_draw(streams_of[3], (TROWS, TCOLS, TOK_DEV, HW), 64.0, 384.0, ((0, 2), (1, 4), (3, 4))),
        "outputs": draw_outputs(jax.random.fold_in(streams_of[9], 71), 0),
        "logsumexp": jnp.clip(7.5 + 2.0 * jax.random.uniform(streams_of[5], (TROWS, TCOLS, HEADS, TOK_DEV), jnp.float32) ** shard_levels(streams_of[5], (TROWS, TCOLS, HEADS, TOK_DEV), ((0, 2), (1, 4), (2, 4)), -0.2, 0.2), 7.5, 9.5),
        "gain_q": jnp.clip(1.0 + 0.15 * jax.random.normal(streams_of[6], (HW,), jnp.float32), 0.25, 1.75).astype(jnp.bfloat16),
        "gain_k": jnp.clip(1.0 + 0.15 * jax.random.normal(streams_of[7], (HW,), jnp.float32), 0.25, 1.75).astype(jnp.bfloat16),
        "far_list": draw_far_list(jax.random.fold_in(streams_of[9], 71), 0),
    }


EPS = 1e-06
POSITIONS = ((1, 1), (0, 1), (2, 1), (1, 0), (1, 2))

def rounded(array):
    return lax.optimization_barrier(array.astype(jnp.bfloat16)).astype(jnp.float32)

def norm_rows(raw, gain):
    raw_wide = raw.astype(jnp.float32)
    rate = lax.rsqrt(lax.optimization_barrier(jnp.mean(raw_wide * raw_wide, axis=-1)) + EPS)
    return ((raw_wide * rate[..., None] * gain.astype(jnp.float32)).astype(jnp.bfloat16), rate)

def block_terms(queries, upstream_tile, lse_tile, delta_tile, keys, vals, key_valid):
    query_count = queries.shape[0]
    key_count = keys.shape[0]
    query_heads = queries.astype(jnp.float32).reshape(query_count, HEADS, HEAD)
    upstream_heads = upstream_tile.astype(jnp.float32).reshape(query_count, HEADS, HEAD)
    key_heads = keys.astype(jnp.float32).reshape(key_count, HEADS, HEAD)
    value_heads = vals.astype(jnp.float32).reshape(key_count, HEADS, HEAD)
    scores = jnp.einsum('ihd,jhd->hij', query_heads, key_heads) / math.sqrt(HEAD)
    weight = jnp.where(key_valid[None, None, :], jnp.exp(scores - lse_tile[:, :, None]), 0.0)
    dweight = jnp.einsum('ihd,jhd->hij', upstream_heads, value_heads)
    dscore = rounded(weight * (dweight - delta_tile[:, :, None]))
    weight_low = rounded(weight)
    return (query_heads, upstream_heads, key_heads, dscore, weight_low)

def query_side(queries, upstream_tile, lse_tile, delta_tile, keys, vals, key_valid):
    query_heads, upstream_heads, key_heads, dscore, weight_low = block_terms(queries, upstream_tile, lse_tile, delta_tile, keys, vals, key_valid)
    grads = jnp.einsum('hij,jhd->ihd', dscore, key_heads) / math.sqrt(HEAD)
    return grads.reshape(queries.shape[0], HW).astype(jnp.bfloat16)

def key_side(queries, upstream_tile, lse_tile, delta_tile, keys, vals, key_valid):
    query_heads, upstream_heads, key_heads, dscore, weight_low = block_terms(queries, upstream_tile, lse_tile, delta_tile, keys, vals, key_valid)
    key_grads = jnp.einsum('hij,ihd->jhd', dscore, query_heads) / math.sqrt(HEAD)
    value_grads = jnp.einsum('hij,ihd->jhd', weight_low, upstream_heads)
    count = keys.shape[0]
    return (key_grads.reshape(count, HW).astype(jnp.bfloat16), value_grads.reshape(count, HW).astype(jnp.bfloat16))

def pick(array, row, col):
    inner = lax.dynamic_index_in_dim(array, row, 0, keepdims=False)
    return lax.dynamic_index_in_dim(inner, col, 0, keepdims=False)

def tile_exists(row, col):
    return (row >= 0) & (row < TROWS) & (col >= 0) & (col < TCOLS)

def reference(q_raw, k_raw, values, upstream, outputs, logsumexp, gain_q, gain_k, far_list):
    query_norm, q_rate = norm_rows(q_raw, gain_q)
    key_norm, k_rate = norm_rows(k_raw, gain_k)
    product = upstream.astype(jnp.float32) * outputs.astype(jnp.float32)
    delta = lax.optimization_barrier(jnp.sum(product.reshape(TROWS, TCOLS, TOK_DEV, HEADS, HEAD), axis=-1)).transpose(0, 1, 3, 2)
    padding = ((1, 1), (1, 1), (0, 0), (0, 0))
    key_pad = jnp.pad(key_norm, padding)
    value_pad = jnp.pad(values, padding)
    query_pad = jnp.pad(query_norm, padding)
    upstream_pad = jnp.pad(upstream, padding)
    lse_pad = jnp.pad(logsumexp, padding)
    delta_pad = jnp.pad(delta, padding)

    def query_tile(flat):
        row = (flat // TCOLS).astype(jnp.int32)
        col = (flat % TCOLS).astype(jnp.int32)
        win_keys = jnp.concatenate([pick(key_pad, row + row_step, col + col_step) for row_step, col_step in POSITIONS], 0)
        win_vals = jnp.concatenate([pick(value_pad, row + row_step, col + col_step) for row_step, col_step in POSITIONS], 0)
        win_valid = jnp.concatenate([jnp.broadcast_to(tile_exists(row + row_step - 1, col + col_step - 1), (TOK_DEV,)) for row_step, col_step in POSITIONS], 0)
        listed = pick(far_list, row, col)
        safe = jnp.maximum(listed, 0)
        owner = (safe // UNITS).astype(jnp.int32)
        first = (safe % UNITS * KB).astype(jnp.int32)

        def one_unit(owner_col, start):
            unit_keys = lax.dynamic_slice_in_dim(pick(key_norm, row, owner_col), start, KB, 0)
            unit_vals = lax.dynamic_slice_in_dim(pick(values, row, owner_col), start, KB, 0)
            return (unit_keys, unit_vals)
        far_keys, far_vals = jax.vmap(one_unit)(owner, first)
        keys = jnp.concatenate([win_keys, far_keys.reshape(FAR * KB, HW)], 0)
        vals = jnp.concatenate([win_vals, far_vals.reshape(FAR * KB, HW)], 0)
        valid = jnp.concatenate([win_valid, jnp.repeat(listed >= 0, KB)], 0)
        return query_side(pick(query_norm, row, col), pick(upstream, row, col), pick(logsumexp, row, col), pick(delta, row, col), keys, vals, valid)
    tiles = jnp.arange(TROWS * TCOLS, dtype=jnp.int32)
    dq_norm = lax.map(query_tile, tiles).reshape(TROWS, TCOLS, TOK_DEV, HW)

    def key_tile(flat):
        row = (flat // TCOLS).astype(jnp.int32)
        col = (flat % TCOLS).astype(jnp.int32)
        own_keys = pick(key_norm, row, col)
        own_vals = pick(values, row, col)
        total_key = jnp.zeros((TOK_DEV, HW), jnp.float32)
        total_value = jnp.zeros((TOK_DEV, HW), jnp.float32)
        for row_step, col_step in POSITIONS:
            valid = jnp.broadcast_to(tile_exists(row + row_step - 1, col + col_step - 1), (TOK_DEV,))
            part_key, part_value = key_side(pick(query_pad, row + row_step, col + col_step), pick(upstream_pad, row + row_step, col + col_step), pick(lse_pad, row + row_step, col + col_step), pick(delta_pad, row + row_step, col + col_step), own_keys, own_vals, valid)
            total_key = total_key + part_key.astype(jnp.float32)
            total_value = total_value + part_value.astype(jnp.float32)

        def add_far(source, carry):
            sum_key, sum_value = carry
            source = jnp.asarray(source).astype(jnp.int32)
            listed = pick(far_list, row, source)
            asked = (listed >= 0) & (listed // UNITS == col)
            present = jnp.any(asked)
            unit = jnp.sum(jnp.where(asked, listed % UNITS, 0)).astype(jnp.int32)
            unit_keys = lax.dynamic_slice_in_dim(own_keys, unit * KB, KB, 0)
            unit_vals = lax.dynamic_slice_in_dim(own_vals, unit * KB, KB, 0)
            part_key, part_value = key_side(pick(query_norm, row, source), pick(upstream, row, source), pick(logsumexp, row, source), pick(delta, row, source), unit_keys, unit_vals, jnp.broadcast_to(present, (KB,)))
            place = (jnp.arange(UNITS, dtype=jnp.int32) == unit).astype(jnp.float32)
            sum_key = sum_key + place[:, None, None] * part_key.astype(jnp.float32)[None]
            sum_value = sum_value + place[:, None, None] * part_value.astype(jnp.float32)[None]
            return (sum_key, sum_value)
        empty = jnp.zeros((UNITS, KB, HW), jnp.float32)
        far_key, far_value = lax.fori_loop(0, TCOLS, add_far, (empty, empty))
        key_grad = (total_key + far_key.reshape(TOK_DEV, HW)).astype(jnp.bfloat16)
        value_grad = (total_value + far_value.reshape(TOK_DEV, HW)).astype(jnp.bfloat16)
        return (key_grad, value_grad)
    dk_norm, dv = lax.map(key_tile, tiles)
    dk_norm = dk_norm.reshape(TROWS, TCOLS, TOK_DEV, HW)
    dv = dv.reshape(TROWS, TCOLS, TOK_DEV, HW)
    gain_qw = gain_q.astype(jnp.float32)
    gain_kw = gain_k.astype(jnp.float32)
    q_wide = q_raw.astype(jnp.float32)
    k_wide = k_raw.astype(jnp.float32)
    dq_wide = dq_norm.astype(jnp.float32)
    dk_wide = dk_norm.astype(jnp.float32)
    q_dot = lax.optimization_barrier(jnp.sum(gain_qw * dq_wide * q_wide, axis=-1))
    k_dot = lax.optimization_barrier(jnp.sum(gain_kw * dk_wide * k_wide, axis=-1))
    dq_raw = (q_rate[..., None] * gain_qw * dq_wide - q_wide * (q_rate ** 3 * q_dot / HW)[..., None]).astype(jnp.bfloat16)
    dk_raw = (k_rate[..., None] * gain_kw * dk_wide - k_wide * (k_rate ** 3 * k_dot / HW)[..., None]).astype(jnp.bfloat16)
    return (dq_raw, dk_raw, dv)
```

```python
import functools
import math

import jax
import jax.numpy as jnp
from jax import lax
from jax.experimental import pallas as pl
from jax.experimental.pallas import tpu as pltpu
from jax.sharding import PartitionSpec as P

UNITS = 4
EPS = 1e-06
MESH = pl.DeviceIdType.MESH
LAST = (((1,), (1,)), ((), ()))
FIRST = (((0,), (0,)), ((), ()))
PLAIN = (((1,), (0,)), ((), ()))
UP, DOWN, LEFT, RIGHT = range(4)
F32 = jnp.float32
BF16 = jnp.bfloat16


def dot(a, b, dims):
    return lax.dot_general(a, b, dims, preferred_element_type=F32)


def kernel(
    sizes,
    q_hbm,
    k_hbm,
    v_hbm,
    u_hbm,
    o_hbm,
    lse_ref,
    gain_q_ref,
    gain_k_ref,
    far_ref,
    dq_out,
    dk_out,
    dv_out,
    q_raw,
    k_raw,
    vals,
    ups,
    outs,
    qn,
    kn,
    stats,
    nbr_stats,
    dq_acc,
    nbr,
    far_pack,
    far_in,
    ret_out,
    ret_in,
    fret_out,
    fret_in,
    total,
    xbuf,
    load_sem,
    nbr_send,
    nbr_recv,
    far_send,
    far_recv,
    ret_send,
    ret_recv,
    fret_send,
    fret_recv,
    x_send,
    x_recv,
):
    rows, cols, parts = sizes
    row = lax.axis_index("ha")
    col = lax.axis_index("wa")
    me = lax.axis_index("hd")
    tokens, width = q_raw.shape
    heads = lse_ref.shape[1]
    hw = width // heads
    kb = tokens // UNITS
    full_width = width * parts
    slots = far_ref.shape[2]
    score_scale = 1.0 / math.sqrt(hw)
    head_lanes = [slice(head * hw, (head + 1) * hw) for head in range(heads)]

    loads = []
    for index, (source, target) in enumerate(
        ((u_hbm, ups), (k_hbm, k_raw), (q_hbm, q_raw), (o_hbm, outs), (v_hbm, vals))
    ):
        copy = pltpu.make_async_copy(source.at[0, 0], target, load_sem.at[index])
        copy.start()
        loads.append(copy)

    exists = (row > 0, row < rows - 1, col > 0, col < cols - 1)
    ids = ({"ha": row - 1}, {"ha": row + 1}, {"wa": col - 1}, {"wa": col + 1})
    inner = (col > 0) & (col < cols - 1)
    far_tiles = range(1, cols - 1)

    barrier = pltpu.get_barrier_semaphore()
    hd_ids = [{"hd": lax.rem(me + off, parts)} for off in range(1, parts)]
    for target in hd_ids:
        pl.semaphore_signal(barrier, inc=1, device_id=target, device_id_type=MESH)
    for side in (UP, DOWN):

        @pl.when(exists[side])
        def _(side=side):
            pl.semaphore_signal(barrier, inc=1, device_id=ids[side], device_id_type=MESH)

    for off in range(1, cols):
        pl.semaphore_signal(
            barrier, inc=1, device_id={"wa": lax.rem(col + off, cols)}, device_id_type=MESH
        )

    def lane_columns(columns):
        lane = lax.broadcasted_iota(jnp.int32, (tokens, 128), 1)
        mat = jnp.zeros((tokens, 128), F32)
        for place, column in columns:
            mat = jnp.where(lane == place, column, mat)
        return mat.T

    def row_sums(block):
        acc = block[:, :hw]
        for lanes in head_lanes[1:]:
            acc = acc + block[:, lanes]
        return jnp.sum(acc, axis=1, keepdims=True)

    def to_columns(rows8):
        return jnp.concatenate([rows8] * (tokens // 8), axis=0).T

    def x_copy(which, off):
        return pltpu.make_async_remote_copy(
            src_ref=xbuf.at[which, me],
            dst_ref=xbuf.at[which, me],
            send_sem=x_send.at[which, off],
            recv_sem=x_recv.at[which, off],
            device_id=hd_ids[off - 1],
            device_id_type=MESH,
        )

    def x_start(which, rows8):
        xbuf[which, me] = rows8
        for off in range(1, parts):
            x_copy(which, off).start()

    def x_finish(which):
        for off in range(1, parts):
            x_copy(which, off).wait()
        acc = xbuf[which, 0]
        for part in range(1, parts):
            acc = acc + xbuf[which, part]
        return acc

    def side_id(side):
        if isinstance(side, int):
            return ids[side]
        return {"wa": jnp.where(side == RIGHT, col + 1, col - 1)}

    def nbr_copy(side, which):
        if which == 2:
            source, target = stats, nbr_stats.at[side ^ 1]
        else:
            source, target = (qn, ups)[which], nbr.at[side ^ 1, which]
        return pltpu.make_async_remote_copy(
            src_ref=source,
            dst_ref=target,
            send_sem=nbr_send.at[side, which],
            recv_sem=nbr_recv.at[side ^ 1, which],
            device_id=ids[side],
            device_id_type=MESH,
        )

    def nbr_wait(side, which):
        if which == 2:
            source, target = stats, nbr_stats.at[side]
        else:
            source, target = (qn, ups)[which], nbr.at[side, which]
        pltpu.make_async_remote_copy(
            src_ref=source,
            dst_ref=target,
            send_sem=nbr_send.at[0, which],
            recv_sem=nbr_recv.at[side, which],
            device_id=side_id(side),
            device_id_type=MESH,
        ).wait_recv()

    def far_copy(tile):
        return pltpu.make_async_remote_copy(
            src_ref=far_pack.at[tile],
            dst_ref=far_in.at[col],
            send_sem=far_send.at[tile],
            recv_sem=far_recv.at[col],
            device_id={"wa": tile},
            device_id_type=MESH,
        )

    def far_wait(peer):
        pltpu.make_async_remote_copy(
            src_ref=far_pack.at[0],
            dst_ref=far_in.at[peer],
            send_sem=far_send.at[0],
            recv_sem=far_recv.at[peer],
            device_id={"wa": peer},
            device_id_type=MESH,
        ).wait_recv()

    def ret_copy(side):
        return pltpu.make_async_remote_copy(
            src_ref=ret_out.at[side],
            dst_ref=ret_in.at[side ^ 1],
            send_sem=ret_send.at[side],
            recv_sem=ret_recv.at[side ^ 1],
            device_id=side_id(side),
            device_id_type=MESH,
        )

    def ret_wait(side):
        pltpu.make_async_remote_copy(
            src_ref=ret_out.at[side],
            dst_ref=ret_in.at[side],
            send_sem=ret_send.at[side],
            recv_sem=ret_recv.at[side],
            device_id=ids[side],
            device_id_type=MESH,
        ).wait_recv()

    def fret_copy(peer):
        return pltpu.make_async_remote_copy(
            src_ref=fret_out.at[peer],
            dst_ref=fret_in.at[col],
            send_sem=fret_send.at[peer],
            recv_sem=fret_recv.at[col],
            device_id={"wa": peer},
            device_id_type=MESH,
        )

    def fret_wait(tile):
        pltpu.make_async_remote_copy(
            src_ref=fret_out.at[tile],
            dst_ref=fret_in.at[tile],
            send_sem=fret_send.at[tile],
            recv_sem=fret_recv.at[tile],
            device_id={"wa": tile},
            device_id_type=MESH,
        ).wait_recv()

    loads[0].wait()
    pl.semaphore_wait(
        barrier,
        parts
        - 1
        + jnp.minimum(row, 1)
        + jnp.minimum(rows - 1 - row, 1)
        + (cols - 1),
    )
    for side in (LEFT, RIGHT, UP, DOWN):

        @pl.when(exists[side])
        def _(side=side):
            nbr_copy(side, 1).start()

    loads[1].wait()
    key_wide = k_raw[...].astype(F32)
    key_squares = row_sums(key_wide * key_wide)
    loads[2].wait()
    query_wide = q_raw[...].astype(F32)
    query_squares = row_sums(query_wide * query_wide)
    x_start(0, lane_columns([(0, query_squares), (1, key_squares)])[0:8])

    loads[3].wait()
    delta_columns = []
    for head, lanes in enumerate(head_lanes):
        product = ups[:, lanes].astype(F32) * outs[:, lanes].astype(F32)
        delta_columns.append((head, jnp.sum(product, axis=1, keepdims=True)))
    stats[0] = lane_columns(delta_columns)[0 : stats.shape[1]]
    for head in range(heads):
        stats[1, head : head + 1, :] = lse_ref[0, head]
    for side in (LEFT, RIGHT, UP, DOWN):

        @pl.when(exists[side])
        def _(side=side):
            nbr_copy(side, 2).start()

    send_unit = []
    send_used = []
    for tile in far_tiles:
        unit = jnp.int32(0)
        asked = jnp.int32(0)
        for slot in range(slots):
            named = jnp.where(col > tile, far_ref[0, tile - 1, slot], far_ref[0, tile + 1, slot])
            wanted = named - col * UNITS
            hit = (wanted >= 0) & (wanted < UNITS)
            unit = jnp.where(hit, wanted, unit)
            asked = jnp.where(hit, 1, asked)
        send_unit.append(unit)
        send_used.append(asked)

    def pick_unit(unit_wanted, source):
        wanted = jnp.full((kb, width), unit_wanted, jnp.int32)
        picked = source[0:kb, :].astype(F32)
        for unit in range(1, UNITS):
            block = source[unit * kb : (unit + 1) * kb, :].astype(F32)
            picked = jnp.where(wanted == unit, block, picked)
        return picked.astype(BF16)

    loads[4].wait()
    for index, tile in enumerate(far_tiles):

        @pl.when(tile != col)
        def _(index=index, tile=tile):
            far_pack[tile, 1] = pick_unit(send_unit[index], vals)

    gain_q = gain_q_ref[...].astype(F32).reshape(1, width)
    gain_k = gain_k_ref[...].astype(F32).reshape(1, width)
    rates = lax.rsqrt(x_finish(0) / full_width + EPS)
    rate_columns = to_columns(rates)
    q_rate = rate_columns[:, 0:1]
    k_rate = rate_columns[:, 1:2]
    qn[...] = (q_raw[...].astype(F32) * q_rate * gain_q).astype(BF16)
    for side in (LEFT, RIGHT, UP, DOWN):

        @pl.when(exists[side])
        def _(side=side):
            nbr_copy(side, 0).start()

    kn[...] = (k_raw[...].astype(F32) * k_rate * gain_k).astype(BF16)
    for index, tile in enumerate(far_tiles):

        @pl.when(tile != col)
        def _(index=index, tile=tile):
            far_pack[tile, 0] = pick_unit(send_unit[index], kn)
            far_copy(tile).start()

    def attend(keys, values, queries, upstream, delta_row, lse_row, used=None):
        weight = jnp.exp(dot(keys, queries, LAST) * score_scale - lse_row)
        if used is not None:
            weight = jnp.where(jnp.full(weight.shape, used, jnp.int32) > 0, weight, 0.0)
        dweight = dot(values, upstream, LAST)
        dscore = (weight * (dweight - delta_row)).astype(BF16)
        dq_part = dot(dscore, keys, FIRST)
        dk_part = (dot(dscore, queries, PLAIN) * score_scale).astype(BF16)
        dv_part = dot(weight.astype(BF16), upstream, PLAIN).astype(BF16)
        return dq_part, dk_part, dv_part

    for head, lanes in enumerate(head_lanes):
        dq_part, dk_part, dv_part = attend(
            kn[:, lanes],
            vals[:, lanes],
            qn[:, lanes],
            ups[:, lanes],
            stats[0, head : head + 1, :],
            stats[1, head : head + 1, :],
        )
        dq_acc[:, lanes] = dq_part
        total[0, :, lanes] = dk_part.astype(F32)
        total[1, :, lanes] = dv_part.astype(F32)

    def side_pass(side):
        for which in (1, 2, 0):
            nbr_wait(side, which)
        for head, lanes in enumerate(head_lanes):
            dq_part, dk_part, dv_part = attend(
                kn[:, lanes],
                vals[:, lanes],
                nbr[side, 0, :, lanes],
                nbr[side, 1, :, lanes],
                nbr_stats[side, 0, head : head + 1, :],
                nbr_stats[side, 1, head : head + 1, :],
            )
            ret_out[side, :, lanes] = dq_part
            total[0, :, lanes] += dk_part.astype(F32)
            total[1, :, lanes] += dv_part.astype(F32)

    def far_pass(peer):
        side = jnp.where(peer > col, LEFT, RIGHT)
        query_col = jnp.where(peer > col, col - 1, col + 1)
        used = jnp.int32(0)
        for slot in range(slots):
            named = far_ref[0, query_col, slot] - peer * UNITS
            used = jnp.where((named >= 0) & (named < UNITS), 1, used)
        far_wait(peer)
        for head, lanes in enumerate(head_lanes):
            dq_part, dk_part, dv_part = attend(
                far_in[peer, 0, :, lanes],
                far_in[peer, 1, :, lanes],
                nbr[side, 0, :, lanes],
                nbr[side, 1, :, lanes],
                nbr_stats[side, 0, head : head + 1, :],
                nbr_stats[side, 1, head : head + 1, :],
                used,
            )
            ret_out[side, :, lanes] += dq_part
            fret_out[peer, 0, :, lanes] = dk_part
            fret_out[peer, 1, :, lanes] = dv_part
        fret_copy(peer).start()

    from_left = 2 * col < cols - 1
    behind = jnp.where(from_left, col, cols - 1 - col)
    first = jnp.where(from_left, RIGHT, LEFT)
    second = jnp.where(from_left, LEFT, RIGHT)
    has_first = jnp.where(from_left, col < cols - 1, col > 0)
    has_second = jnp.where(from_left, col > 0, col < cols - 1)

    @pl.when(has_first)
    def _():
        side_pass(first)

    for index in range((cols - 1) // 2):

        @pl.when(inner & (index < behind))
        def _(index=index):
            far_pass(jnp.where(from_left, index, cols - 1 - index))

    @pl.when(has_first)
    def _():
        ret_copy(first).start()

    for side in (UP, DOWN):

        @pl.when(exists[side])
        def _(side=side):
            side_pass(side)
            ret_copy(side).start()

    @pl.when(has_second)
    def _():
        side_pass(second)

    for index in range(2, cols):

        @pl.when(inner & (index > behind))
        def _(index=index):
            far_pass(jnp.where(from_left, index, cols - 1 - index))

    @pl.when(has_second)
    def _():
        ret_copy(second).start()

    for side in range(4):

        @pl.when(exists[side])
        def _(side=side):
            ret_wait(side)
            dq_acc[...] += ret_in[side]

    dq_norm = (dq_acc[...] * score_scale).astype(BF16).astype(F32)
    query_wide = q_raw[...].astype(F32)
    weighted = gain_q * dq_norm
    x_start(1, lane_columns([(0, row_sums(weighted * query_wide))])[0:8])

    for index, tile in enumerate(far_tiles):

        @pl.when(tile != col)
        def _(index=index, tile=tile):
            fret_wait(tile)
            for unit in range(UNITS):
                picked = jnp.where(send_unit[index] == unit, send_used[index], 0)
                spread = jnp.full((kb, width), picked, jnp.int32) > 0
                place = slice(unit * kb, (unit + 1) * kb)
                for which in range(2):
                    total[which, place, :] += jnp.where(
                        spread, fret_in[tile, which].astype(F32), 0.0
                    )

    dk_norm = total[0].astype(BF16).astype(F32)
    key_wide = k_raw[...].astype(F32)
    key_weighted = gain_k * dk_norm
    x_start(2, lane_columns([(1, row_sums(key_weighted * key_wide))])[0:8])
    dv_out[0, 0] = total[1].astype(BF16)

    q_factor = rates * rates * rates * x_finish(1) / full_width
    q_factor = to_columns(q_factor)[:, 0:1]
    dq_out[0, 0] = (q_rate * weighted - query_wide * q_factor).astype(BF16)

    for side in range(4):

        @pl.when(exists[side])
        def _(side=side):
            for which in range(3):
                nbr_copy(side, which).wait_send()
            ret_copy(side).wait_send()

    for tile in far_tiles:

        @pl.when(tile != col)
        def _(tile=tile):
            far_copy(tile).wait_send()

    for peer in range(cols):

        @pl.when(inner & (peer != col))
        def _(peer=peer):
            fret_copy(peer).wait_send()

    k_factor = rates * rates * rates * x_finish(2) / full_width
    k_factor = to_columns(k_factor)[:, 1:2]
    dk_out[0, 0] = (k_rate * key_weighted - key_wide * k_factor).astype(BF16)


def copy_kernel(dq_in, dk_in, dv_in, dq_out, dk_out, dv_out, sem):
    pairs = ((dq_in, dq_out), (dk_in, dk_out), (dv_in, dv_out))
    copies = [
        pltpu.make_async_copy(source, target, sem.at[index])
        for index, (source, target) in enumerate(pairs)
    ]
    for copy in copies:
        copy.start()
    for copy in copies:
        copy.wait()


def body(sizes, q_raw, k_raw, values, upstream, outputs, logsumexp, gain_q, gain_k, far_list):
    rows, cols, parts = sizes
    tokens, width = q_raw.shape[2:]
    heads = logsumexp.shape[2]
    kb = tokens // UNITS
    stat_rows = -(-heads // 8) * 8
    shape = jax.ShapeDtypeStruct(q_raw.shape, BF16)
    vmem = pl.BlockSpec(memory_space=pltpu.VMEM)
    anywhere = pl.BlockSpec(memory_space=pltpu.HBM)
    tile = pltpu.VMEM((tokens, width), BF16)
    pair = (2, tokens, width)
    dma = pltpu.SemaphoreType.DMA
    grads = pl.pallas_call(
        functools.partial(kernel, sizes),
        out_shape=(pltpu.VMEM(q_raw.shape, BF16),) * 3,
        in_specs=[anywhere] * 5 + [vmem] * 3 + [pl.BlockSpec(memory_space=pltpu.SMEM)],
        out_specs=(vmem,) * 3,
        scratch_shapes=[
            tile,
            tile,
            tile,
            tile,
            tile,
            tile,
            tile,
            pltpu.VMEM((2, stat_rows, tokens), F32),
            pltpu.VMEM((4, 2, stat_rows, tokens), F32),
            pltpu.VMEM((tokens, width), F32),
            pltpu.VMEM((4,) + pair, BF16),
            pltpu.VMEM((cols, 2, kb, width), BF16),
            pltpu.VMEM((cols, 2, kb, width), BF16),
            pltpu.VMEM((4, tokens, width), F32),
            pltpu.VMEM((4, tokens, width), F32),
            pltpu.VMEM((cols, 2, kb, width), BF16),
            pltpu.VMEM((cols, 2, kb, width), BF16),
            pltpu.VMEM(pair, F32),
            pltpu.VMEM((3, parts, 8, 128), F32),
            dma((5,)),
            dma((4, 3)),
            dma((4, 3)),
            dma((cols,)),
            dma((cols,)),
            dma((4,)),
            dma((4,)),
            dma((cols,)),
            dma((cols,)),
            dma((3, parts)),
            dma((3, parts)),
        ],
        compiler_params=pltpu.CompilerParams(collective_id=0, has_side_effects=True),
    )(
        q_raw,
        k_raw,
        values,
        upstream,
        outputs,
        logsumexp.transpose(0, 2, 1, 3),
        gain_q,
        gain_k,
        far_list,
    )
    return pl.pallas_call(
        copy_kernel,
        out_shape=(shape, shape, shape),
        in_specs=[vmem] * 3,
        out_specs=(anywhere,) * 3,
        scratch_shapes=[dma((3,))],
        compiler_params=pltpu.CompilerParams(vmem_limit_bytes=4 << 20),
    )(*grads)


def solution(mesh):
    sizes = (mesh.shape["ha"], mesh.shape["wa"], mesh.shape["hd"])
    tile = P("ha", "wa", None, "hd")
    return jax.shard_map(
        functools.partial(body, sizes),
        mesh=mesh,
        in_specs=(tile,) * 5 + (P("ha", "wa", "hd", None), P("hd"), P("hd"), P("ha", None, None)),
        out_specs=(tile,) * 3,
        check_vma=False,
    )
```

```python
import functools
import math

import jax
import jax.numpy as jnp
from jax import lax
from jax.experimental import pallas as pl
from jax.experimental.pallas import tpu as pltpu
from jax.sharding import PartitionSpec as P

UNITS = 4
EPS = 1e-06
MESH = pl.DeviceIdType.MESH
LAST = (((1,), (1,)), ((), ()))
FIRST = (((0,), (0,)), ((), ()))
PLAIN = (((1,), (0,)), ((), ()))
UP, DOWN, LEFT, RIGHT = range(4)
CODE_MAX = 32767.0
F32 = jnp.float32
BF16 = jnp.bfloat16


def dot(a, b, dims):
    return lax.dot_general(a, b, dims, preferred_element_type=F32)


def kernel(
    sizes,
    q_hbm,
    k_hbm,
    v_hbm,
    u_hbm,
    o_hbm,
    lse_ref,
    gain_q_ref,
    gain_k_ref,
    far_ref,
    dq_out,
    dk_out,
    dv_out,
    q_raw,
    k_raw,
    vals,
    ups,
    outs,
    qn,
    kn,
    stats,
    nbr_stats,
    dq_acc,
    nbr,
    far_pack,
    far_in,
    ret_acc,
    ret_out,
    ret_in,
    ret_scale,
    ret_scale_in,
    fret_out,
    fret_in,
    total,
    xbuf,
    load_sem,
    nbr_send,
    nbr_recv,
    far_send,
    far_recv,
    ret_send,
    ret_recv,
    fret_send,
    fret_recv,
    x_send,
    x_recv,
):
    rows, cols, parts = sizes
    row = lax.axis_index("ha")
    col = lax.axis_index("wa")
    me = lax.axis_index("hd")
    tokens, width = q_raw.shape
    heads = lse_ref.shape[1]
    hw = width // heads
    kb = tokens // UNITS
    full_width = width * parts
    slots = far_ref.shape[2]
    score_scale = 1.0 / math.sqrt(hw)
    head_lanes = [slice(head * hw, (head + 1) * hw) for head in range(heads)]

    loads = []
    for index, (source, target) in enumerate(
        ((u_hbm, ups), (k_hbm, k_raw), (q_hbm, q_raw), (o_hbm, outs), (v_hbm, vals))
    ):
        copy = pltpu.make_async_copy(source.at[0, 0], target, load_sem.at[index])
        copy.start()
        loads.append(copy)

    exists = (row > 0, row < rows - 1, col > 0, col < cols - 1)
    ids = ({"ha": row - 1}, {"ha": row + 1}, {"wa": col - 1}, {"wa": col + 1})
    inner = (col > 0) & (col < cols - 1)
    far_tiles = range(1, cols - 1)

    barrier = pltpu.get_barrier_semaphore()
    hd_ids = [{"hd": lax.rem(me + off, parts)} for off in range(1, parts)]
    for target in hd_ids:
        pl.semaphore_signal(barrier, inc=1, device_id=target, device_id_type=MESH)
    for side in (UP, DOWN):

        @pl.when(exists[side])
        def _(side=side):
            pl.semaphore_signal(barrier, inc=1, device_id=ids[side], device_id_type=MESH)

    for off in range(1, cols):
        pl.semaphore_signal(
            barrier, inc=1, device_id={"wa": lax.rem(col + off, cols)}, device_id_type=MESH
        )

    def lane_columns(columns):
        lane = lax.broadcasted_iota(jnp.int32, (tokens, 128), 1)
        mat = jnp.zeros((tokens, 128), F32)
        for place, column in columns:
            mat = jnp.where(lane == place, column, mat)
        return mat.T

    def row_sums(block):
        acc = block[:, :hw]
        for lanes in head_lanes[1:]:
            acc = acc + block[:, lanes]
        return jnp.sum(acc, axis=1, keepdims=True)

    def to_columns(rows8):
        return jnp.concatenate([rows8] * (tokens // 8), axis=0).T

    def x_copy(which, off):
        return pltpu.make_async_remote_copy(
            src_ref=xbuf.at[which, me],
            dst_ref=xbuf.at[which, me],
            send_sem=x_send.at[which, off],
            recv_sem=x_recv.at[which, off],
            device_id=hd_ids[off - 1],
            device_id_type=MESH,
        )

    def x_start(which, rows8):
        xbuf[which, me] = rows8
        for off in range(1, parts):
            x_copy(which, off).start()

    def x_finish(which):
        for off in range(1, parts):
            x_copy(which, off).wait()
        acc = xbuf[which, 0]
        for part in range(1, parts):
            acc = acc + xbuf[which, part]
        return acc

    def side_id(side):
        if isinstance(side, int):
            return ids[side]
        return {"wa": jnp.where(side == RIGHT, col + 1, col - 1)}

    def nbr_copy(side, which):
        if which == 2:
            source, target = stats, nbr_stats.at[side ^ 1]
        else:
            source, target = (qn, ups)[which], nbr.at[side ^ 1, which]
        return pltpu.make_async_remote_copy(
            src_ref=source,
            dst_ref=target,
            send_sem=nbr_send.at[side, which],
            recv_sem=nbr_recv.at[side ^ 1, which],
            device_id=ids[side],
            device_id_type=MESH,
        )

    def nbr_wait(side, which):
        if which == 2:
            source, target = stats, nbr_stats.at[side]
        else:
            source, target = (qn, ups)[which], nbr.at[side, which]
        pltpu.make_async_remote_copy(
            src_ref=source,
            dst_ref=target,
            send_sem=nbr_send.at[0, which],
            recv_sem=nbr_recv.at[side, which],
            device_id=side_id(side),
            device_id_type=MESH,
        ).wait_recv()

    def far_copy(tile):
        return pltpu.make_async_remote_copy(
            src_ref=far_pack.at[tile],
            dst_ref=far_in.at[col],
            send_sem=far_send.at[tile],
            recv_sem=far_recv.at[col],
            device_id={"wa": tile},
            device_id_type=MESH,
        )

    def far_wait(peer):
        pltpu.make_async_remote_copy(
            src_ref=far_pack.at[0],
            dst_ref=far_in.at[peer],
            send_sem=far_send.at[0],
            recv_sem=far_recv.at[peer],
            device_id={"wa": peer},
            device_id_type=MESH,
        ).wait_recv()

    def ret_copy(side, which):
        source, target = ((ret_out, ret_in), (ret_scale, ret_scale_in))[which]
        return pltpu.make_async_remote_copy(
            src_ref=source.at[side],
            dst_ref=target.at[side ^ 1],
            send_sem=ret_send.at[side, which],
            recv_sem=ret_recv.at[side ^ 1, which],
            device_id=side_id(side),
            device_id_type=MESH,
        )

    def ret_start(side):
        part = ret_acc[side]
        largest = jnp.abs(part[:, head_lanes[0]])
        for lanes in head_lanes[1:]:
            largest = jnp.maximum(largest, jnp.abs(part[:, lanes]))
        largest = jnp.maximum(jnp.max(largest, axis=1, keepdims=True), 1e-30)
        coded = jnp.round(part * (CODE_MAX / largest))
        ret_out[side] = coded.astype(jnp.int32).astype(jnp.int16)
        ret_copy(side, 0).start()
        ret_scale[side] = lane_columns([(0, largest / CODE_MAX)])[0:8]
        ret_copy(side, 1).start()

    def ret_wait(side):
        for which in range(2):
            source, target = ((ret_out, ret_in), (ret_scale, ret_scale_in))[which]
            pltpu.make_async_remote_copy(
                src_ref=source.at[side],
                dst_ref=target.at[side],
                send_sem=ret_send.at[side, which],
                recv_sem=ret_recv.at[side, which],
                device_id=ids[side],
                device_id_type=MESH,
            ).wait_recv()

    def fret_copy(peer):
        return pltpu.make_async_remote_copy(
            src_ref=fret_out.at[peer],
            dst_ref=fret_in.at[col],
            send_sem=fret_send.at[peer],
            recv_sem=fret_recv.at[col],
            device_id={"wa": peer},
            device_id_type=MESH,
        )

    def fret_wait(tile):
        pltpu.make_async_remote_copy(
            src_ref=fret_out.at[tile],
            dst_ref=fret_in.at[tile],
            send_sem=fret_send.at[tile],
            recv_sem=fret_recv.at[tile],
            device_id={"wa": tile},
            device_id_type=MESH,
        ).wait_recv()

    loads[0].wait()
    pl.semaphore_wait(
        barrier,
        parts
        - 1
        + jnp.minimum(row, 1)
        + jnp.minimum(rows - 1 - row, 1)
        + (cols - 1),
    )
    for side in (LEFT, RIGHT, UP, DOWN):

        @pl.when(exists[side])
        def _(side=side):
            nbr_copy(side, 1).start()

    loads[1].wait()
    key_wide = k_raw[...].astype(F32)
    key_squares = row_sums(key_wide * key_wide)
    loads[2].wait()
    query_wide = q_raw[...].astype(F32)
    query_squares = row_sums(query_wide * query_wide)
    x_start(0, lane_columns([(0, query_squares), (1, key_squares)])[0:8])

    loads[3].wait()
    delta_columns = []
    for head, lanes in enumerate(head_lanes):
        product = ups[:, lanes].astype(F32) * outs[:, lanes].astype(F32)
        delta_columns.append((head, jnp.sum(product, axis=1, keepdims=True)))
    stats[0] = lane_columns(delta_columns)[0 : stats.shape[1]]
    for head in range(heads):
        stats[1, head : head + 1, :] = lse_ref[0, head]
    for side in (LEFT, RIGHT, UP, DOWN):

        @pl.when(exists[side])
        def _(side=side):
            nbr_copy(side, 2).start()

    send_unit = []
    send_used = []
    for tile in far_tiles:
        unit = jnp.int32(0)
        asked = jnp.int32(0)
        for slot in range(slots):
            named = jnp.where(col > tile, far_ref[0, tile - 1, slot], far_ref[0, tile + 1, slot])
            wanted = named - col * UNITS
            hit = (wanted >= 0) & (wanted < UNITS)
            unit = jnp.where(hit, wanted, unit)
            asked = jnp.where(hit, 1, asked)
        send_unit.append(unit)
        send_used.append(asked)

    def pick_unit(unit_wanted, source):
        wanted = jnp.full((kb, width), unit_wanted, jnp.int32)
        picked = source[0:kb, :].astype(F32)
        for unit in range(1, UNITS):
            block = source[unit * kb : (unit + 1) * kb, :].astype(F32)
            picked = jnp.where(wanted == unit, block, picked)
        return picked.astype(BF16)

    loads[4].wait()
    for index, tile in enumerate(far_tiles):

        @pl.when(tile != col)
        def _(index=index, tile=tile):
            far_pack[tile, 1] = pick_unit(send_unit[index], vals)

    gain_q = gain_q_ref[...].astype(F32).reshape(1, width)
    gain_k = gain_k_ref[...].astype(F32).reshape(1, width)
    rates = lax.rsqrt(x_finish(0) / full_width + EPS)
    rate_columns = to_columns(rates)
    q_rate = rate_columns[:, 0:1]
    k_rate = rate_columns[:, 1:2]
    qn[...] = (q_raw[...].astype(F32) * q_rate * gain_q).astype(BF16)
    for side in (LEFT, RIGHT, UP, DOWN):

        @pl.when(exists[side])
        def _(side=side):
            nbr_copy(side, 0).start()

    kn[...] = (k_raw[...].astype(F32) * k_rate * gain_k).astype(BF16)
    for index, tile in enumerate(far_tiles):

        @pl.when(tile != col)
        def _(index=index, tile=tile):
            far_pack[tile, 0] = pick_unit(send_unit[index], kn)
            far_copy(tile).start()

    def attend(keys, values, queries, upstream, delta_row, lse_row, used=None):
        weight = jnp.exp(dot(keys, queries, LAST) * score_scale - lse_row)
        if used is not None:
            weight = jnp.where(jnp.full(weight.shape, used, jnp.int32) > 0, weight, 0.0)
        dweight = dot(values, upstream, LAST)
        dscore = (weight * (dweight - delta_row)).astype(BF16)
        dq_part = dot(dscore, keys, FIRST)
        dk_part = (dot(dscore, queries, PLAIN) * score_scale).astype(BF16)
        dv_part = dot(weight.astype(BF16), upstream, PLAIN).astype(BF16)
        return dq_part, dk_part, dv_part

    for head, lanes in enumerate(head_lanes):
        dq_part, dk_part, dv_part = attend(
            kn[:, lanes],
            vals[:, lanes],
            qn[:, lanes],
            ups[:, lanes],
            stats[0, head : head + 1, :],
            stats[1, head : head + 1, :],
        )
        dq_acc[:, lanes] = dq_part
        total[0, :, lanes] = dk_part.astype(F32)
        total[1, :, lanes] = dv_part.astype(F32)

    def side_pass(side):
        for which in (1, 2, 0):
            nbr_wait(side, which)
        for head, lanes in enumerate(head_lanes):
            dq_part, dk_part, dv_part = attend(
                kn[:, lanes],
                vals[:, lanes],
                nbr[side, 0, :, lanes],
                nbr[side, 1, :, lanes],
                nbr_stats[side, 0, head : head + 1, :],
                nbr_stats[side, 1, head : head + 1, :],
            )
            ret_acc[side, :, lanes] = dq_part
            total[0, :, lanes] += dk_part.astype(F32)
            total[1, :, lanes] += dv_part.astype(F32)

    def far_pass(peer):
        side = jnp.where(peer > col, LEFT, RIGHT)
        query_col = jnp.where(peer > col, col - 1, col + 1)
        used = jnp.int32(0)
        for slot in range(slots):
            named = far_ref[0, query_col, slot] - peer * UNITS
            used = jnp.where((named >= 0) & (named < UNITS), 1, used)
        far_wait(peer)
        for head, lanes in enumerate(head_lanes):
            dq_part, dk_part, dv_part = attend(
                far_in[peer, 0, :, lanes],
                far_in[peer, 1, :, lanes],
                nbr[side, 0, :, lanes],
                nbr[side, 1, :, lanes],
                nbr_stats[side, 0, head : head + 1, :],
                nbr_stats[side, 1, head : head + 1, :],
                used,
            )
            ret_acc[side, :, lanes] += dq_part
            fret_out[peer, 0, :, lanes] = dk_part
            fret_out[peer, 1, :, lanes] = dv_part
        fret_copy(peer).start()

    from_left = 2 * col < cols - 1
    behind = jnp.where(from_left, col, cols - 1 - col)
    first = jnp.where(from_left, RIGHT, LEFT)
    second = jnp.where(from_left, LEFT, RIGHT)
    has_first = jnp.where(from_left, col < cols - 1, col > 0)
    has_second = jnp.where(from_left, col > 0, col < cols - 1)

    @pl.when(has_first)
    def _():
        side_pass(first)

    for index in range((cols - 1) // 2):

        @pl.when(inner & (index < behind))
        def _(index=index):
            far_pass(jnp.where(from_left, index, cols - 1 - index))

    @pl.when(has_first)
    def _():
        ret_start(first)

    for side in (UP, DOWN):

        @pl.when(exists[side])
        def _(side=side):
            side_pass(side)
            ret_start(side)

    @pl.when(has_second)
    def _():
        side_pass(second)

    for index in range(2, cols):

        @pl.when(inner & (index > behind))
        def _(index=index):
            far_pass(jnp.where(from_left, index, cols - 1 - index))

    @pl.when(has_second)
    def _():
        ret_start(second)

    for side in range(4):

        @pl.when(exists[side])
        def _(side=side):
            ret_wait(side)
            scale = to_columns(ret_scale_in[side])[:, 0:1]
            dq_acc[...] += ret_in[side].astype(jnp.int32).astype(F32) * scale

    dq_norm = (dq_acc[...] * score_scale).astype(BF16).astype(F32)
    query_wide = q_raw[...].astype(F32)
    weighted = gain_q * dq_norm
    x_start(1, lane_columns([(0, row_sums(weighted * query_wide))])[0:8])

    for index, tile in enumerate(far_tiles):

        @pl.when(tile != col)
        def _(index=index, tile=tile):
            fret_wait(tile)
            for unit in range(UNITS):
                picked = jnp.where(send_unit[index] == unit, send_used[index], 0)
                spread = jnp.full((kb, width), picked, jnp.int32) > 0
                place = slice(unit * kb, (unit + 1) * kb)
                for which in range(2):
                    total[which, place, :] += jnp.where(
                        spread, fret_in[tile, which].astype(F32), 0.0
                    )

    dk_norm = total[0].astype(BF16).astype(F32)
    key_wide = k_raw[...].astype(F32)
    key_weighted = gain_k * dk_norm
    x_start(2, lane_columns([(1, row_sums(key_weighted * key_wide))])[0:8])
    dv_out[0, 0] = total[1].astype(BF16)

    q_factor = rates * rates * rates * x_finish(1) / full_width
    q_factor = to_columns(q_factor)[:, 0:1]
    dq_out[0, 0] = (q_rate * weighted - query_wide * q_factor).astype(BF16)

    for side in range(4):

        @pl.when(exists[side])
        def _(side=side):
            for which in range(3):
                nbr_copy(side, which).wait_send()
            for which in range(2):
                ret_copy(side, which).wait_send()

    for tile in far_tiles:

        @pl.when(tile != col)
        def _(tile=tile):
            far_copy(tile).wait_send()

    for peer in range(cols):

        @pl.when(inner & (peer != col))
        def _(peer=peer):
            fret_copy(peer).wait_send()

    k_factor = rates * rates * rates * x_finish(2) / full_width
    k_factor = to_columns(k_factor)[:, 1:2]
    dk_out[0, 0] = (k_rate * key_weighted - key_wide * k_factor).astype(BF16)


def copy_kernel(dq_in, dk_in, dv_in, dq_out, dk_out, dv_out, sem):
    pairs = ((dq_in, dq_out), (dk_in, dk_out), (dv_in, dv_out))
    copies = [
        pltpu.make_async_copy(source, target, sem.at[index])
        for index, (source, target) in enumerate(pairs)
    ]
    for copy in copies:
        copy.start()
    for copy in copies:
        copy.wait()


def body(sizes, q_raw, k_raw, values, upstream, outputs, logsumexp, gain_q, gain_k, far_list):
    rows, cols, parts = sizes
    tokens, width = q_raw.shape[2:]
    heads = logsumexp.shape[2]
    kb = tokens // UNITS
    stat_rows = -(-heads // 8) * 8
    shape = jax.ShapeDtypeStruct(q_raw.shape, BF16)
    vmem = pl.BlockSpec(memory_space=pltpu.VMEM)
    anywhere = pl.BlockSpec(memory_space=pltpu.HBM)
    tile = pltpu.VMEM((tokens, width), BF16)
    pair = (2, tokens, width)
    dma = pltpu.SemaphoreType.DMA
    grads = pl.pallas_call(
        functools.partial(kernel, sizes),
        out_shape=(pltpu.VMEM(q_raw.shape, BF16),) * 3,
        in_specs=[anywhere] * 5 + [vmem] * 3 + [pl.BlockSpec(memory_space=pltpu.SMEM)],
        out_specs=(vmem,) * 3,
        scratch_shapes=[
            tile,
            tile,
            tile,
            tile,
            tile,
            tile,
            tile,
            pltpu.VMEM((2, stat_rows, tokens), F32),
            pltpu.VMEM((4, 2, stat_rows, tokens), F32),
            pltpu.VMEM((tokens, width), F32),
            pltpu.VMEM((4,) + pair, BF16),
            pltpu.VMEM((cols, 2, kb, width), BF16),
            pltpu.VMEM((cols, 2, kb, width), BF16),
            pltpu.VMEM((4, tokens, width), F32),
            pltpu.VMEM((4, tokens, width), jnp.int16),
            pltpu.VMEM((4, tokens, width), jnp.int16),
            pltpu.VMEM((4, 8, tokens), F32),
            pltpu.VMEM((4, 8, tokens), F32),
            pltpu.VMEM((cols, 2, kb, width), BF16),
            pltpu.VMEM((cols, 2, kb, width), BF16),
            pltpu.VMEM(pair, F32),
            pltpu.VMEM((3, parts, 8, 128), F32),
            dma((5,)),
            dma((4, 3)),
            dma((4, 3)),
            dma((cols,)),
            dma((cols,)),
            dma((4, 2)),
            dma((4, 2)),
            dma((cols,)),
            dma((cols,)),
            dma((3, parts)),
            dma((3, parts)),
        ],
        compiler_params=pltpu.CompilerParams(collective_id=0, has_side_effects=True),
    )(
        q_raw,
        k_raw,
        values,
        upstream,
        outputs,
        logsumexp.transpose(0, 2, 1, 3),
        gain_q,
        gain_k,
        far_list,
    )
    return pl.pallas_call(
        copy_kernel,
        out_shape=(shape, shape, shape),
        in_specs=[vmem] * 3,
        out_specs=(anywhere,) * 3,
        scratch_shapes=[dma((3,))],
        compiler_params=pltpu.CompilerParams(vmem_limit_bytes=4 << 20),
    )(*grads)


def solution(mesh):
    sizes = (mesh.shape["ha"], mesh.shape["wa"], mesh.shape["hd"])
    tile = P("ha", "wa", None, "hd")
    return jax.shard_map(
        functools.partial(body, sizes),
        mesh=mesh,
        in_specs=(tile,) * 5 + (P("ha", "wa", "hd", None), P("hd"), P("hd"), P("ha", None, None)),
        out_specs=(tile,) * 3,
        check_vma=False,
    )
```

```python
import functools
import math

import jax
import jax.numpy as jnp
from jax import lax
from jax.experimental import pallas as pl
from jax.experimental.pallas import tpu as pltpu
from jax.sharding import PartitionSpec as P

UNITS = 4
EPS = 1e-06
MESH = pl.DeviceIdType.MESH
LAST = (((1,), (1,)), ((), ()))
FIRST = (((0,), (0,)), ((), ()))
PLAIN = (((1,), (0,)), ((), ()))
LEFT, RIGHT = 0, 1
CODE_MAX = 32767.0
F32 = jnp.float32
BF16 = jnp.bfloat16


def dot(a, b, dims):
    return lax.dot_general(a, b, dims, preferred_element_type=F32)


def kernel(
    sizes,
    q_hbm,
    k_hbm,
    v_hbm,
    u_hbm,
    o_hbm,
    lse_hbm,
    gain_q_hbm,
    gain_k_hbm,
    far_hbm,
    dq_out,
    dk_out,
    dv_out,
    q_raw,
    k_raw,
    vals,
    ups,
    outs,
    qn,
    kn,
    gain_q_ref,
    gain_k_ref,
    far_ref,
    stats,
    nbr_stats,
    dq_acc,
    nbr_q,
    nbr_u,
    far_pack,
    near_in,
    near_out,
    past_in,
    past_out,
    ret_acc,
    ret_out,
    ret_in,
    ret_scale,
    ret_scale_in,
    fret_in,
    total,
    xbuf,
    load_sem,
    nbr_send,
    nbr_recv,
    far_send,
    near_recv,
    past_recv,
    ret_send,
    ret_recv,
    near_send,
    past_send,
    fret_recv,
    x_send,
    x_recv,
):
    rows, cols, parts = sizes
    row = lax.axis_index("ha")
    col = lax.axis_index("wa")
    me = lax.axis_index("hd")
    tokens, width = q_raw.shape
    heads = lse_hbm.shape[2]
    hw = width // heads
    kb = tokens // UNITS
    full_width = width * parts
    slots = far_ref.shape[2]
    near_slots = near_in.shape[0]
    past_slots = past_in.shape[0]
    score_scale = 1.0 / math.sqrt(hw)
    head_lanes = [slice(head * hw, (head + 1) * hw) for head in range(heads)]

    barrier = pltpu.get_barrier_semaphore()
    hd_ids = [{"hd": lax.rem(me + off, parts)} for off in range(1, parts)]
    for target in hd_ids:
        pl.semaphore_signal(barrier, inc=1, device_id=target, device_id_type=MESH)

    exists = [col > 0, col < cols - 1]
    ids = [{"wa": col - 1}, {"wa": col + 1}]
    facing = [RIGHT, LEFT]
    if rows == 2:
        exists.append(True)
        ids.append({"ha": 1 - row})
        facing.append(2)
        pl.semaphore_signal(barrier, inc=1, device_id=ids[2], device_id_type=MESH)
    elif rows > 2:
        exists += [row > 0, row < rows - 1]
        ids += [{"ha": row - 1}, {"ha": row + 1}]
        facing += [3, 2]
        for side in (2, 3):

            @pl.when(exists[side])
            def _(side=side):
                pl.semaphore_signal(barrier, inc=1, device_id=ids[side], device_id_type=MESH)

    sides = range(len(ids))
    upright = range(2, len(ids))
    for off in range(1, cols):
        pl.semaphore_signal(
            barrier, inc=1, device_id={"wa": lax.rem(col + off, cols)}, device_id_type=MESH
        )

    loads = []
    for index, (source, target) in enumerate(
        (
            (u_hbm.at[0, 0], ups),
            (k_hbm.at[0, 0], k_raw),
            (q_hbm.at[0, 0], q_raw),
            (o_hbm.at[0, 0], outs),
            (v_hbm.at[0, 0], vals),
            (lse_hbm.at[0, 0], stats.at[1, pl.ds(0, heads)]),
            (gain_q_hbm, gain_q_ref),
            (gain_k_hbm, gain_k_ref),
            (far_hbm, far_ref),
        )
    ):
        copy = pltpu.make_async_copy(source, target, load_sem.at[index])
        copy.start()
        loads.append(copy)

    inner = (col > 0) & (col < cols - 1)
    far_tiles = range(1, cols - 1)

    def lane_columns(columns):
        lane = lax.broadcasted_iota(jnp.int32, (tokens, 128), 1)
        mat = jnp.zeros((tokens, 128), F32)
        for place, column in columns:
            mat = jnp.where(lane == place, column, mat)
        return mat.T

    def row_sums(block):
        acc = block[:, :hw]
        for lanes in head_lanes[1:]:
            acc = acc + block[:, lanes]
        return jnp.sum(acc, axis=1, keepdims=True)

    def to_columns(rows8):
        return jnp.concatenate([rows8] * (tokens // 8), axis=0).T

    def x_copy(which, off):
        return pltpu.make_async_remote_copy(
            src_ref=xbuf.at[which, me],
            dst_ref=xbuf.at[which, me],
            send_sem=x_send.at[which, off],
            recv_sem=x_recv.at[which, off],
            device_id=hd_ids[off - 1],
            device_id_type=MESH,
        )

    def x_start(which, rows8):
        xbuf[which, me] = rows8
        for off in range(1, parts):
            x_copy(which, off).start()

    def x_finish(which):
        for off in range(1, parts):
            x_copy(which, off).wait()
        acc = xbuf[which, 0]
        for part in range(1, parts):
            acc = acc + xbuf[which, part]
        return acc

    def side_id(side):
        if isinstance(side, int):
            return ids[side]
        return {"wa": jnp.where(side == RIGHT, col + 1, col - 1)}

    def face(side):
        return facing[side] if isinstance(side, int) else 1 - side

    def nbr_refs(side, message):
        if message == 0:
            return ups, nbr_u.at[side]
        if message == 1:
            return stats, nbr_stats.at[side]
        lanes = head_lanes[message - 2]
        return qn.at[:, lanes], nbr_q.at[side, :, lanes]

    messages = range(2 + heads)

    def nbr_copy(side, message):
        return pltpu.make_async_remote_copy(
            src_ref=nbr_refs(side, message)[0],
            dst_ref=nbr_refs(face(side), message)[1],
            send_sem=nbr_send.at[side, message],
            recv_sem=nbr_recv.at[face(side), message],
            device_id=ids[side],
            device_id_type=MESH,
        )

    def nbr_wait(side, message):
        pltpu.make_async_remote_copy(
            src_ref=nbr_refs(side, message)[0],
            dst_ref=nbr_refs(side, message)[1],
            send_sem=nbr_send.at[side, message],
            recv_sem=nbr_recv.at[side, message],
            device_id=ids[side],
            device_id_type=MESH,
        ).wait_recv()

    def nearer_left(tile):
        return 2 * tile < cols - 1

    from_left = nearer_left(col)
    behind = jnp.where(from_left, col, cols - 1 - col)
    first = jnp.where(from_left, RIGHT, LEFT)
    second = 1 - first
    has_first = jnp.where(from_left, col < cols - 1, col > 0)
    has_second = jnp.where(from_left, col > 0, col < cols - 1)

    def far_copy(tile, near):
        rank = col if nearer_left(tile) else cols - 1 - col
        landing, recv = (near_in, near_recv) if near else (past_in, past_recv)
        place = rank if near else rank - 2
        return pltpu.make_async_remote_copy(
            src_ref=far_pack.at[tile],
            dst_ref=landing.at[place],
            send_sem=far_send.at[tile],
            recv_sem=recv.at[place],
            device_id={"wa": tile},
            device_id_type=MESH,
        )

    def is_near(tile):
        return col < tile if nearer_left(tile) else col > tile

    def is_past(tile):
        return col > tile if nearer_left(tile) else col < tile

    def ranked(rank):
        return jnp.where(from_left, rank, cols - 1 - rank)

    def far_wait(place, near):
        landing, recv = (near_in, near_recv) if near else (past_in, past_recv)
        pltpu.make_async_remote_copy(
            src_ref=far_pack.at[0],
            dst_ref=landing.at[place],
            send_sem=far_send.at[0],
            recv_sem=recv.at[place],
            device_id={"wa": ranked(place if near else place + 2)},
            device_id_type=MESH,
        ).wait_recv()

    def fret_copy(place, near):
        source, send = (near_out, near_send) if near else (past_out, past_send)
        return pltpu.make_async_remote_copy(
            src_ref=source.at[place],
            dst_ref=fret_in.at[col],
            send_sem=send.at[place],
            recv_sem=fret_recv.at[col],
            device_id={"wa": ranked(place if near else place + 2)},
            device_id_type=MESH,
        )

    def fret_wait(tile):
        pltpu.make_async_remote_copy(
            src_ref=fret_in.at[tile],
            dst_ref=fret_in.at[tile],
            send_sem=near_send.at[0],
            recv_sem=fret_recv.at[tile],
            device_id={"wa": tile},
            device_id_type=MESH,
        ).wait_recv()

    def ret_copy(side, which):
        source, target = ((ret_out, ret_in), (ret_scale, ret_scale_in))[which]
        return pltpu.make_async_remote_copy(
            src_ref=source.at[side],
            dst_ref=target.at[face(side)],
            send_sem=ret_send.at[side, which],
            recv_sem=ret_recv.at[face(side), which],
            device_id=side_id(side),
            device_id_type=MESH,
        )

    def ret_start(side):
        part = ret_acc[side]
        largest = jnp.abs(part[:, head_lanes[0]])
        for lanes in head_lanes[1:]:
            largest = jnp.maximum(largest, jnp.abs(part[:, lanes]))
        largest = jnp.maximum(jnp.max(largest, axis=1, keepdims=True), 1e-30)
        coded = jnp.round(part * (CODE_MAX / largest))
        ret_out[side] = coded.astype(jnp.int32).astype(jnp.int16)
        ret_copy(side, 0).start()
        ret_scale[side] = lane_columns([(0, largest / CODE_MAX)])[0:8]
        ret_copy(side, 1).start()

    def ret_wait(side):
        for which in range(2):
            source, target = ((ret_out, ret_in), (ret_scale, ret_scale_in))[which]
            pltpu.make_async_remote_copy(
                src_ref=source.at[side],
                dst_ref=target.at[side],
                send_sem=ret_send.at[side, which],
                recv_sem=ret_recv.at[side, which],
                device_id=ids[side],
                device_id_type=MESH,
            ).wait_recv()

    greeted = parts - 1 + cols - 1
    if rows == 2:
        greeted = greeted + 1
    elif rows > 2:
        greeted = greeted + jnp.minimum(row, 1) + jnp.minimum(rows - 1 - row, 1)
    loads[0].wait()
    pl.semaphore_wait(barrier, greeted)
    for side in sides:

        @pl.when(exists[side])
        def _(side=side):
            nbr_copy(side, 0).start()

    loads[1].wait()
    key_wide = k_raw[...].astype(F32)
    key_squares = row_sums(key_wide * key_wide)
    loads[2].wait()
    query_wide = q_raw[...].astype(F32)
    query_squares = row_sums(query_wide * query_wide)
    x_start(0, lane_columns([(0, query_squares), (1, key_squares)])[0:8])

    loads[3].wait()
    loads[5].wait()
    delta_columns = []
    for head, lanes in enumerate(head_lanes):
        product = ups[:, lanes].astype(F32) * outs[:, lanes].astype(F32)
        delta_columns.append((head, jnp.sum(product, axis=1, keepdims=True)))
    stats[0] = lane_columns(delta_columns)[0 : stats.shape[1]]
    for side in sides:

        @pl.when(exists[side])
        def _(side=side):
            nbr_copy(side, 1).start()

        @pl.when(jnp.logical_not(exists[side]))
        def _(side=side):
            nbr_u[side] = jnp.zeros(nbr_u.shape[1:], BF16)
            nbr_q[side] = jnp.zeros(nbr_q.shape[1:], BF16)
            nbr_stats[side] = jnp.zeros(nbr_stats.shape[1:], F32)
            ret_in[side] = jnp.zeros(ret_in.shape[1:], jnp.int16)
            ret_scale_in[side] = jnp.zeros(ret_scale_in.shape[1:], F32)

    for place in range(near_slots):

        @pl.when(jnp.logical_not(inner) | (place >= behind))
        def _(place=place):
            near_in[place] = jnp.zeros(near_in.shape[1:], BF16)

    for place in range(past_slots):

        @pl.when(jnp.logical_not(inner) | (place + 2 <= behind))
        def _(place=place):
            past_in[place] = jnp.zeros(past_in.shape[1:], BF16)

    loads[8].wait()
    send_unit = []
    send_used = []
    for tile in far_tiles:
        unit = jnp.int32(0)
        asked = jnp.int32(0)
        for slot in range(slots):
            named = jnp.where(col > tile, far_ref[0, tile - 1, slot], far_ref[0, tile + 1, slot])
            wanted = named - col * UNITS
            hit = (wanted >= 0) & (wanted < UNITS)
            unit = jnp.where(hit, wanted, unit)
            asked = jnp.where(hit, 1, asked)
        send_unit.append(unit)
        send_used.append(jnp.where(col == tile, 0, asked))

    def rank_used(rank, near):
        peer = ranked(rank)
        query_col = jnp.clip(jnp.where(peer > col, col - 1, col + 1), 0, cols - 1)
        used = jnp.int32(0)
        for slot in range(slots):
            named = far_ref[0, query_col, slot] - peer * UNITS
            used = jnp.where((named >= 0) & (named < UNITS), 1, used)
        return jnp.where(rank < behind if near else rank > behind, used, 0)

    near_used = [rank_used(place, True) for place in range(near_slots)]
    past_used = [rank_used(place + 2, False) for place in range(past_slots)]

    def pick_unit(unit_wanted, source):
        wanted = jnp.full((kb, width), unit_wanted, jnp.int32)
        picked = source[0:kb, :].astype(F32)
        for unit in range(1, UNITS):
            block = source[unit * kb : (unit + 1) * kb, :].astype(F32)
            picked = jnp.where(wanted == unit, block, picked)
        return picked.astype(BF16)

    loads[4].wait()
    for index, tile in enumerate(far_tiles):
        far_pack[tile, 1] = pick_unit(send_unit[index], vals)

    loads[6].wait()
    loads[7].wait()
    gain_q = gain_q_ref[...].astype(F32).reshape(1, width)
    gain_k = gain_k_ref[...].astype(F32).reshape(1, width)
    rates = lax.rsqrt(x_finish(0) / full_width + EPS)
    rate_columns = to_columns(rates)
    q_rate = rate_columns[:, 0:1]
    k_rate = rate_columns[:, 1:2]
    qn[...] = (q_raw[...].astype(F32) * q_rate * gain_q).astype(BF16)
    for side in sides:

        @pl.when(exists[side])
        def _(side=side):
            for head in range(heads):
                nbr_copy(side, 2 + head).start()

    kn[...] = (k_raw[...].astype(F32) * k_rate * gain_k).astype(BF16)
    for index, tile in enumerate(far_tiles):
        far_pack[tile, 0] = pick_unit(send_unit[index], kn)
    for near in (True, False):
        for tile in far_tiles:

            @pl.when(is_near(tile) if near else is_past(tile))
            def _(tile=tile, near=near):
                far_copy(tile, near).start()

    def attend(keys, values, queries, upstream, delta_row, lse_row, used=None):
        weight = jnp.exp(dot(keys, queries, LAST) * score_scale - lse_row)
        if used is not None:
            weight = jnp.where(used, weight, 0.0)
        dweight = dot(values, upstream, LAST)
        dscore = (weight * (dweight - delta_row)).astype(BF16)
        weight_low = weight.astype(BF16)
        dq_part = dot(dscore, keys, FIRST)
        dk_parts, dv_parts = [], []
        for start in range(0, queries.shape[0], tokens):
            block = slice(start, start + tokens)
            dk_part = dot(dscore[:, block], queries[block], PLAIN) * score_scale
            dk_parts.append(dk_part.astype(BF16))
            dv_parts.append(dot(weight_low[:, block], upstream[block], PLAIN).astype(BF16))
        return dq_part, dk_parts, dv_parts

    for head, lanes in enumerate(head_lanes):
        dq_part, (dk_part,), (dv_part,) = attend(
            kn[:, lanes],
            vals[:, lanes],
            qn[:, lanes],
            ups[:, lanes],
            stats[0, head : head + 1, :],
            stats[1, head : head + 1, :],
        )
        dq_acc[:, lanes] = dq_part
        total[0, :, lanes] = dk_part.astype(F32)
        total[1, :, lanes] = dv_part.astype(F32)

    def stat_row(which, head):
        return jnp.concatenate([nbr_stats[side, which, head : head + 1, :] for side in sides], axis=1)

    for head, lanes in enumerate(head_lanes):
        for side in sides:

            @pl.when(exists[side])
            def _(side=side, head=head):
                for message in (0, 1, 2) if head == 0 else (2 + head,):
                    nbr_wait(side, message)

        dq_part, dk_parts, dv_parts = attend(
            kn[:, lanes],
            vals[:, lanes],
            nbr_q[:, :, lanes].reshape(len(sides) * tokens, hw),
            nbr_u[:, :, lanes].reshape(len(sides) * tokens, hw),
            stat_row(0, head),
            stat_row(1, head),
        )
        ret_acc[:, :, lanes] = dq_part.reshape(len(sides), tokens, hw)
        for which, terms in enumerate((dk_parts, dv_parts)):
            acc = total[which, :, lanes]
            for term in terms:
                acc = acc + term.astype(F32)
            total[which, :, lanes] = acc

    for side in upright:

        @pl.when(exists[side])
        def _(side=side):
            ret_start(side)

    def far_pass(near):
        landing, outgoing = (near_in, near_out) if near else (past_in, past_out)
        flags = near_used if near else past_used
        side = first if near else second
        count = len(flags)
        for place in range(count):

            @pl.when(place < behind if near else place + 2 > behind)
            def _(place=place):
                far_wait(place, near)

        used = jnp.concatenate([jnp.full((kb, tokens), flag, jnp.int32) for flag in flags], axis=0) > 0
        for head, lanes in enumerate(head_lanes):
            dq_part, (dk_part,), (dv_part,) = attend(
                landing[:, 0, :, lanes].reshape(count * kb, hw),
                landing[:, 1, :, lanes].reshape(count * kb, hw),
                nbr_q[side, :, lanes],
                nbr_u[side, :, lanes],
                nbr_stats[side, 0, head : head + 1, :],
                nbr_stats[side, 1, head : head + 1, :],
                used,
            )
            ret_acc[side, :, lanes] += dq_part
            outgoing[:, 0, :, lanes] = dk_part.reshape(count, kb, hw)
            outgoing[:, 1, :, lanes] = dv_part.reshape(count, kb, hw)

    if near_slots:

        @pl.when(inner)
        def _():
            far_pass(True)

    @pl.when(has_first)
    def _():
        ret_start(first)

    for place in range(near_slots):

        @pl.when(inner & (place < behind))
        def _(place=place):
            fret_copy(place, True).start()

    if past_slots:

        @pl.when(inner)
        def _():
            far_pass(False)

    for place in range(past_slots):

        @pl.when(inner & (place + 2 > behind))
        def _(place=place):
            fret_copy(place, False).start()

    @pl.when(has_second)
    def _():
        ret_start(second)

    for side in sides:

        @pl.when(exists[side])
        def _(side=side):
            ret_wait(side)

    dq_sum = dq_acc[...]
    for side in sides:
        scale = to_columns(ret_scale_in[side])[:, 0:1]
        dq_sum = dq_sum + ret_in[side].astype(jnp.int32).astype(F32) * scale
    dq_norm = (dq_sum * score_scale).astype(BF16).astype(F32)
    query_wide = q_raw[...].astype(F32)
    weighted = gain_q * dq_norm
    x_start(1, lane_columns([(0, row_sums(weighted * query_wide))])[0:8])

    for tile in far_tiles:

        @pl.when(tile != col)
        def _(tile=tile):
            fret_wait(tile)

    for unit in range(UNITS):
        place = slice(unit * kb, (unit + 1) * kb)
        for which in range(2):
            acc = total[which, place, :]
            for index, tile in enumerate(far_tiles):
                picked = jnp.where(send_unit[index] == unit, send_used[index], 0)
                spread = jnp.full((kb, width), picked, jnp.int32) > 0
                acc = acc + jnp.where(spread, fret_in[tile, which].astype(F32), 0.0)
            total[which, place, :] = acc

    dk_norm = total[0].astype(BF16).astype(F32)
    key_wide = k_raw[...].astype(F32)
    key_weighted = gain_k * dk_norm
    x_start(2, lane_columns([(1, row_sums(key_weighted * key_wide))])[0:8])
    dv_out[0, 0] = total[1].astype(BF16)

    q_factor = rates * rates * rates * x_finish(1) / full_width
    q_factor = to_columns(q_factor)[:, 0:1]
    dq_out[0, 0] = (q_rate * weighted - query_wide * q_factor).astype(BF16)

    for side in sides:

        @pl.when(exists[side])
        def _(side=side):
            for message in messages:
                nbr_copy(side, message).wait_send()
            for which in range(2):
                ret_copy(side, which).wait_send()

    for near in (True, False):
        for tile in far_tiles:

            @pl.when(is_near(tile) if near else is_past(tile))
            def _(tile=tile, near=near):
                far_copy(tile, near).wait_send()

    for place in range(near_slots):

        @pl.when(inner & (place < behind))
        def _(place=place):
            fret_copy(place, True).wait_send()

    for place in range(past_slots):

        @pl.when(inner & (place + 2 > behind))
        def _(place=place):
            fret_copy(place, False).wait_send()

    k_factor = rates * rates * rates * x_finish(2) / full_width
    k_factor = to_columns(k_factor)[:, 1:2]
    dk_out[0, 0] = (k_rate * key_weighted - key_wide * k_factor).astype(BF16)


def copy_kernel(dq_in, dk_in, dv_in, dq_out, dk_out, dv_out, sem):
    pairs = ((dq_in, dq_out), (dk_in, dk_out), (dv_in, dv_out))
    copies = [
        pltpu.make_async_copy(source, target, sem.at[index])
        for index, (source, target) in enumerate(pairs)
    ]
    for copy in copies:
        copy.start()
    for copy in copies:
        copy.wait()


def body(sizes, q_raw, k_raw, values, upstream, outputs, logsumexp, gain_q, gain_k, far_list):
    rows, cols, parts = sizes
    tokens, width = q_raw.shape[2:]
    heads = logsumexp.shape[2]
    kb = tokens // UNITS
    stat_rows = -(-heads // 8) * 8
    sides = 2 + (1 if rows == 2 else 2 if rows > 2 else 0)
    near_slots = max((cols - 1) // 2, 1)
    past_slots = max(cols - 2, 1)
    shape = jax.ShapeDtypeStruct(q_raw.shape, BF16)
    vmem = pl.BlockSpec(memory_space=pltpu.VMEM)
    anywhere = pl.BlockSpec(memory_space=pltpu.HBM)
    tile = pltpu.VMEM((tokens, width), BF16)
    near_units = pltpu.VMEM((near_slots, 2, kb, width), BF16)
    past_units = pltpu.VMEM((past_slots, 2, kb, width), BF16)
    dma = pltpu.SemaphoreType.DMA
    grads = pl.pallas_call(
        functools.partial(kernel, sizes),
        out_shape=(pltpu.VMEM(q_raw.shape, BF16),) * 3,
        in_specs=[anywhere] * 9,
        out_specs=(vmem,) * 3,
        scratch_shapes=[
            tile,
            tile,
            tile,
            tile,
            tile,
            tile,
            tile,
            pltpu.VMEM(gain_q.shape, BF16),
            pltpu.VMEM(gain_k.shape, BF16),
            pltpu.SMEM(far_list.shape, jnp.int32),
            pltpu.VMEM((2, stat_rows, tokens), F32),
            pltpu.VMEM((sides, 2, stat_rows, tokens), F32),
            pltpu.VMEM((tokens, width), F32),
            pltpu.VMEM((sides, tokens, width), BF16),
            pltpu.VMEM((sides, tokens, width), BF16),
            pltpu.VMEM((cols, 2, kb, width), BF16),
            near_units,
            near_units,
            past_units,
            past_units,
            pltpu.VMEM((sides, tokens, width), F32),
            pltpu.VMEM((sides, tokens, width), jnp.int16),
            pltpu.VMEM((sides, tokens, width), jnp.int16),
            pltpu.VMEM((sides, 8, tokens), F32),
            pltpu.VMEM((sides, 8, tokens), F32),
            pltpu.VMEM((cols, 2, kb, width), BF16),
            pltpu.VMEM((2, tokens, width), F32),
            pltpu.VMEM((3, parts, 8, 128), F32),
            dma((9,)),
            dma((sides, 2 + heads)),
            dma((sides, 2 + heads)),
            dma((cols,)),
            dma((near_slots,)),
            dma((past_slots,)),
            dma((sides, 2)),
            dma((sides, 2)),
            dma((near_slots,)),
            dma((past_slots,)),
            dma((cols,)),
            dma((3, parts)),
            dma((3, parts)),
        ],
        compiler_params=pltpu.CompilerParams(collective_id=0, has_side_effects=True),
    )(q_raw, k_raw, values, upstream, outputs, logsumexp, gain_q, gain_k, far_list)
    return pl.pallas_call(
        copy_kernel,
        out_shape=(shape, shape, shape),
        in_specs=[vmem] * 3,
        out_specs=(anywhere,) * 3,
        scratch_shapes=[dma((3,))],
        compiler_params=pltpu.CompilerParams(vmem_limit_bytes=4 << 20),
    )(*grads)


def solution(mesh):
    sizes = (mesh.shape["ha"], mesh.shape["wa"], mesh.shape["hd"])
    tile = P("ha", "wa", None, "hd")
    return jax.shard_map(
        functools.partial(body, sizes),
        mesh=mesh,
        in_specs=(tile,) * 5 + (P("ha", "wa", "hd", None), P("hd"), P("hd"), P("ha", None, None)),
        out_specs=(tile,) * 3,
        check_vma=False,
    )
```

```python
import functools
import math

import jax
import jax.numpy as jnp
from jax import lax
from jax.experimental import pallas as pl
from jax.experimental.pallas import tpu as pltpu
from jax.sharding import PartitionSpec as P

UNITS = 4
EPS = 1e-06
MESH = pl.DeviceIdType.MESH
LAST = (((1,), (1,)), ((), ()))
FIRST = (((0,), (0,)), ((), ()))
PLAIN = (((1,), (0,)), ((), ()))
LEFT, RIGHT = 0, 1
CODE_MAX = 32767.0
F32 = jnp.float32
BF16 = jnp.bfloat16


def dot(a, b, dims):
    return lax.dot_general(a, b, dims, preferred_element_type=F32)


def kernel(
    sizes,
    q_hbm,
    k_hbm,
    v_hbm,
    u_hbm,
    o_hbm,
    lse_hbm,
    gain_q_hbm,
    gain_k_hbm,
    far_hbm,
    dq_out,
    dk_out,
    dv_out,
    q_raw,
    k_raw,
    vals,
    ups,
    outs,
    qn,
    kn,
    lse_ref,
    gain_q_ref,
    gain_k_ref,
    far_ref,
    stats,
    nbr_stats,
    dq_acc,
    nbr_q,
    nbr_u,
    far_pack,
    near_in,
    near_out,
    own_in,
    own_out,
    ret_acc,
    ret_out,
    ret_in,
    ret_scale,
    ret_scale_in,
    fret_in,
    total,
    xbuf,
    load_sem,
    nbr_send,
    nbr_recv,
    far_send,
    near_recv,
    own_recv,
    ret_send,
    ret_recv,
    near_send,
    own_send,
    fret_recv,
    x_send,
    x_recv,
):
    rows, cols, parts = sizes
    row = lax.axis_index("ha")
    col = lax.axis_index("wa")
    me = lax.axis_index("hd")
    tokens, width = q_raw.shape
    heads = lse_hbm.shape[1]
    hw = width // heads
    kb = tokens // UNITS
    full_width = width * parts
    slots = far_ref.shape[2]
    near_slots = near_in.shape[0]
    own_slots = own_in.shape[0]
    score_scale = 1.0 / math.sqrt(hw)
    head_lanes = [slice(head * hw, (head + 1) * hw) for head in range(heads)]

    barrier = pltpu.get_barrier_semaphore()
    hd_ids = [{"hd": lax.rem(me + off, parts)} for off in range(1, parts)]
    for target in hd_ids:
        pl.semaphore_signal(barrier, inc=1, device_id=target, device_id_type=MESH)

    exists = [col > 0, col < cols - 1]
    ids = [{"wa": col - 1}, {"wa": col + 1}]
    facing = [RIGHT, LEFT]
    if rows == 2:
        exists.append(True)
        ids.append({"ha": 1 - row})
        facing.append(2)
        pl.semaphore_signal(barrier, inc=1, device_id=ids[2], device_id_type=MESH)
    elif rows > 2:
        exists += [row > 0, row < rows - 1]
        ids += [{"ha": row - 1}, {"ha": row + 1}]
        facing += [3, 2]
        for side in (2, 3):

            @pl.when(exists[side])
            def _(side=side):
                pl.semaphore_signal(barrier, inc=1, device_id=ids[side], device_id_type=MESH)

    sides = range(len(ids))
    upright = range(2, len(ids))
    for off in range(1, cols):
        pl.semaphore_signal(
            barrier, inc=1, device_id={"wa": lax.rem(col + off, cols)}, device_id_type=MESH
        )

    loads = []
    for index, (source, target) in enumerate(
        (
            (u_hbm.at[0, 0], ups),
            (k_hbm.at[0, 0], k_raw),
            (q_hbm.at[0, 0], q_raw),
            (o_hbm.at[0, 0], outs),
            (v_hbm.at[0, 0], vals),
            (lse_hbm.at[0], lse_ref),
            (gain_q_hbm, gain_q_ref),
            (gain_k_hbm, gain_k_ref),
            (far_hbm, far_ref),
        )
    ):
        copy = pltpu.make_async_copy(source, target, load_sem.at[index])
        copy.start()
        loads.append(copy)

    inner = (col > 0) & (col < cols - 1)

    def lane_columns(columns):
        lane = lax.broadcasted_iota(jnp.int32, (tokens, 128), 1)
        mat = jnp.zeros((tokens, 128), F32)
        for place, column in columns:
            mat = jnp.where(lane == place, column, mat)
        return mat.T

    def row_sums(block):
        acc = block[:, :hw]
        for lanes in head_lanes[1:]:
            acc = acc + block[:, lanes]
        return jnp.sum(acc, axis=1, keepdims=True)

    def to_columns(rows8):
        return jnp.concatenate([rows8] * (tokens // 8), axis=0).T

    def x_copy(which, off):
        return pltpu.make_async_remote_copy(
            src_ref=xbuf.at[which, me],
            dst_ref=xbuf.at[which, me],
            send_sem=x_send.at[which, off],
            recv_sem=x_recv.at[which, off],
            device_id=hd_ids[off - 1],
            device_id_type=MESH,
        )

    def x_start(which, rows8):
        xbuf[which, me] = rows8
        for off in range(1, parts):
            x_copy(which, off).start()

    def x_finish(which):
        for off in range(1, parts):
            x_copy(which, off).wait()
        acc = xbuf[which, 0]
        for part in range(1, parts):
            acc = acc + xbuf[which, part]
        return acc

    def side_id(side):
        if isinstance(side, int):
            return ids[side]
        return {"wa": jnp.where(side == RIGHT, col + 1, col - 1)}

    def face(side):
        return facing[side] if isinstance(side, int) else 1 - side

    def nbr_refs(side, message):
        if message == 0:
            return ups, nbr_u.at[side]
        if message == 1:
            return stats, nbr_stats.at[side]
        lanes = head_lanes[message - 2]
        return qn.at[:, lanes], nbr_q.at[side, :, lanes]

    messages = range(2 + heads)

    def nbr_copy(side, message):
        return pltpu.make_async_remote_copy(
            src_ref=nbr_refs(side, message)[0],
            dst_ref=nbr_refs(face(side), message)[1],
            send_sem=nbr_send.at[side, message],
            recv_sem=nbr_recv.at[face(side), message],
            device_id=ids[side],
            device_id_type=MESH,
        )

    def nbr_wait(side, message):
        pltpu.make_async_remote_copy(
            src_ref=nbr_refs(side, message)[0],
            dst_ref=nbr_refs(side, message)[1],
            send_sem=nbr_send.at[side, message],
            recv_sem=nbr_recv.at[side, message],
            device_id=ids[side],
            device_id_type=MESH,
        ).wait_recv()

    def nearer_left(tile):
        return 2 * tile < cols - 1

    from_left = nearer_left(col)
    behind = jnp.where(from_left, col, cols - 1 - col)
    first = jnp.where(from_left, RIGHT, LEFT)
    second = 1 - first
    has_first = jnp.where(from_left, col < cols - 1, col > 0)
    has_second = jnp.where(from_left, col > 0, col < cols - 1)

    def keeps_right(tile):
        return 2 * (tile + 1) < cols - 1

    def keeps_left(tile):
        return 2 * (tile - 1) > cols - 2

    has_own = keeps_right(col) | keeps_left(col)
    near_tiles = range(1, cols - 1)
    own_tiles = [tile for tile in range(cols) if keeps_right(tile) or keeps_left(tile)]

    def far_copy(index, tile, near):
        rank = col if nearer_left(tile) else cols - 1 - col
        landing, recv = (near_in, near_recv) if near else (own_in, own_recv)
        place = rank if near else rank - 2
        return pltpu.make_async_remote_copy(
            src_ref=far_pack.at[index],
            dst_ref=landing.at[place],
            send_sem=far_send.at[index],
            recv_sem=recv.at[place],
            device_id={"wa": tile},
            device_id_type=MESH,
        )

    def is_near(tile):
        return col < tile if nearer_left(tile) else col > tile

    def is_own(tile):
        return col > tile + 1 if keeps_right(tile) else col < tile - 1

    far_kinds = [(tile, True) for tile in near_tiles] + [(tile, False) for tile in own_tiles]

    def is_sent(tile, near):
        return is_near(tile) if near else is_own(tile)

    def near_here(place):
        return inner & (place < behind)

    def own_here(place):
        return has_own & (place >= behind)

    def ranked(rank):
        return jnp.where(from_left, rank, cols - 1 - rank)

    def far_wait(place, near):
        landing, recv = (near_in, near_recv) if near else (own_in, own_recv)
        pltpu.make_async_remote_copy(
            src_ref=far_pack.at[0],
            dst_ref=landing.at[place],
            send_sem=far_send.at[0],
            recv_sem=recv.at[place],
            device_id={"wa": ranked(place if near else place + 2)},
            device_id_type=MESH,
        ).wait_recv()

    def slot_of(near):
        if near:
            return col - 1
        after = col - cols + len(own_tiles)
        return len(near_tiles) + jnp.where(from_left, col, after)

    def fret_copy(place, near):
        source, send = (near_out, near_send) if near else (own_out, own_send)
        return pltpu.make_async_remote_copy(
            src_ref=source.at[place],
            dst_ref=fret_in.at[slot_of(near)],
            send_sem=send.at[place],
            recv_sem=fret_recv.at[slot_of(near)],
            device_id={"wa": ranked(place if near else place + 2)},
            device_id_type=MESH,
        )

    def fret_wait(index):
        pltpu.make_async_remote_copy(
            src_ref=fret_in.at[index],
            dst_ref=fret_in.at[index],
            send_sem=near_send.at[0],
            recv_sem=fret_recv.at[index],
            device_id={"wa": far_kinds[index][0]},
            device_id_type=MESH,
        ).wait_recv()

    def ret_copy(side, which):
        source, target = ((ret_out, ret_in), (ret_scale, ret_scale_in))[which]
        return pltpu.make_async_remote_copy(
            src_ref=source.at[side],
            dst_ref=target.at[face(side)],
            send_sem=ret_send.at[side, which],
            recv_sem=ret_recv.at[face(side), which],
            device_id=side_id(side),
            device_id_type=MESH,
        )

    def ret_start(side):
        part = ret_acc[side]
        largest = jnp.abs(part[:, head_lanes[0]])
        for lanes in head_lanes[1:]:
            largest = jnp.maximum(largest, jnp.abs(part[:, lanes]))
        largest = jnp.maximum(jnp.max(largest, axis=1, keepdims=True), 1e-30)
        coded = jnp.round(part * (CODE_MAX / largest))
        ret_out[side] = coded.astype(jnp.int32).astype(jnp.int16)
        ret_copy(side, 0).start()
        ret_scale[side] = lane_columns([(0, largest / CODE_MAX)])[0:8]
        ret_copy(side, 1).start()

    def ret_wait(side):
        for which in range(2):
            source, target = ((ret_out, ret_in), (ret_scale, ret_scale_in))[which]
            pltpu.make_async_remote_copy(
                src_ref=source.at[side],
                dst_ref=target.at[side],
                send_sem=ret_send.at[side, which],
                recv_sem=ret_recv.at[side, which],
                device_id=ids[side],
                device_id_type=MESH,
            ).wait_recv()

    greeted = parts - 1 + cols - 1
    if rows == 2:
        greeted = greeted + 1
    elif rows > 2:
        greeted = greeted + jnp.minimum(row, 1) + jnp.minimum(rows - 1 - row, 1)
    loads[0].wait()
    pl.semaphore_wait(barrier, greeted)
    for side in sides:

        @pl.when(exists[side])
        def _(side=side):
            nbr_copy(side, 0).start()

    loads[1].wait()
    key_wide = k_raw[...].astype(F32)
    key_squares = row_sums(key_wide * key_wide)
    loads[2].wait()
    query_wide = q_raw[...].astype(F32)
    query_squares = row_sums(query_wide * query_wide)
    x_start(0, lane_columns([(0, query_squares), (1, key_squares)])[0:8])

    loads[3].wait()
    loads[5].wait()
    delta_columns = []
    for head, lanes in enumerate(head_lanes):
        product = ups[:, lanes].astype(F32) * outs[:, lanes].astype(F32)
        delta_columns.append((head, jnp.sum(product, axis=1, keepdims=True)))
    stats[0] = lane_columns(delta_columns)[0 : stats.shape[1]]
    for head in range(heads):
        stats[1, head : head + 1, :] = lse_ref[head]
    for side in sides:

        @pl.when(exists[side])
        def _(side=side):
            nbr_copy(side, 1).start()

        @pl.when(jnp.logical_not(exists[side]))
        def _(side=side):
            nbr_u[side] = jnp.zeros(nbr_u.shape[1:], BF16)
            nbr_q[side] = jnp.zeros(nbr_q.shape[1:], BF16)
            nbr_stats[side] = jnp.zeros(nbr_stats.shape[1:], F32)
            ret_in[side] = jnp.zeros(ret_in.shape[1:], jnp.int16)
            ret_scale_in[side] = jnp.zeros(ret_scale_in.shape[1:], F32)

    for place in range(near_slots):

        @pl.when(jnp.logical_not(near_here(place)))
        def _(place=place):
            near_in[place] = jnp.zeros(near_in.shape[1:], BF16)

    for place in range(own_slots):

        @pl.when(jnp.logical_not(own_here(place)))
        def _(place=place):
            own_in[place] = jnp.zeros(own_in.shape[1:], BF16)

    loads[8].wait()
    send_unit = []
    send_used = []
    for tile, near in far_kinds:
        query_col = tile if not near else tile + 1 if nearer_left(tile) else tile - 1
        unit = jnp.int32(0)
        asked = jnp.int32(0)
        for slot in range(slots):
            wanted = far_ref[0, query_col, slot] - col * UNITS
            hit = (wanted >= 0) & (wanted < UNITS)
            unit = jnp.where(hit, wanted, unit)
            asked = jnp.where(hit, 1, asked)
        send_unit.append(unit)
        send_used.append(jnp.where(is_sent(tile, near), asked, 0))

    def place_used(place, near):
        peer = ranked(place if near else place + 2)
        query_col = col
        if near:
            query_col = jnp.clip(jnp.where(from_left, col + 1, col - 1), 0, cols - 1)
        used = jnp.int32(0)
        for slot in range(slots):
            named = far_ref[0, query_col, slot] - peer * UNITS
            used = jnp.where((named >= 0) & (named < UNITS), 1, used)
        return jnp.where(near_here(place) if near else own_here(place), used, 0)

    near_used = [place_used(place, True) for place in range(near_slots)]
    own_used = [place_used(place, False) for place in range(own_slots)]

    def pick_unit(unit_wanted, source):
        wanted = jnp.full((kb, width), unit_wanted, jnp.int32)
        picked = source[0:kb, :].astype(F32)
        for unit in range(1, UNITS):
            block = source[unit * kb : (unit + 1) * kb, :].astype(F32)
            picked = jnp.where(wanted == unit, block, picked)
        return picked.astype(BF16)

    loads[4].wait()
    for index in range(len(far_kinds)):
        far_pack[index, 1] = pick_unit(send_unit[index], vals)

    loads[6].wait()
    loads[7].wait()
    gain_q = gain_q_ref[...].astype(F32).reshape(1, width)
    gain_k = gain_k_ref[...].astype(F32).reshape(1, width)
    rates = lax.rsqrt(x_finish(0) / full_width + EPS)
    rate_columns = to_columns(rates)
    q_rate = rate_columns[:, 0:1]
    k_rate = rate_columns[:, 1:2]
    qn[...] = (q_raw[...].astype(F32) * q_rate * gain_q).astype(BF16)
    for side in sides:

        @pl.when(exists[side])
        def _(side=side):
            for head in range(heads):
                nbr_copy(side, 2 + head).start()

    kn[...] = (k_raw[...].astype(F32) * k_rate * gain_k).astype(BF16)
    for index, (tile, near) in enumerate(far_kinds):
        far_pack[index, 0] = pick_unit(send_unit[index], kn)

        @pl.when(is_sent(tile, near))
        def _(index=index, tile=tile, near=near):
            far_copy(index, tile, near).start()

    def attend(keys, values, queries, upstream, delta_row, lse_row, used=None):
        weight = jnp.exp(dot(keys, queries, LAST) * score_scale - lse_row)
        if used is not None:
            weight = jnp.where(used, weight, 0.0)
        dweight = dot(values, upstream, LAST)
        dscore = (weight * (dweight - delta_row)).astype(BF16)
        weight_low = weight.astype(BF16)
        dq_part = dot(dscore, keys, FIRST)
        dk_parts, dv_parts = [], []
        for start in range(0, queries.shape[0], tokens):
            block = slice(start, start + tokens)
            dk_part = dot(dscore[:, block], queries[block], PLAIN) * score_scale
            dk_parts.append(dk_part.astype(BF16))
            dv_parts.append(dot(weight_low[:, block], upstream[block], PLAIN).astype(BF16))
        return dq_part, dk_parts, dv_parts

    for head, lanes in enumerate(head_lanes):
        dq_part, (dk_part,), (dv_part,) = attend(
            kn[:, lanes],
            vals[:, lanes],
            qn[:, lanes],
            ups[:, lanes],
            stats[0, head : head + 1, :],
            stats[1, head : head + 1, :],
        )
        dq_acc[:, lanes] = dq_part
        total[0, :, lanes] = dk_part.astype(F32)
        total[1, :, lanes] = dv_part.astype(F32)

    def stat_row(which, head):
        return jnp.concatenate([nbr_stats[side, which, head : head + 1, :] for side in sides], axis=1)

    for head, lanes in enumerate(head_lanes):
        for side in sides:

            @pl.when(exists[side])
            def _(side=side, head=head):
                for message in (0, 1, 2) if head == 0 else (2 + head,):
                    nbr_wait(side, message)

        dq_part, dk_parts, dv_parts = attend(
            kn[:, lanes],
            vals[:, lanes],
            nbr_q[:, :, lanes].reshape(len(sides) * tokens, hw),
            nbr_u[:, :, lanes].reshape(len(sides) * tokens, hw),
            stat_row(0, head),
            stat_row(1, head),
        )
        ret_acc[:, :, lanes] = dq_part.reshape(len(sides), tokens, hw)
        for which, terms in enumerate((dk_parts, dv_parts)):
            acc = total[which, :, lanes]
            for term in terms:
                acc = acc + term.astype(F32)
            total[which, :, lanes] = acc

    for side in upright:

        @pl.when(exists[side])
        def _(side=side):
            ret_start(side)

    def far_pass(near):
        landing, outgoing = (near_in, near_out) if near else (own_in, own_out)
        flags = near_used if near else own_used
        here = near_here if near else own_here
        count = len(flags)
        for place in range(count):

            @pl.when(here(place))
            def _(place=place):
                far_wait(place, near)

        used = jnp.concatenate([jnp.full((kb, tokens), flag, jnp.int32) for flag in flags], axis=0) > 0
        for head, lanes in enumerate(head_lanes):
            dq_part, (dk_part,), (dv_part,) = attend(
                landing[:, 0, :, lanes].reshape(count * kb, hw),
                landing[:, 1, :, lanes].reshape(count * kb, hw),
                nbr_q[first, :, lanes] if near else qn[:, lanes],
                nbr_u[first, :, lanes] if near else ups[:, lanes],
                nbr_stats[first, 0, head : head + 1, :] if near else stats[0, head : head + 1, :],
                nbr_stats[first, 1, head : head + 1, :] if near else stats[1, head : head + 1, :],
                used,
            )
            if near:
                ret_acc[first, :, lanes] += dq_part
            else:
                dq_acc[:, lanes] += dq_part
            outgoing[:, 0, :, lanes] = dk_part.reshape(count, kb, hw)
            outgoing[:, 1, :, lanes] = dv_part.reshape(count, kb, hw)
        for place in range(count):

            @pl.when(here(place))
            def _(place=place):
                fret_copy(place, near).start()

    if near_tiles:

        @pl.when(inner)
        def _():
            far_pass(True)

    @pl.when(has_first)
    def _():
        ret_start(first)

    @pl.when(has_second)
    def _():
        ret_start(second)

    if own_tiles:

        @pl.when(has_own)
        def _():
            far_pass(False)

    for side in sides:

        @pl.when(exists[side])
        def _(side=side):
            ret_wait(side)

    dq_sum = dq_acc[...]
    for side in sides:
        scale = to_columns(ret_scale_in[side])[:, 0:1]
        dq_sum = dq_sum + ret_in[side].astype(jnp.int32).astype(F32) * scale
    dq_norm = (dq_sum * score_scale).astype(BF16).astype(F32)
    query_wide = q_raw[...].astype(F32)
    weighted = gain_q * dq_norm
    x_start(1, lane_columns([(0, row_sums(weighted * query_wide))])[0:8])

    for index, (tile, near) in enumerate(far_kinds):

        @pl.when(is_sent(tile, near))
        def _(index=index):
            fret_wait(index)

    for unit in range(UNITS):
        place = slice(unit * kb, (unit + 1) * kb)
        for which in range(2):
            acc = total[which, place, :]
            for index in range(len(far_kinds)):
                picked = jnp.where(send_unit[index] == unit, send_used[index], 0)
                spread = jnp.full((kb, width), picked, jnp.int32) > 0
                acc = acc + jnp.where(spread, fret_in[index, which].astype(F32), 0.0)
            total[which, place, :] = acc

    dk_norm = total[0].astype(BF16).astype(F32)
    key_wide = k_raw[...].astype(F32)
    key_weighted = gain_k * dk_norm
    x_start(2, lane_columns([(1, row_sums(key_weighted * key_wide))])[0:8])
    dv_out[0, 0] = total[1].astype(BF16)

    q_factor = rates * rates * rates * x_finish(1) / full_width
    q_factor = to_columns(q_factor)[:, 0:1]
    dq_out[0, 0] = (q_rate * weighted - query_wide * q_factor).astype(BF16)

    for side in sides:

        @pl.when(exists[side])
        def _(side=side):
            for message in messages:
                nbr_copy(side, message).wait_send()
            for which in range(2):
                ret_copy(side, which).wait_send()

    for index, (tile, near) in enumerate(far_kinds):

        @pl.when(is_sent(tile, near))
        def _(index=index, tile=tile, near=near):
            far_copy(index, tile, near).wait_send()

    for place in range(near_slots):

        @pl.when(near_here(place))
        def _(place=place):
            fret_copy(place, True).wait_send()

    for place in range(own_slots):

        @pl.when(own_here(place))
        def _(place=place):
            fret_copy(place, False).wait_send()

    k_factor = rates * rates * rates * x_finish(2) / full_width
    k_factor = to_columns(k_factor)[:, 1:2]
    dk_out[0, 0] = (k_rate * key_weighted - key_wide * k_factor).astype(BF16)


def copy_kernel(dq_in, dk_in, dv_in, dq_out, dk_out, dv_out, sem):
    pairs = ((dq_in, dq_out), (dk_in, dk_out), (dv_in, dv_out))
    copies = [
        pltpu.make_async_copy(source, target, sem.at[index])
        for index, (source, target) in enumerate(pairs)
    ]
    for copy in copies:
        copy.start()
    for copy in copies:
        copy.wait()


def body(sizes, q_raw, k_raw, values, upstream, outputs, logsumexp, gain_q, gain_k, far_list):
    rows, cols, parts = sizes
    tokens, width = q_raw.shape[2:]
    heads = logsumexp.shape[2]
    lse = logsumexp.transpose(0, 2, 1, 3)
    kb = tokens // UNITS
    stat_rows = -(-heads // 8) * 8
    sides = 2 + (1 if rows == 2 else 2 if rows > 2 else 0)
    near_slots = max((cols - 1) // 2, 1)
    own_slots = max(cols - 2, 1)
    kinds = max(2 * cols, 1)
    shape = jax.ShapeDtypeStruct(q_raw.shape, BF16)
    vmem = pl.BlockSpec(memory_space=pltpu.VMEM)
    anywhere = pl.BlockSpec(memory_space=pltpu.HBM)
    tile = pltpu.VMEM((tokens, width), BF16)
    near_units = pltpu.VMEM((near_slots, 2, kb, width), BF16)
    own_units = pltpu.VMEM((own_slots, 2, kb, width), BF16)
    dma = pltpu.SemaphoreType.DMA
    grads = pl.pallas_call(
        functools.partial(kernel, sizes),
        out_shape=(pltpu.VMEM(q_raw.shape, BF16),) * 3,
        in_specs=[anywhere] * 9,
        out_specs=(vmem,) * 3,
        scratch_shapes=[
            tile,
            tile,
            tile,
            tile,
            tile,
            tile,
            tile,
            pltpu.VMEM(lse.shape[1:], F32),
            pltpu.VMEM(gain_q.shape, BF16),
            pltpu.VMEM(gain_k.shape, BF16),
            pltpu.SMEM(far_list.shape, jnp.int32),
            pltpu.VMEM((2, stat_rows, tokens), F32),
            pltpu.VMEM((sides, 2, stat_rows, tokens), F32),
            pltpu.VMEM((tokens, width), F32),
            pltpu.VMEM((sides, tokens, width), BF16),
            pltpu.VMEM((sides, tokens, width), BF16),
            pltpu.VMEM((kinds, 2, kb, width), BF16),
            near_units,
            near_units,
            own_units,
            own_units,
            pltpu.VMEM((sides, tokens, width), F32),
            pltpu.VMEM((sides, tokens, width), jnp.int16),
            pltpu.VMEM((sides, tokens, width), jnp.int16),
            pltpu.VMEM((sides, 8, tokens), F32),
            pltpu.VMEM((sides, 8, tokens), F32),
            pltpu.VMEM((kinds, 2, kb, width), BF16),
            pltpu.VMEM((2, tokens, width), F32),
            pltpu.VMEM((3, parts, 8, 128), F32),
            dma((9,)),
            dma((sides, 2 + heads)),
            dma((sides, 2 + heads)),
            dma((kinds,)),
            dma((near_slots,)),
            dma((own_slots,)),
            dma((sides, 2)),
            dma((sides, 2)),
            dma((near_slots,)),
            dma((own_slots,)),
            dma((kinds,)),
            dma((3, parts)),
            dma((3, parts)),
        ],
        compiler_params=pltpu.CompilerParams(collective_id=0, has_side_effects=True),
    )(q_raw, k_raw, values, upstream, outputs, lse, gain_q, gain_k, far_list)
    return pl.pallas_call(
        copy_kernel,
        out_shape=(shape, shape, shape),
        in_specs=[vmem] * 3,
        out_specs=(anywhere,) * 3,
        scratch_shapes=[dma((3,))],
        compiler_params=pltpu.CompilerParams(vmem_limit_bytes=4 << 20),
    )(*grads)


def solution(mesh):
    sizes = (mesh.shape["ha"], mesh.shape["wa"], mesh.shape["hd"])
    tile = P("ha", "wa", None, "hd")
    return jax.shard_map(
        functools.partial(body, sizes),
        mesh=mesh,
        in_specs=(tile,) * 5 + (P("ha", "wa", "hd", None), P("hd"), P("hd"), P("ha", None, None)),
        out_specs=(tile,) * 3,
        check_vma=False,
    )
```

```python
import functools
import math

import jax
import jax.numpy as jnp
from jax import lax
from jax.experimental import pallas as pl
from jax.experimental.pallas import tpu as pltpu
from jax.sharding import PartitionSpec as P

UNITS = 4
EPS = 1e-06
MESH = pl.DeviceIdType.MESH
LAST = (((1,), (1,)), ((), ()))
FIRST = (((0,), (0,)), ((), ()))
PLAIN = (((1,), (0,)), ((), ()))
LEFT, RIGHT = 0, 1
CODE_MAX = 32767.0
F32 = jnp.float32
BF16 = jnp.bfloat16


def dot(a, b, dims):
    return lax.dot_general(a, b, dims, preferred_element_type=F32)


def kernel(
    sizes,
    q_hbm,
    k_hbm,
    v_hbm,
    u_hbm,
    o_hbm,
    lse_hbm,
    gain_q_hbm,
    gain_k_hbm,
    far_hbm,
    dq_out,
    dk_out,
    dv_out,
    q_raw,
    k_raw,
    vals,
    ups,
    outs,
    qn,
    kn,
    lse_ref,
    gain_q_ref,
    gain_k_ref,
    far_ref,
    stats,
    nbr_stats,
    dq_acc,
    nbr_q,
    nbr_u,
    far_pack,
    near_in,
    near_out,
    own_in,
    own_out,
    ret_acc,
    ret_out,
    ret_in,
    ret_scale,
    ret_scale_in,
    fret_in,
    total,
    xbuf,
    load_sem,
    nbr_send,
    nbr_recv,
    far_send,
    near_recv,
    own_recv,
    ret_send,
    ret_recv,
    near_send,
    own_send,
    fret_recv,
    x_send,
    x_recv,
):
    rows, cols, parts = sizes
    row = lax.axis_index("ha")
    col = lax.axis_index("wa")
    me = lax.axis_index("hd")
    tokens, width = q_raw.shape
    heads = lse_hbm.shape[1]
    hw = width // heads
    kb = tokens // UNITS
    full_width = width * parts
    slots = far_ref.shape[2]
    near_slots = near_in.shape[0]
    own_slots = own_in.shape[0]
    score_scale = 1.0 / math.sqrt(hw)
    head_lanes = [slice(head * hw, (head + 1) * hw) for head in range(heads)]

    barrier = pltpu.get_barrier_semaphore()
    hd_ids = [{"hd": lax.rem(me + off, parts)} for off in range(1, parts)]
    for target in hd_ids:
        pl.semaphore_signal(barrier, inc=1, device_id=target, device_id_type=MESH)

    exists = [col > 0, col < cols - 1]
    ids = [{"wa": col - 1}, {"wa": col + 1}]
    facing = [RIGHT, LEFT]
    if rows == 2:
        exists.append(True)
        ids.append({"ha": 1 - row})
        facing.append(2)
        pl.semaphore_signal(barrier, inc=1, device_id=ids[2], device_id_type=MESH)
    elif rows > 2:
        exists += [row > 0, row < rows - 1]
        ids += [{"ha": row - 1}, {"ha": row + 1}]
        facing += [3, 2]
        for side in (2, 3):

            @pl.when(exists[side])
            def _(side=side):
                pl.semaphore_signal(barrier, inc=1, device_id=ids[side], device_id_type=MESH)

    sides = range(len(ids))
    upright = range(2, len(ids))
    for off in range(1, cols):
        pl.semaphore_signal(
            barrier, inc=1, device_id={"wa": lax.rem(col + off, cols)}, device_id_type=MESH
        )

    loads = []
    for index, (source, target) in enumerate(
        (
            (u_hbm.at[0, 0], ups),
            (k_hbm.at[0, 0], k_raw),
            (q_hbm.at[0, 0], q_raw),
            (o_hbm.at[0, 0], outs),
            (v_hbm.at[0, 0], vals),
            (lse_hbm.at[0], lse_ref),
            (gain_q_hbm, gain_q_ref),
            (gain_k_hbm, gain_k_ref),
            (far_hbm, far_ref),
        )
    ):
        copy = pltpu.make_async_copy(source, target, load_sem.at[index])
        copy.start()
        loads.append(copy)

    inner = (col > 0) & (col < cols - 1)

    def lane_columns(columns):
        lane = lax.broadcasted_iota(jnp.int32, (tokens, 128), 1)
        mat = jnp.zeros((tokens, 128), F32)
        for place, column in columns:
            mat = jnp.where(lane == place, column, mat)
        return mat.T

    def row_sums(block):
        acc = block[:, :hw]
        for lanes in head_lanes[1:]:
            acc = acc + block[:, lanes]
        return jnp.sum(acc, axis=1, keepdims=True)

    def to_columns(rows8):
        return jnp.concatenate([rows8] * (tokens // 8), axis=0).T

    def x_copy(which, off):
        return pltpu.make_async_remote_copy(
            src_ref=xbuf.at[which, me],
            dst_ref=xbuf.at[which, me],
            send_sem=x_send.at[which, off],
            recv_sem=x_recv.at[which, off],
            device_id=hd_ids[off - 1],
            device_id_type=MESH,
        )

    def x_start(which, rows8):
        xbuf[which, me] = rows8
        for off in range(1, parts):
            x_copy(which, off).start()

    def x_finish(which):
        for off in range(1, parts):
            x_copy(which, off).wait()
        acc = xbuf[which, 0]
        for part in range(1, parts):
            acc = acc + xbuf[which, part]
        return acc

    def side_id(side):
        if isinstance(side, int):
            return ids[side]
        return {"wa": jnp.where(side == RIGHT, col + 1, col - 1)}

    def face(side):
        return facing[side] if isinstance(side, int) else 1 - side

    def nbr_refs(side, message):
        if message == 0:
            return ups, nbr_u.at[side]
        if message == 1:
            return stats, nbr_stats.at[side]
        lanes = head_lanes[message - 2]
        return qn.at[:, lanes], nbr_q.at[side, :, lanes]

    messages = range(2 + heads)

    def nbr_copy(side, message):
        return pltpu.make_async_remote_copy(
            src_ref=nbr_refs(side, message)[0],
            dst_ref=nbr_refs(face(side), message)[1],
            send_sem=nbr_send.at[side, message],
            recv_sem=nbr_recv.at[face(side), message],
            device_id=ids[side],
            device_id_type=MESH,
        )

    def nbr_wait(side, message):
        pltpu.make_async_remote_copy(
            src_ref=nbr_refs(side, message)[0],
            dst_ref=nbr_refs(side, message)[1],
            send_sem=nbr_send.at[side, message],
            recv_sem=nbr_recv.at[side, message],
            device_id=ids[side],
            device_id_type=MESH,
        ).wait_recv()

    def nearer_left(tile):
        return 2 * tile < cols - 1

    from_left = nearer_left(col)
    behind = jnp.where(from_left, col, cols - 1 - col)
    first = jnp.where(from_left, RIGHT, LEFT)
    second = 1 - first
    has_first = jnp.where(from_left, col < cols - 1, col > 0)
    has_second = jnp.where(from_left, col > 0, col < cols - 1)

    def keeps_right(tile):
        return 2 * (tile + 1) < cols - 1

    def keeps_left(tile):
        return 2 * (tile - 1) > cols - 2

    has_own = keeps_right(col) | keeps_left(col)
    near_tiles = range(1, cols - 1)
    own_tiles = [tile for tile in range(cols) if keeps_right(tile) or keeps_left(tile)]

    def far_copy(index, tile, near):
        rank = col if nearer_left(tile) else cols - 1 - col
        landing, recv = (near_in, near_recv) if near else (own_in, own_recv)
        place = rank if near else rank - 2
        return pltpu.make_async_remote_copy(
            src_ref=far_pack.at[index],
            dst_ref=landing.at[place],
            send_sem=far_send.at[index],
            recv_sem=recv.at[place],
            device_id={"wa": tile},
            device_id_type=MESH,
        )

    def is_near(tile):
        return col < tile if nearer_left(tile) else col > tile

    def is_own(tile):
        return col > tile + 1 if keeps_right(tile) else col < tile - 1

    far_kinds = [(tile, True) for tile in near_tiles] + [(tile, False) for tile in own_tiles]

    def is_sent(tile, near):
        return is_near(tile) if near else is_own(tile)

    def near_here(place):
        return inner & (place < behind)

    def own_here(place):
        return has_own & (place >= behind)

    def ranked(rank):
        return jnp.where(from_left, rank, cols - 1 - rank)

    def far_wait(place, near):
        landing, recv = (near_in, near_recv) if near else (own_in, own_recv)
        pltpu.make_async_remote_copy(
            src_ref=far_pack.at[0],
            dst_ref=landing.at[place],
            send_sem=far_send.at[0],
            recv_sem=recv.at[place],
            device_id={"wa": ranked(place if near else place + 2)},
            device_id_type=MESH,
        ).wait_recv()

    def slot_of(near):
        if near:
            return col - 1
        after = col - cols + len(own_tiles)
        return len(near_tiles) + jnp.where(from_left, col, after)

    def fret_copy(place, near, which):
        source, send = (near_out, near_send) if near else (own_out, own_send)
        return pltpu.make_async_remote_copy(
            src_ref=source.at[place, which],
            dst_ref=fret_in.at[slot_of(near), which],
            send_sem=send.at[place, which],
            recv_sem=fret_recv.at[slot_of(near), which],
            device_id={"wa": ranked(place if near else place + 2)},
            device_id_type=MESH,
        )

    def fret_wait(index, which):
        pltpu.make_async_remote_copy(
            src_ref=fret_in.at[index, which],
            dst_ref=fret_in.at[index, which],
            send_sem=near_send.at[0, which],
            recv_sem=fret_recv.at[index, which],
            device_id={"wa": far_kinds[index][0]},
            device_id_type=MESH,
        ).wait_recv()

    def ret_copy(side, which):
        source, target = ((ret_out, ret_in), (ret_scale, ret_scale_in))[which]
        return pltpu.make_async_remote_copy(
            src_ref=source.at[side],
            dst_ref=target.at[face(side)],
            send_sem=ret_send.at[side, which],
            recv_sem=ret_recv.at[face(side), which],
            device_id=side_id(side),
            device_id_type=MESH,
        )

    def ret_start(side):
        part = ret_acc[side]
        largest = jnp.abs(part[:, head_lanes[0]])
        for lanes in head_lanes[1:]:
            largest = jnp.maximum(largest, jnp.abs(part[:, lanes]))
        largest = jnp.maximum(jnp.max(largest, axis=1, keepdims=True), 1e-30)
        coded = jnp.round(part * (CODE_MAX / largest))
        ret_out[side] = coded.astype(jnp.int32).astype(jnp.int16)
        ret_copy(side, 0).start()
        ret_scale[side] = lane_columns([(0, largest / CODE_MAX)])[0:8]
        ret_copy(side, 1).start()

    def ret_wait(side):
        for which in range(2):
            source, target = ((ret_out, ret_in), (ret_scale, ret_scale_in))[which]
            pltpu.make_async_remote_copy(
                src_ref=source.at[side],
                dst_ref=target.at[side],
                send_sem=ret_send.at[side, which],
                recv_sem=ret_recv.at[side, which],
                device_id=ids[side],
                device_id_type=MESH,
            ).wait_recv()

    greeted = parts - 1 + cols - 1
    if rows == 2:
        greeted = greeted + 1
    elif rows > 2:
        greeted = greeted + jnp.minimum(row, 1) + jnp.minimum(rows - 1 - row, 1)
    loads[0].wait()
    pl.semaphore_wait(barrier, greeted)
    for side in sides:

        @pl.when(exists[side])
        def _(side=side):
            nbr_copy(side, 0).start()

    loads[1].wait()
    key_wide = k_raw[...].astype(F32)
    key_squares = row_sums(key_wide * key_wide)
    loads[2].wait()
    query_wide = q_raw[...].astype(F32)
    query_squares = row_sums(query_wide * query_wide)
    x_start(0, lane_columns([(0, query_squares), (1, key_squares)])[0:8])

    loads[3].wait()
    loads[5].wait()
    delta_columns = []
    for head, lanes in enumerate(head_lanes):
        product = ups[:, lanes].astype(F32) * outs[:, lanes].astype(F32)
        delta_columns.append((head, jnp.sum(product, axis=1, keepdims=True)))
    stats[0] = lane_columns(delta_columns)[0 : stats.shape[1]]
    for head in range(heads):
        stats[1, head : head + 1, :] = lse_ref[head]
    for side in sides:

        @pl.when(exists[side])
        def _(side=side):
            nbr_copy(side, 1).start()

        @pl.when(jnp.logical_not(exists[side]))
        def _(side=side):
            nbr_u[side] = jnp.zeros(nbr_u.shape[1:], BF16)
            nbr_q[side] = jnp.zeros(nbr_q.shape[1:], BF16)
            nbr_stats[side] = jnp.zeros(nbr_stats.shape[1:], F32)
            ret_in[side] = jnp.zeros(ret_in.shape[1:], jnp.int16)
            ret_scale_in[side] = jnp.zeros(ret_scale_in.shape[1:], F32)

    for place in range(near_slots):

        @pl.when(jnp.logical_not(near_here(place)))
        def _(place=place):
            near_in[place] = jnp.zeros(near_in.shape[1:], BF16)

    for place in range(own_slots):

        @pl.when(jnp.logical_not(own_here(place)))
        def _(place=place):
            own_in[place] = jnp.zeros(own_in.shape[1:], BF16)

    loads[8].wait()
    send_unit = []
    send_used = []
    for tile, near in far_kinds:
        query_col = tile if not near else tile + 1 if nearer_left(tile) else tile - 1
        unit = jnp.int32(0)
        asked = jnp.int32(0)
        for slot in range(slots):
            wanted = far_ref[0, query_col, slot] - col * UNITS
            hit = (wanted >= 0) & (wanted < UNITS)
            unit = jnp.where(hit, wanted, unit)
            asked = jnp.where(hit, 1, asked)
        send_unit.append(unit)
        send_used.append(jnp.where(is_sent(tile, near), asked, 0))

    def place_used(place, near):
        peer = ranked(place if near else place + 2)
        query_col = col
        if near:
            query_col = jnp.clip(jnp.where(from_left, col + 1, col - 1), 0, cols - 1)
        used = jnp.int32(0)
        for slot in range(slots):
            named = far_ref[0, query_col, slot] - peer * UNITS
            used = jnp.where((named >= 0) & (named < UNITS), 1, used)
        return jnp.where(near_here(place) if near else own_here(place), used, 0)

    near_used = [place_used(place, True) for place in range(near_slots)]
    own_used = [place_used(place, False) for place in range(own_slots)]

    def pick_unit(unit_wanted, source):
        wanted = jnp.full((kb, width), unit_wanted, jnp.int32)
        picked = source[0:kb, :].astype(F32)
        for unit in range(1, UNITS):
            block = source[unit * kb : (unit + 1) * kb, :].astype(F32)
            picked = jnp.where(wanted == unit, block, picked)
        return picked.astype(BF16)

    loads[4].wait()
    for index in range(len(far_kinds)):
        far_pack[index, 1] = pick_unit(send_unit[index], vals)

    loads[6].wait()
    loads[7].wait()
    gain_q = gain_q_ref[...].astype(F32).reshape(1, width)
    gain_k = gain_k_ref[...].astype(F32).reshape(1, width)
    rates = lax.rsqrt(x_finish(0) / full_width + EPS)
    rate_columns = to_columns(rates)
    q_rate = rate_columns[:, 0:1]
    k_rate = rate_columns[:, 1:2]
    kn[...] = (k_raw[...].astype(F32) * k_rate * gain_k).astype(BF16)

    def far_start(early):
        for index, (tile, near) in enumerate(far_kinds):
            soon = jnp.logical_or(near, (col - tile) * (col - tile) == 4)

            @pl.when(is_sent(tile, near) & (soon if early else jnp.logical_not(soon)))
            def _(index=index, tile=tile, near=near):
                far_pack[index, 0] = pick_unit(send_unit[index], kn)
                far_copy(index, tile, near).start()

    far_start(True)
    qn[...] = (q_raw[...].astype(F32) * q_rate * gain_q).astype(BF16)
    for side in sides:

        @pl.when(exists[side])
        def _(side=side):
            for head in range(heads):
                nbr_copy(side, 2 + head).start()

    far_start(False)

    def attend(keys, values, queries, upstream, delta_row, lse_row, used=None):
        weight = jnp.exp(dot(keys, queries, LAST) * score_scale - lse_row)
        if used is not None:
            weight = jnp.where(used, weight, 0.0)
        dweight = dot(values, upstream, LAST)
        dscore = (weight * (dweight - delta_row)).astype(BF16)
        weight_low = weight.astype(BF16)
        dq_part = dot(dscore, keys, FIRST)
        dk_parts, dv_parts = [], []
        for start in range(0, queries.shape[0], tokens):
            block = slice(start, start + tokens)
            dk_part = dot(dscore[:, block], queries[block], PLAIN) * score_scale
            dk_parts.append(dk_part.astype(BF16))
            dv_parts.append(dot(weight_low[:, block], upstream[block], PLAIN).astype(BF16))
        return dq_part, dk_parts, dv_parts

    for head, lanes in enumerate(head_lanes):
        dq_part, (dk_part,), (dv_part,) = attend(
            kn[:, lanes],
            vals[:, lanes],
            qn[:, lanes],
            ups[:, lanes],
            stats[0, head : head + 1, :],
            stats[1, head : head + 1, :],
        )
        dq_acc[:, lanes] = dq_part
        total[0, :, lanes] = dk_part.astype(F32)
        total[1, :, lanes] = dv_part.astype(F32)

    def own_pass(place):
        far_wait(place, False)
        used = jnp.full((kb, tokens), own_used[place], jnp.int32) > 0
        for head, lanes in enumerate(head_lanes):
            dq_part, (dk_part,), (dv_part,) = attend(
                own_in[place, 0, :, lanes],
                own_in[place, 1, :, lanes],
                qn[:, lanes],
                ups[:, lanes],
                stats[0, head : head + 1, :],
                stats[1, head : head + 1, :],
                used,
            )
            dq_acc[:, lanes] += dq_part
            own_out[place, 0, :, lanes] = dk_part
            own_out[place, 1, :, lanes] = dv_part
        for which in range(2):
            fret_copy(place, False, which).start()

    def stat_row(which, head):
        return jnp.concatenate([nbr_stats[side, which, head : head + 1, :] for side in sides], axis=1)

    for place in range(own_slots)[:1]:

        @pl.when(own_here(place))
        def _(place=place):
            own_pass(place)

    for place in range(near_slots):

        @pl.when(near_here(place))
        def _(place=place):
            far_wait(place, True)

    near_mask = (
        jnp.concatenate([jnp.full((kb, tokens), flag, jnp.int32) for flag in near_used], axis=0) > 0
    )
    for head, lanes in enumerate(head_lanes):
        for side in sides:

            @pl.when(exists[side])
            def _(side=side, head=head):
                for message in (0, 1, 2) if head == 0 else (2 + head,):
                    nbr_wait(side, message)

        dq_part, dk_parts, dv_parts = attend(
            kn[:, lanes],
            vals[:, lanes],
            nbr_q[:, :, lanes].reshape(len(sides) * tokens, hw),
            nbr_u[:, :, lanes].reshape(len(sides) * tokens, hw),
            stat_row(0, head),
            stat_row(1, head),
        )
        ret_acc[:, :, lanes] = dq_part.reshape(len(sides), tokens, hw)
        for which, terms in enumerate((dk_parts, dv_parts)):
            acc = total[which, :, lanes]
            for term in terms:
                acc = acc + term.astype(F32)
            total[which, :, lanes] = acc
        dq_part, (dk_part,), (dv_part,) = attend(
            near_in[:, 0, :, lanes].reshape(near_slots * kb, hw),
            near_in[:, 1, :, lanes].reshape(near_slots * kb, hw),
            nbr_q[first, :, lanes],
            nbr_u[first, :, lanes],
            nbr_stats[first, 0, head : head + 1, :],
            nbr_stats[first, 1, head : head + 1, :],
            near_mask,
        )
        ret_acc[first, :, lanes] += dq_part
        near_out[:, 0, :, lanes] = dk_part.reshape(near_slots, kb, hw)
        near_out[:, 1, :, lanes] = dv_part.reshape(near_slots, kb, hw)

    @pl.when(has_first)
    def _():
        ret_start(first)

    for side in upright:

        @pl.when(exists[side])
        def _(side=side):
            ret_start(side)

    @pl.when(has_second)
    def _():
        ret_start(second)

    for place in range(near_slots):

        @pl.when(near_here(place))
        def _(place=place):
            for which in range(2):
                fret_copy(place, True, which).start()

    for place in range(own_slots)[1:]:

        @pl.when(own_here(place))
        def _(place=place):
            own_pass(place)

    for side in sides:

        @pl.when(exists[side])
        def _(side=side):
            ret_wait(side)

    dq_sum = dq_acc[...]
    for side in sides:
        scale = to_columns(ret_scale_in[side])[:, 0:1]
        dq_sum = dq_sum + ret_in[side].astype(jnp.int32).astype(F32) * scale
    dq_norm = (dq_sum * score_scale).astype(BF16).astype(F32)
    query_wide = q_raw[...].astype(F32)
    weighted = gain_q * dq_norm
    x_start(1, lane_columns([(0, row_sums(weighted * query_wide))])[0:8])

    def add_far(which):
        for index, (tile, near) in enumerate(far_kinds):

            @pl.when(is_sent(tile, near))
            def _(index=index):
                fret_wait(index, which)

        blocks = []
        for unit in range(UNITS):
            acc = total[which, unit * kb : (unit + 1) * kb, :]
            for index in range(len(far_kinds)):
                picked = jnp.where(send_unit[index] == unit, send_used[index], 0)
                spread = jnp.full((kb, width), picked, jnp.int32) > 0
                acc = acc + jnp.where(spread, fret_in[index, which].astype(F32), 0.0)
            blocks.append(acc)
        return jnp.concatenate(blocks, axis=0).astype(BF16)

    dk_norm = add_far(0).astype(F32)
    key_wide = k_raw[...].astype(F32)
    key_weighted = gain_k * dk_norm
    x_start(2, lane_columns([(1, row_sums(key_weighted * key_wide))])[0:8])

    q_factor = rates * rates * rates * x_finish(1) / full_width
    q_factor = to_columns(q_factor)[:, 0:1]
    dq_out[0, 0] = (q_rate * weighted - query_wide * q_factor).astype(BF16)

    dv_out[0, 0] = add_far(1)
    for side in sides:

        @pl.when(exists[side])
        def _(side=side):
            for message in messages:
                nbr_copy(side, message).wait_send()
            for which in range(2):
                ret_copy(side, which).wait_send()

    for index, (tile, near) in enumerate(far_kinds):

        @pl.when(is_sent(tile, near))
        def _(index=index, tile=tile, near=near):
            far_copy(index, tile, near).wait_send()

    for place in range(near_slots):

        @pl.when(near_here(place))
        def _(place=place):
            for which in range(2):
                fret_copy(place, True, which).wait_send()

    for place in range(own_slots):

        @pl.when(own_here(place))
        def _(place=place):
            for which in range(2):
                fret_copy(place, False, which).wait_send()

    k_factor = rates * rates * rates * x_finish(2) / full_width
    k_factor = to_columns(k_factor)[:, 1:2]
    dk_out[0, 0] = (k_rate * key_weighted - key_wide * k_factor).astype(BF16)


def copy_kernel(dq_in, dk_in, dv_in, dq_out, dk_out, dv_out, sem):
    pairs = ((dq_in, dq_out), (dk_in, dk_out), (dv_in, dv_out))
    copies = [
        pltpu.make_async_copy(source, target, sem.at[index])
        for index, (source, target) in enumerate(pairs)
    ]
    for copy in copies:
        copy.start()
    for copy in copies:
        copy.wait()


def body(sizes, q_raw, k_raw, values, upstream, outputs, logsumexp, gain_q, gain_k, far_list):
    rows, cols, parts = sizes
    tokens, width = q_raw.shape[2:]
    heads = logsumexp.shape[2]
    lse = logsumexp.transpose(0, 2, 1, 3)
    kb = tokens // UNITS
    stat_rows = -(-heads // 8) * 8
    sides = 2 + (1 if rows == 2 else 2 if rows > 2 else 0)
    near_slots = max((cols - 1) // 2, 1)
    own_slots = max(cols - 2, 1)
    kinds = max(2 * cols, 1)
    shape = jax.ShapeDtypeStruct(q_raw.shape, BF16)
    vmem = pl.BlockSpec(memory_space=pltpu.VMEM)
    anywhere = pl.BlockSpec(memory_space=pltpu.HBM)
    tile = pltpu.VMEM((tokens, width), BF16)
    near_units = pltpu.VMEM((near_slots, 2, kb, width), BF16)
    own_units = pltpu.VMEM((own_slots, 2, kb, width), BF16)
    dma = pltpu.SemaphoreType.DMA
    grads = pl.pallas_call(
        functools.partial(kernel, sizes),
        out_shape=(pltpu.VMEM(q_raw.shape, BF16),) * 3,
        in_specs=[anywhere] * 9,
        out_specs=(vmem,) * 3,
        scratch_shapes=[
            tile,
            tile,
            tile,
            tile,
            tile,
            tile,
            tile,
            pltpu.VMEM(lse.shape[1:], F32),
            pltpu.VMEM(gain_q.shape, BF16),
            pltpu.VMEM(gain_k.shape, BF16),
            pltpu.SMEM(far_list.shape, jnp.int32),
            pltpu.VMEM((2, stat_rows, tokens), F32),
            pltpu.VMEM((sides, 2, stat_rows, tokens), F32),
            pltpu.VMEM((tokens, width), F32),
            pltpu.VMEM((sides, tokens, width), BF16),
            pltpu.VMEM((sides, tokens, width), BF16),
            pltpu.VMEM((kinds, 2, kb, width), BF16),
            near_units,
            near_units,
            own_units,
            own_units,
            pltpu.VMEM((sides, tokens, width), F32),
            pltpu.VMEM((sides, tokens, width), jnp.int16),
            pltpu.VMEM((sides, tokens, width), jnp.int16),
            pltpu.VMEM((sides, 8, tokens), F32),
            pltpu.VMEM((sides, 8, tokens), F32),
            pltpu.VMEM((kinds, 2, kb, width), BF16),
            pltpu.VMEM((2, tokens, width), F32),
            pltpu.VMEM((3, parts, 8, 128), F32),
            dma((9,)),
            dma((sides, 2 + heads)),
            dma((sides, 2 + heads)),
            dma((kinds,)),
            dma((near_slots,)),
            dma((own_slots,)),
            dma((sides, 2)),
            dma((sides, 2)),
            dma((near_slots, 2)),
            dma((own_slots, 2)),
            dma((kinds, 2)),
            dma((3, parts)),
            dma((3, parts)),
        ],
        compiler_params=pltpu.CompilerParams(collective_id=0, has_side_effects=True),
    )(q_raw, k_raw, values, upstream, outputs, lse, gain_q, gain_k, far_list)
    return pl.pallas_call(
        copy_kernel,
        out_shape=(shape, shape, shape),
        in_specs=[vmem] * 3,
        out_specs=(anywhere,) * 3,
        scratch_shapes=[dma((3,))],
        compiler_params=pltpu.CompilerParams(vmem_limit_bytes=4 << 20),
    )(*grads)


def solution(mesh):
    sizes = (mesh.shape["ha"], mesh.shape["wa"], mesh.shape["hd"])
    tile = P("ha", "wa", None, "hd")
    return jax.shard_map(
        functools.partial(body, sizes),
        mesh=mesh,
        in_specs=(tile,) * 5 + (P("ha", "wa", "hd", None), P("hd"), P("hd"), P("ha", None, None)),
        out_specs=(tile,) * 3,
        check_vma=False,
    )
```

```python
import functools
import math

import jax
import jax.numpy as jnp
from jax import lax
from jax.experimental import pallas as pl
from jax.experimental.pallas import tpu as pltpu
from jax.sharding import PartitionSpec as P

UNITS = 4
EPS = 1e-06
MESH = pl.DeviceIdType.MESH
LAST = (((1,), (1,)), ((), ()))
FIRST = (((0,), (0,)), ((), ()))
PLAIN = (((1,), (0,)), ((), ()))
LEFT, RIGHT = 0, 1
CODE_MAX = 32767.0
F32 = jnp.float32
BF16 = jnp.bfloat16


def dot(a, b, dims):
    return lax.dot_general(a, b, dims, preferred_element_type=F32)


def kernel(
    sizes,
    q_hbm,
    k_hbm,
    v_hbm,
    u_hbm,
    o_hbm,
    lse_hbm,
    gain_q_hbm,
    gain_k_hbm,
    far_hbm,
    dq_out,
    dk_out,
    dv_out,
    q_raw,
    k_raw,
    vals,
    ups,
    outs,
    qn,
    kn,
    lse_ref,
    gain_q_ref,
    gain_k_ref,
    far_ref,
    stats,
    nbr_stats,
    dq_acc,
    nbr_q,
    nbr_u,
    far_pack,
    near_in,
    near_out,
    own_in,
    own_out,
    ret_acc,
    ret_out,
    ret_in,
    ret_scale,
    ret_scale_in,
    fret_in,
    total,
    xbuf,
    load_sem,
    nbr_send,
    nbr_recv,
    far_send,
    near_recv,
    own_recv,
    ret_send,
    ret_recv,
    near_send,
    own_send,
    fret_recv,
    x_send,
    x_recv,
):
    rows, cols, parts = sizes
    row = lax.axis_index("ha")
    col = lax.axis_index("wa")
    me = lax.axis_index("hd")
    tokens, width = q_raw.shape
    heads = lse_hbm.shape[1]
    hw = width // heads
    kb = tokens // UNITS
    full_width = width * parts
    slots = far_ref.shape[2]
    near_slots = near_in.shape[0]
    own_slots = own_in.shape[0]
    score_scale = 1.0 / math.sqrt(hw)
    head_lanes = [slice(head * hw, (head + 1) * hw) for head in range(heads)]

    barrier = pltpu.get_barrier_semaphore()
    hd_ids = [{"hd": lax.rem(me + off, parts)} for off in range(parts)]
    hd_order = sorted(range(1, parts), key=lambda off: abs(2 * off - parts))
    for target in hd_ids[1:]:
        pl.semaphore_signal(barrier, inc=1, device_id=target, device_id_type=MESH)

    exists = [col > 0, col < cols - 1]
    ids = [{"wa": col - 1}, {"wa": col + 1}]
    facing = [RIGHT, LEFT]
    if rows == 2:
        exists.append(True)
        ids.append({"ha": 1 - row})
        facing.append(2)
        pl.semaphore_signal(barrier, inc=1, device_id=ids[2], device_id_type=MESH)
    elif rows > 2:
        exists += [row > 0, row < rows - 1]
        ids += [{"ha": row - 1}, {"ha": row + 1}]
        facing += [3, 2]
        for side in (2, 3):

            @pl.when(exists[side])
            def _(side=side):
                pl.semaphore_signal(barrier, inc=1, device_id=ids[side], device_id_type=MESH)

    sides = range(len(ids))
    upright = range(2, len(ids))
    for off in range(1, cols):
        pl.semaphore_signal(
            barrier, inc=1, device_id={"wa": lax.rem(col + off, cols)}, device_id_type=MESH
        )

    loads = []
    for index, (source, target) in enumerate(
        (
            (k_hbm.at[0, 0], k_raw),
            (q_hbm.at[0, 0], q_raw),
            (far_hbm, far_ref),
            (v_hbm.at[0, 0], vals),
            (u_hbm.at[0, 0], ups),
            (o_hbm.at[0, 0], outs),
            (lse_hbm.at[0], lse_ref),
            (gain_k_hbm, gain_k_ref),
            (gain_q_hbm, gain_q_ref),
        )
    ):
        copy = pltpu.make_async_copy(source, target, load_sem.at[index])
        copy.start()
        loads.append(copy)

    inner = (col > 0) & (col < cols - 1)

    def lane_columns(columns):
        lane = lax.broadcasted_iota(jnp.int32, (tokens, 128), 1)
        mat = jnp.zeros((tokens, 128), F32)
        for place, column in columns:
            mat = jnp.where(lane == place, column, mat)
        return mat.T

    def row_sums(block):
        acc = block[:, :hw]
        for lanes in head_lanes[1:]:
            acc = acc + block[:, lanes]
        return jnp.sum(acc, axis=1, keepdims=True)

    def to_columns(rows8):
        return jnp.concatenate([rows8] * (tokens // 8), axis=0).T

    def x_copy(which, off):
        return pltpu.make_async_remote_copy(
            src_ref=xbuf.at[which, me],
            dst_ref=xbuf.at[which, me],
            send_sem=x_send.at[which, off],
            recv_sem=x_recv.at[which, off],
            device_id=hd_ids[off],
            device_id_type=MESH,
        )

    def x_start(which, rows8):
        xbuf[which, me] = rows8
        for off in hd_order:
            x_copy(which, off).start()

    def x_finish(which):
        for off in range(1, parts):
            x_copy(which, off).wait()
        acc = xbuf[which, 0]
        for part in range(1, parts):
            acc = acc + xbuf[which, part]
        return acc

    def side_id(side):
        if isinstance(side, int):
            return ids[side]
        return {"wa": jnp.where(side == RIGHT, col + 1, col - 1)}

    def face(side):
        return facing[side] if isinstance(side, int) else 1 - side

    def nbr_refs(side, message):
        if message == 0:
            return u_hbm.at[0, 0], nbr_u.at[side]
        if message == 1:
            return stats, nbr_stats.at[side]
        lanes = head_lanes[message - 2]
        return qn.at[:, lanes], nbr_q.at[side, :, lanes]

    messages = range(2 + heads)

    def nbr_copy(side, message):
        return pltpu.make_async_remote_copy(
            src_ref=nbr_refs(side, message)[0],
            dst_ref=nbr_refs(face(side), message)[1],
            send_sem=nbr_send.at[side, message],
            recv_sem=nbr_recv.at[face(side), message],
            device_id=ids[side],
            device_id_type=MESH,
        )

    def nbr_wait(side, message):
        pltpu.make_async_remote_copy(
            src_ref=nbr_refs(side, message)[0],
            dst_ref=nbr_refs(side, message)[1],
            send_sem=nbr_send.at[side, message],
            recv_sem=nbr_recv.at[side, message],
            device_id=ids[side],
            device_id_type=MESH,
        ).wait_recv()

    def nearer_left(tile):
        return 2 * tile < cols - 1

    from_left = nearer_left(col)
    behind = jnp.where(from_left, col, cols - 1 - col)
    first = jnp.where(from_left, RIGHT, LEFT)
    second = 1 - first
    has_first = jnp.where(from_left, col < cols - 1, col > 0)
    has_second = jnp.where(from_left, col > 0, col < cols - 1)

    def keeps_right(tile):
        return 2 * (tile + 1) < cols - 1

    def keeps_left(tile):
        return 2 * (tile - 1) > cols - 2

    has_own = keeps_right(col) | keeps_left(col)
    near_tiles = range(1, cols - 1)
    own_tiles = [tile for tile in range(cols) if keeps_right(tile) or keeps_left(tile)]

    def far_copy(index, tile, near, which):
        rank = col if nearer_left(tile) else cols - 1 - col
        landing, recv = (near_in, near_recv) if near else (own_in, own_recv)
        place = rank if near else rank - 2
        return pltpu.make_async_remote_copy(
            src_ref=far_pack.at[index, which],
            dst_ref=landing.at[place, which],
            send_sem=far_send.at[index, which],
            recv_sem=recv.at[place, which],
            device_id={"wa": tile},
            device_id_type=MESH,
        )

    def is_near(tile):
        return col < tile if nearer_left(tile) else col > tile

    def is_own(tile):
        return col > tile + 1 if keeps_right(tile) else col < tile - 1

    far_kinds = [(tile, True) for tile in near_tiles] + [(tile, False) for tile in own_tiles]

    def is_sent(tile, near):
        return is_near(tile) if near else is_own(tile)

    def near_here(place):
        return inner & (place < behind)

    def own_here(place):
        return has_own & (place >= behind)

    def ranked(rank):
        return jnp.where(from_left, rank, cols - 1 - rank)

    def far_wait(place, near):
        landing, recv = (near_in, near_recv) if near else (own_in, own_recv)
        for which in range(2):
            pltpu.make_async_remote_copy(
                src_ref=far_pack.at[0, which],
                dst_ref=landing.at[place, which],
                send_sem=far_send.at[0, which],
                recv_sem=recv.at[place, which],
                device_id={"wa": ranked(place if near else place + 2)},
                device_id_type=MESH,
            ).wait_recv()

    def slot_of(near):
        if near:
            return col - 1
        after = col - cols + len(own_tiles)
        return len(near_tiles) + jnp.where(from_left, col, after)

    def fret_copy(place, near, which):
        source, send = (near_out, near_send) if near else (own_out, own_send)
        return pltpu.make_async_remote_copy(
            src_ref=source.at[place, which],
            dst_ref=fret_in.at[slot_of(near), which],
            send_sem=send.at[place, which],
            recv_sem=fret_recv.at[slot_of(near), which],
            device_id={"wa": ranked(place if near else place + 2)},
            device_id_type=MESH,
        )

    def fret_wait(index, which):
        pltpu.make_async_remote_copy(
            src_ref=fret_in.at[index, which],
            dst_ref=fret_in.at[index, which],
            send_sem=near_send.at[0, which],
            recv_sem=fret_recv.at[index, which],
            device_id={"wa": far_kinds[index][0]},
            device_id_type=MESH,
        ).wait_recv()

    def ret_copy(side, which):
        source, target = ((ret_out, ret_in), (ret_scale, ret_scale_in))[which]
        return pltpu.make_async_remote_copy(
            src_ref=source.at[side],
            dst_ref=target.at[face(side)],
            send_sem=ret_send.at[side, which],
            recv_sem=ret_recv.at[face(side), which],
            device_id=side_id(side),
            device_id_type=MESH,
        )

    def ret_start(side):
        part = ret_acc[side]
        largest = jnp.abs(part[:, head_lanes[0]])
        for lanes in head_lanes[1:]:
            largest = jnp.maximum(largest, jnp.abs(part[:, lanes]))
        largest = jnp.maximum(jnp.max(largest, axis=1, keepdims=True), 1e-30)
        coded = jnp.round(part * (CODE_MAX / largest))
        ret_out[side] = coded.astype(jnp.int32).astype(jnp.int16)
        ret_copy(side, 0).start()
        ret_scale[side] = lane_columns([(0, largest / CODE_MAX)])[0:8]
        ret_copy(side, 1).start()

    def ret_wait(side):
        for which in range(2):
            source, target = ((ret_out, ret_in), (ret_scale, ret_scale_in))[which]
            pltpu.make_async_remote_copy(
                src_ref=source.at[side],
                dst_ref=target.at[side],
                send_sem=ret_send.at[side, which],
                recv_sem=ret_recv.at[side, which],
                device_id=ids[side],
                device_id_type=MESH,
            ).wait_recv()

    greeted = parts - 1 + cols - 1
    if rows == 2:
        greeted = greeted + 1
    elif rows > 2:
        greeted = greeted + jnp.minimum(row, 1) + jnp.minimum(rows - 1 - row, 1)
    pl.semaphore_wait(barrier, greeted)
    for side in sides:

        @pl.when(exists[side])
        def _(side=side):
            nbr_copy(side, 0).start()

    loads[0].wait()
    key_wide = k_raw[...].astype(F32)
    key_squares = row_sums(key_wide * key_wide)
    loads[1].wait()
    query_wide = q_raw[...].astype(F32)
    query_squares = row_sums(query_wide * query_wide)
    x_start(0, lane_columns([(0, query_squares), (1, key_squares)])[0:8])

    loads[2].wait()
    send_unit = []
    send_used = []
    for tile, near in far_kinds:
        query_col = tile if not near else tile + 1 if nearer_left(tile) else tile - 1
        unit = jnp.int32(0)
        asked = jnp.int32(0)
        for slot in range(slots):
            wanted = far_ref[0, query_col, slot] - col * UNITS
            hit = (wanted >= 0) & (wanted < UNITS)
            unit = jnp.where(hit, wanted, unit)
            asked = jnp.where(hit, 1, asked)
        send_unit.append(unit)
        send_used.append(jnp.where(is_sent(tile, near), asked, 0))

    def pick_unit(unit_wanted, source):
        wanted = jnp.full((kb, width), unit_wanted, jnp.int32)
        picked = source[0:kb, :].astype(F32)
        for unit in range(1, UNITS):
            block = source[unit * kb : (unit + 1) * kb, :].astype(F32)
            picked = jnp.where(wanted == unit, block, picked)
        return picked.astype(BF16)

    def far_start(which, source, early):
        for index, (tile, near) in enumerate(far_kinds):
            soon = jnp.logical_or(near, (col - tile) * (col - tile) == 4)

            @pl.when(is_sent(tile, near) & (soon if early else jnp.logical_not(soon)))
            def _(index=index, tile=tile, near=near):
                far_pack[index, which] = pick_unit(send_unit[index], source)
                far_copy(index, tile, near, which).start()

    loads[3].wait()
    far_start(1, vals, True)

    loads[4].wait()
    loads[5].wait()
    loads[6].wait()
    delta_columns = []
    for head, lanes in enumerate(head_lanes):
        product = ups[:, lanes].astype(F32) * outs[:, lanes].astype(F32)
        delta_columns.append((head, jnp.sum(product, axis=1, keepdims=True)))
    stats[0] = lane_columns(delta_columns)[0 : stats.shape[1]]
    for head in range(heads):
        stats[1, head : head + 1, :] = lse_ref[head]
    for side in sides:

        @pl.when(exists[side])
        def _(side=side):
            nbr_copy(side, 1).start()

    loads[7].wait()
    loads[8].wait()
    gain_q = gain_q_ref[...].astype(F32).reshape(1, width)
    gain_k = gain_k_ref[...].astype(F32).reshape(1, width)
    rates = lax.rsqrt(x_finish(0) / full_width + EPS)
    rate_columns = to_columns(rates)
    q_rate = rate_columns[:, 0:1]
    k_rate = rate_columns[:, 1:2]
    kn[...] = (k_raw[...].astype(F32) * k_rate * gain_k).astype(BF16)
    far_start(0, kn, True)
    qn[...] = (q_raw[...].astype(F32) * q_rate * gain_q).astype(BF16)
    for side in sides:

        @pl.when(exists[side])
        def _(side=side):
            for head in range(heads):
                nbr_copy(side, 2 + head).start()

    far_start(0, kn, False)
    far_start(1, vals, False)

    def place_used(place, near):
        peer = ranked(place if near else place + 2)
        query_col = col
        if near:
            query_col = jnp.clip(jnp.where(from_left, col + 1, col - 1), 0, cols - 1)
        used = jnp.int32(0)
        for slot in range(slots):
            named = far_ref[0, query_col, slot] - peer * UNITS
            used = jnp.where((named >= 0) & (named < UNITS), 1, used)
        return jnp.where(near_here(place) if near else own_here(place), used, 0)

    near_used = [place_used(place, True) for place in range(near_slots)]
    own_used = [place_used(place, False) for place in range(own_slots)]

    for side in sides:

        @pl.when(jnp.logical_not(exists[side]))
        def _(side=side):
            nbr_u[side] = jnp.zeros(nbr_u.shape[1:], BF16)
            nbr_q[side] = jnp.zeros(nbr_q.shape[1:], BF16)
            nbr_stats[side] = jnp.zeros(nbr_stats.shape[1:], F32)
            ret_in[side] = jnp.zeros(ret_in.shape[1:], jnp.int16)
            ret_scale_in[side] = jnp.zeros(ret_scale_in.shape[1:], F32)

    for place in range(near_slots):

        @pl.when(jnp.logical_not(near_here(place)))
        def _(place=place):
            near_in[place] = jnp.zeros(near_in.shape[1:], BF16)

    def attend(keys, values, queries, upstream, delta_row, lse_row, used=None):
        weight = jnp.exp(dot(keys, queries, LAST) * score_scale - lse_row)
        if used is not None:
            weight = jnp.where(used, weight, 0.0)
        dweight = dot(values, upstream, LAST)
        dscore = (weight * (dweight - delta_row)).astype(BF16)
        weight_low = weight.astype(BF16)
        dq_part = dot(dscore, keys, FIRST)
        dk_parts, dv_parts = [], []
        for start in range(0, queries.shape[0], tokens):
            block = slice(start, start + tokens)
            dk_part = dot(dscore[:, block], queries[block], PLAIN) * score_scale
            dk_parts.append(dk_part.astype(BF16))
            dv_parts.append(dot(weight_low[:, block], upstream[block], PLAIN).astype(BF16))
        return dq_part, dk_parts, dv_parts

    for head, lanes in enumerate(head_lanes):
        dq_part, (dk_part,), (dv_part,) = attend(
            kn[:, lanes],
            vals[:, lanes],
            qn[:, lanes],
            ups[:, lanes],
            stats[0, head : head + 1, :],
            stats[1, head : head + 1, :],
        )
        dq_acc[:, lanes] = dq_part
        total[0, :, lanes] = dk_part.astype(F32)
        total[1, :, lanes] = dv_part.astype(F32)

    def own_pass(place):
        far_wait(place, False)
        used = jnp.full((kb, tokens), own_used[place], jnp.int32) > 0
        for head, lanes in enumerate(head_lanes):
            dq_part, (dk_part,), (dv_part,) = attend(
                own_in[place, 0, :, lanes],
                own_in[place, 1, :, lanes],
                qn[:, lanes],
                ups[:, lanes],
                stats[0, head : head + 1, :],
                stats[1, head : head + 1, :],
                used,
            )
            dq_acc[:, lanes] += dq_part
            own_out[place, 0, :, lanes] = dk_part
            own_out[place, 1, :, lanes] = dv_part
        for which in range(2):
            fret_copy(place, False, which).start()

    def stat_row(which, head):
        return jnp.concatenate([nbr_stats[side, which, head : head + 1, :] for side in sides], axis=1)

    for place in range(own_slots)[:1]:

        @pl.when(own_here(place))
        def _(place=place):
            own_pass(place)

    for place in range(near_slots):

        @pl.when(near_here(place))
        def _(place=place):
            far_wait(place, True)

    near_mask = (
        jnp.concatenate([jnp.full((kb, tokens), flag, jnp.int32) for flag in near_used], axis=0) > 0
    )
    for head, lanes in enumerate(head_lanes):
        for side in sides:

            @pl.when(exists[side])
            def _(side=side, head=head):
                for message in (0, 1, 2) if head == 0 else (2 + head,):
                    nbr_wait(side, message)

        dq_part, dk_parts, dv_parts = attend(
            kn[:, lanes],
            vals[:, lanes],
            nbr_q[:, :, lanes].reshape(len(sides) * tokens, hw),
            nbr_u[:, :, lanes].reshape(len(sides) * tokens, hw),
            stat_row(0, head),
            stat_row(1, head),
        )
        ret_acc[:, :, lanes] = dq_part.reshape(len(sides), tokens, hw)
        for which, terms in enumerate((dk_parts, dv_parts)):
            acc = total[which, :, lanes]
            for term in terms:
                acc = acc + term.astype(F32)
            total[which, :, lanes] = acc
        dq_part, (dk_part,), (dv_part,) = attend(
            near_in[:, 0, :, lanes].reshape(near_slots * kb, hw),
            near_in[:, 1, :, lanes].reshape(near_slots * kb, hw),
            nbr_q[first, :, lanes],
            nbr_u[first, :, lanes],
            nbr_stats[first, 0, head : head + 1, :],
            nbr_stats[first, 1, head : head + 1, :],
            near_mask,
        )
        ret_acc[first, :, lanes] += dq_part
        near_out[:, 0, :, lanes] = dk_part.reshape(near_slots, kb, hw)
        near_out[:, 1, :, lanes] = dv_part.reshape(near_slots, kb, hw)

    @pl.when(has_first)
    def _():
        ret_start(first)

    for side in upright:

        @pl.when(exists[side])
        def _(side=side):
            ret_start(side)

    @pl.when(has_second)
    def _():
        ret_start(second)

    for place in range(near_slots):

        @pl.when(near_here(place))
        def _(place=place):
            for which in range(2):
                fret_copy(place, True, which).start()

    for place in range(own_slots)[1:]:

        @pl.when(own_here(place))
        def _(place=place):
            own_pass(place)

    for side in sides:

        @pl.when(exists[side])
        def _(side=side):
            ret_wait(side)

    dq_sum = dq_acc[...]
    for side in sides:
        scale = to_columns(ret_scale_in[side])[:, 0:1]
        dq_sum = dq_sum + ret_in[side].astype(jnp.int32).astype(F32) * scale
    dq_norm = (dq_sum * score_scale).astype(BF16).astype(F32)
    query_wide = q_raw[...].astype(F32)
    weighted = gain_q * dq_norm
    x_start(1, lane_columns([(0, row_sums(weighted * query_wide))])[0:8])

    def add_far(which):
        for index, (tile, near) in enumerate(far_kinds):

            @pl.when(is_sent(tile, near))
            def _(index=index):
                fret_wait(index, which)

        blocks = []
        for unit in range(UNITS):
            acc = total[which, unit * kb : (unit + 1) * kb, :]
            for index in range(len(far_kinds)):
                picked = jnp.where(send_unit[index] == unit, send_used[index], 0)
                spread = jnp.full((kb, width), picked, jnp.int32) > 0
                acc = acc + jnp.where(spread, fret_in[index, which].astype(F32), 0.0)
            blocks.append(acc)
        return jnp.concatenate(blocks, axis=0).astype(BF16)

    dk_norm = add_far(0).astype(F32)
    key_wide = k_raw[...].astype(F32)
    key_weighted = gain_k * dk_norm
    x_start(2, lane_columns([(1, row_sums(key_weighted * key_wide))])[0:8])

    q_factor = rates * rates * rates * x_finish(1) / full_width
    q_factor = to_columns(q_factor)[:, 0:1]
    dq_out[0, 0] = (q_rate * weighted - query_wide * q_factor).astype(BF16)

    dv_out[0, 0] = add_far(1)
    for side in sides:

        @pl.when(exists[side])
        def _(side=side):
            for message in messages:
                nbr_copy(side, message).wait_send()
            for which in range(2):
                ret_copy(side, which).wait_send()

    for index, (tile, near) in enumerate(far_kinds):

        @pl.when(is_sent(tile, near))
        def _(index=index, tile=tile, near=near):
            for which in range(2):
                far_copy(index, tile, near, which).wait_send()

    for place in range(near_slots):

        @pl.when(near_here(place))
        def _(place=place):
            for which in range(2):
                fret_copy(place, True, which).wait_send()

    for place in range(own_slots):

        @pl.when(own_here(place))
        def _(place=place):
            for which in range(2):
                fret_copy(place, False, which).wait_send()

    k_factor = rates * rates * rates * x_finish(2) / full_width
    k_factor = to_columns(k_factor)[:, 1:2]
    dk_out[0, 0] = (k_rate * key_weighted - key_wide * k_factor).astype(BF16)


def copy_kernel(dq_in, dk_in, dv_in, dq_out, dk_out, dv_out, sem):
    pairs = ((dq_in, dq_out), (dk_in, dk_out), (dv_in, dv_out))
    copies = [
        pltpu.make_async_copy(source, target, sem.at[index])
        for index, (source, target) in enumerate(pairs)
    ]
    for copy in copies:
        copy.start()
    for copy in copies:
        copy.wait()


def body(sizes, q_raw, k_raw, values, upstream, outputs, logsumexp, gain_q, gain_k, far_list):
    rows, cols, parts = sizes
    tokens, width = q_raw.shape[2:]
    heads = logsumexp.shape[2]
    lse = logsumexp.transpose(0, 2, 1, 3)
    kb = tokens // UNITS
    stat_rows = -(-heads // 8) * 8
    sides = 2 + (1 if rows == 2 else 2 if rows > 2 else 0)
    near_slots = max((cols - 1) // 2, 1)
    own_slots = max(cols - 2, 1)
    kinds = max(2 * cols, 1)
    shape = jax.ShapeDtypeStruct(q_raw.shape, BF16)
    vmem = pl.BlockSpec(memory_space=pltpu.VMEM)
    anywhere = pl.BlockSpec(memory_space=pltpu.HBM)
    tile = pltpu.VMEM((tokens, width), BF16)
    near_units = pltpu.VMEM((near_slots, 2, kb, width), BF16)
    own_units = pltpu.VMEM((own_slots, 2, kb, width), BF16)
    dma = pltpu.SemaphoreType.DMA
    grads = pl.pallas_call(
        functools.partial(kernel, sizes),
        out_shape=(pltpu.VMEM(q_raw.shape, BF16),) * 3,
        in_specs=[anywhere] * 9,
        out_specs=(vmem,) * 3,
        scratch_shapes=[
            tile,
            tile,
            tile,
            tile,
            tile,
            tile,
            tile,
            pltpu.VMEM(lse.shape[1:], F32),
            pltpu.VMEM(gain_q.shape, BF16),
            pltpu.VMEM(gain_k.shape, BF16),
            pltpu.SMEM(far_list.shape, jnp.int32),
            pltpu.VMEM((2, stat_rows, tokens), F32),
            pltpu.VMEM((sides, 2, stat_rows, tokens), F32),
            pltpu.VMEM((tokens, width), F32),
            pltpu.VMEM((sides, tokens, width), BF16),
            pltpu.VMEM((sides, tokens, width), BF16),
            pltpu.VMEM((kinds, 2, kb, width), BF16),
            near_units,
            near_units,
            own_units,
            own_units,
            pltpu.VMEM((sides, tokens, width), F32),
            pltpu.VMEM((sides, tokens, width), jnp.int16),
            pltpu.VMEM((sides, tokens, width), jnp.int16),
            pltpu.VMEM((sides, 8, tokens), F32),
            pltpu.VMEM((sides, 8, tokens), F32),
            pltpu.VMEM((kinds, 2, kb, width), BF16),
            pltpu.VMEM((2, tokens, width), F32),
            pltpu.VMEM((3, parts, 8, 128), F32),
            dma((9,)),
            dma((sides, 2 + heads)),
            dma((sides, 2 + heads)),
            dma((kinds, 2)),
            dma((near_slots, 2)),
            dma((own_slots, 2)),
            dma((sides, 2)),
            dma((sides, 2)),
            dma((near_slots, 2)),
            dma((own_slots, 2)),
            dma((kinds, 2)),
            dma((3, parts)),
            dma((3, parts)),
        ],
        compiler_params=pltpu.CompilerParams(collective_id=0, has_side_effects=True),
    )(q_raw, k_raw, values, upstream, outputs, lse, gain_q, gain_k, far_list)
    return pl.pallas_call(
        copy_kernel,
        out_shape=(shape, shape, shape),
        in_specs=[vmem] * 3,
        out_specs=(anywhere,) * 3,
        scratch_shapes=[dma((3,))],
        compiler_params=pltpu.CompilerParams(vmem_limit_bytes=4 << 20),
    )(*grads)


def solution(mesh):
    sizes = (mesh.shape["ha"], mesh.shape["wa"], mesh.shape["hd"])
    tile = P("ha", "wa", None, "hd")
    return jax.shard_map(
        functools.partial(body, sizes),
        mesh=mesh,
        in_specs=(tile,) * 5 + (P("ha", "wa", "hd", None), P("hd"), P("hd"), P("ha", None, None)),
        out_specs=(tile,) * 3,
        check_vma=False,
    )
```

```python
import functools
import math

import jax
import jax.numpy as jnp
from jax import lax
from jax.experimental import pallas as pl
from jax.experimental.pallas import tpu as pltpu
from jax.sharding import PartitionSpec as P

UNITS = 4
EPS = 1e-06
MESH = pl.DeviceIdType.MESH
LAST = (((1,), (1,)), ((), ()))
FIRST = (((0,), (0,)), ((), ()))
PLAIN = (((1,), (0,)), ((), ()))
LEFT, RIGHT = 0, 1
CODE_MAX = 32767.0
F32 = jnp.float32
BF16 = jnp.bfloat16


def dot(a, b, dims):
    return lax.dot_general(a, b, dims, preferred_element_type=F32)


def kernel(
    sizes,
    q_hbm,
    k_hbm,
    v_hbm,
    u_hbm,
    o_hbm,
    lse_hbm,
    gain_q_hbm,
    gain_k_hbm,
    far_hbm,
    dq_out,
    dk_out,
    dv_out,
    q_raw,
    k_raw,
    vals,
    ups,
    outs,
    qn,
    kn,
    lse_ref,
    gain_q_ref,
    gain_k_ref,
    far_ref,
    stats,
    nbr_stats,
    dq_acc,
    nbr_q,
    nbr_u,
    far_pack,
    near_in,
    near_out,
    own_in,
    own_out,
    ret_acc,
    ret_out,
    ret_in,
    ret_scale,
    ret_scale_in,
    fret_in,
    total,
    xbuf,
    load_sem,
    nbr_send,
    nbr_recv,
    far_send,
    near_recv,
    own_recv,
    ret_send,
    ret_recv,
    near_send,
    own_send,
    fret_recv,
    x_send,
    x_recv,
):
    rows, cols, parts = sizes
    row = lax.axis_index("ha")
    col = lax.axis_index("wa")
    me = lax.axis_index("hd")
    tokens, width = q_raw.shape
    heads = lse_hbm.shape[1]
    hw = width // heads
    kb = tokens // UNITS
    full_width = width * parts
    slots = far_ref.shape[2]
    near_slots = near_in.shape[0]
    own_slots = own_in.shape[0]
    score_scale = 1.0 / math.sqrt(hw)
    head_lanes = [slice(head * hw, (head + 1) * hw) for head in range(heads)]
    split = (heads + 1) // 2
    groups = [slice(0, split * hw), slice(split * hw, width)] if heads > 1 else [slice(0, width)]

    barrier = pltpu.get_barrier_semaphore()
    hd_ids = [{"hd": lax.rem(me + off, parts)} for off in range(1, parts)]
    for target in hd_ids:
        pl.semaphore_signal(barrier, inc=1, device_id=target, device_id_type=MESH)

    exists = [col > 0, col < cols - 1]
    ids = [{"wa": col - 1}, {"wa": col + 1}]
    facing = [RIGHT, LEFT]
    if rows == 2:
        exists.append(True)
        ids.append({"ha": 1 - row})
        facing.append(2)
        pl.semaphore_signal(barrier, inc=1, device_id=ids[2], device_id_type=MESH)
    elif rows > 2:
        exists += [row > 0, row < rows - 1]
        ids += [{"ha": row - 1}, {"ha": row + 1}]
        facing += [3, 2]
        for side in (2, 3):

            @pl.when(exists[side])
            def _(side=side):
                pl.semaphore_signal(barrier, inc=1, device_id=ids[side], device_id_type=MESH)

    sides = range(len(ids))
    upright = range(2, len(ids))
    for off in range(1, cols):
        pl.semaphore_signal(
            barrier, inc=1, device_id={"wa": lax.rem(col + off, cols)}, device_id_type=MESH
        )

    loads = []
    for index, (source, target) in enumerate(
        (
            (u_hbm.at[0, 0], ups),
            (k_hbm.at[0, 0], k_raw),
            (q_hbm.at[0, 0], q_raw),
            (o_hbm.at[0, 0], outs),
            (v_hbm.at[0, 0], vals),
            (lse_hbm.at[0], lse_ref),
            (gain_q_hbm, gain_q_ref),
            (gain_k_hbm, gain_k_ref),
            (far_hbm, far_ref),
        )
    ):
        copy = pltpu.make_async_copy(source, target, load_sem.at[index])
        copy.start()
        loads.append(copy)

    inner = (col > 0) & (col < cols - 1)

    def lane_columns(columns):
        lane = lax.broadcasted_iota(jnp.int32, (tokens, 128), 1)
        mat = jnp.zeros((tokens, 128), F32)
        for place, column in columns:
            mat = jnp.where(lane == place, column, mat)
        return mat.T

    def row_sums(block):
        acc = block[:, :hw]
        for lanes in head_lanes[1:]:
            acc = acc + block[:, lanes]
        return jnp.sum(acc, axis=1, keepdims=True)

    def to_columns(rows8):
        return jnp.concatenate([rows8] * (tokens // 8), axis=0).T

    def x_copy(which, off):
        return pltpu.make_async_remote_copy(
            src_ref=xbuf.at[which, me],
            dst_ref=xbuf.at[which, me],
            send_sem=x_send.at[which, off],
            recv_sem=x_recv.at[which, off],
            device_id=hd_ids[off - 1],
            device_id_type=MESH,
        )

    def x_start(which, rows8):
        xbuf[which, me] = rows8
        for off in range(1, parts):
            x_copy(which, off).start()

    def x_finish(which):
        for off in range(1, parts):
            x_copy(which, off).wait()
        acc = xbuf[which, 0]
        for part in range(1, parts):
            acc = acc + xbuf[which, part]
        return acc

    def side_id(side):
        if isinstance(side, int):
            return ids[side]
        return {"wa": jnp.where(side == RIGHT, col + 1, col - 1)}

    def face(side):
        return facing[side] if isinstance(side, int) else 1 - side

    def nbr_refs(side, message):
        if message == 0:
            return ups, nbr_u.at[side]
        if message == 1:
            return stats, nbr_stats.at[side]
        lanes = head_lanes[message - 2]
        return qn.at[:, lanes], nbr_q.at[side, :, lanes]

    messages = range(2 + heads)

    def nbr_copy(side, message):
        return pltpu.make_async_remote_copy(
            src_ref=nbr_refs(side, message)[0],
            dst_ref=nbr_refs(face(side), message)[1],
            send_sem=nbr_send.at[side, message],
            recv_sem=nbr_recv.at[face(side), message],
            device_id=ids[side],
            device_id_type=MESH,
        )

    def nbr_wait(side, message):
        pltpu.make_async_remote_copy(
            src_ref=nbr_refs(side, message)[0],
            dst_ref=nbr_refs(side, message)[1],
            send_sem=nbr_send.at[side, message],
            recv_sem=nbr_recv.at[side, message],
            device_id=ids[side],
            device_id_type=MESH,
        ).wait_recv()

    def nearer_left(tile):
        return 2 * tile < cols - 1

    from_left = nearer_left(col)
    behind = jnp.where(from_left, col, cols - 1 - col)
    first = jnp.where(from_left, RIGHT, LEFT)
    second = 1 - first
    has_first = jnp.where(from_left, col < cols - 1, col > 0)
    has_second = jnp.where(from_left, col > 0, col < cols - 1)

    def keeps_right(tile):
        return 2 * (tile + 1) < cols - 1

    def keeps_left(tile):
        return 2 * (tile - 1) > cols - 2

    has_own = keeps_right(col) | keeps_left(col)
    near_tiles = range(1, cols - 1)
    own_tiles = [tile for tile in range(cols) if keeps_right(tile) or keeps_left(tile)]

    def far_copy(index, tile, near):
        rank = col if nearer_left(tile) else cols - 1 - col
        landing, recv = (near_in, near_recv) if near else (own_in, own_recv)
        place = rank if near else rank - 2
        return pltpu.make_async_remote_copy(
            src_ref=far_pack.at[index],
            dst_ref=landing.at[place],
            send_sem=far_send.at[index],
            recv_sem=recv.at[place],
            device_id={"wa": tile},
            device_id_type=MESH,
        )

    def is_near(tile):
        return col < tile if nearer_left(tile) else col > tile

    def is_own(tile):
        return col > tile + 1 if keeps_right(tile) else col < tile - 1

    far_kinds = [(tile, True) for tile in near_tiles] + [(tile, False) for tile in own_tiles]

    def is_sent(tile, near):
        return is_near(tile) if near else is_own(tile)

    def near_here(place):
        return inner & (place < behind)

    def own_here(place):
        return has_own & (place >= behind)

    def ranked(rank):
        return jnp.where(from_left, rank, cols - 1 - rank)

    def far_wait(place, near):
        landing, recv = (near_in, near_recv) if near else (own_in, own_recv)
        pltpu.make_async_remote_copy(
            src_ref=far_pack.at[0],
            dst_ref=landing.at[place],
            send_sem=far_send.at[0],
            recv_sem=recv.at[place],
            device_id={"wa": ranked(place if near else place + 2)},
            device_id_type=MESH,
        ).wait_recv()

    def slot_of(near):
        if near:
            return col - 1
        after = col - cols + len(own_tiles)
        return len(near_tiles) + jnp.where(from_left, col, after)

    def fret_copy(place, near, which):
        source, send = (near_out, near_send) if near else (own_out, own_send)
        return pltpu.make_async_remote_copy(
            src_ref=source.at[place, which],
            dst_ref=fret_in.at[slot_of(near), which],
            send_sem=send.at[place, which],
            recv_sem=fret_recv.at[slot_of(near), which],
            device_id={"wa": ranked(place if near else place + 2)},
            device_id_type=MESH,
        )

    def fret_wait(index, which):
        pltpu.make_async_remote_copy(
            src_ref=fret_in.at[index, which],
            dst_ref=fret_in.at[index, which],
            send_sem=near_send.at[0, which],
            recv_sem=fret_recv.at[index, which],
            device_id={"wa": far_kinds[index][0]},
            device_id_type=MESH,
        ).wait_recv()

    def ret_refs(side, group, which):
        if which == 0:
            return ret_out.at[side, :, groups[group]], ret_in.at[side, :, groups[group]]
        return ret_scale.at[side, group], ret_scale_in.at[side, group]

    def ret_copy(side, group, which):
        return pltpu.make_async_remote_copy(
            src_ref=ret_refs(side, group, which)[0],
            dst_ref=ret_refs(face(side), group, which)[1],
            send_sem=ret_send.at[side, group, which],
            recv_sem=ret_recv.at[face(side), group, which],
            device_id=side_id(side),
            device_id_type=MESH,
        )

    def ret_start(side, group):
        part = ret_acc[side, :, groups[group]]
        largest = jnp.abs(part[:, :hw])
        for start in range(hw, part.shape[1], hw):
            largest = jnp.maximum(largest, jnp.abs(part[:, start : start + hw]))
        largest = jnp.maximum(jnp.max(largest, axis=1, keepdims=True), 1e-30)
        coded = jnp.round(part * (CODE_MAX / largest))
        ret_out[side, :, groups[group]] = coded.astype(jnp.int32).astype(jnp.int16)
        ret_copy(side, group, 0).start()
        place = face(side) * len(groups) + group
        ret_scale[side, group] = lane_columns([(place, largest / CODE_MAX)])[0:8]
        ret_copy(side, group, 1).start()

    def ret_wait(side):
        for group in range(len(groups)):
            for which in range(2):
                pltpu.make_async_remote_copy(
                    src_ref=ret_refs(side, group, which)[0],
                    dst_ref=ret_refs(side, group, which)[1],
                    send_sem=ret_send.at[side, group, which],
                    recv_sem=ret_recv.at[side, group, which],
                    device_id=ids[side],
                    device_id_type=MESH,
                ).wait_recv()

    def ret_start_all(group):
        @pl.when(has_first)
        def _():
            ret_start(first, group)

        for side in upright:

            @pl.when(exists[side])
            def _(side=side):
                ret_start(side, group)

        @pl.when(has_second)
        def _():
            ret_start(second, group)

    greeted = parts - 1 + cols - 1
    if rows == 2:
        greeted = greeted + 1
    elif rows > 2:
        greeted = greeted + jnp.minimum(row, 1) + jnp.minimum(rows - 1 - row, 1)
    loads[0].wait()
    pl.semaphore_wait(barrier, greeted)
    for side in sides:

        @pl.when(exists[side])
        def _(side=side):
            nbr_copy(side, 0).start()

    loads[1].wait()
    key_wide = k_raw[...].astype(F32)
    key_squares = row_sums(key_wide * key_wide)
    loads[2].wait()
    query_wide = q_raw[...].astype(F32)
    query_squares = row_sums(query_wide * query_wide)
    x_start(0, lane_columns([(0, query_squares), (1, key_squares)])[0:8])

    loads[3].wait()
    loads[5].wait()
    delta_columns = []
    for head, lanes in enumerate(head_lanes):
        product = ups[:, lanes].astype(F32) * outs[:, lanes].astype(F32)
        delta_columns.append((head, jnp.sum(product, axis=1, keepdims=True)))
    stats[0] = lane_columns(delta_columns)[0 : stats.shape[1]]
    for head in range(heads):
        stats[1, head : head + 1, :] = lse_ref[head]
    for side in sides:

        @pl.when(exists[side])
        def _(side=side):
            nbr_copy(side, 1).start()

        @pl.when(jnp.logical_not(exists[side]))
        def _(side=side):
            nbr_u[side] = jnp.zeros(nbr_u.shape[1:], BF16)
            nbr_q[side] = jnp.zeros(nbr_q.shape[1:], BF16)
            nbr_stats[side] = jnp.zeros(nbr_stats.shape[1:], F32)
            ret_in[side] = jnp.zeros(ret_in.shape[1:], jnp.int16)
            ret_scale_in[side] = jnp.zeros(ret_scale_in.shape[1:], F32)

    for place in range(near_slots):

        @pl.when(jnp.logical_not(near_here(place)))
        def _(place=place):
            near_in[place] = jnp.zeros(near_in.shape[1:], BF16)

    for place in range(own_slots):

        @pl.when(jnp.logical_not(own_here(place)))
        def _(place=place):
            own_in[place] = jnp.zeros(own_in.shape[1:], BF16)

    loads[8].wait()
    send_unit = []
    send_used = []
    for tile, near in far_kinds:
        query_col = tile if not near else tile + 1 if nearer_left(tile) else tile - 1
        unit = jnp.int32(0)
        asked = jnp.int32(0)
        for slot in range(slots):
            wanted = far_ref[0, query_col, slot] - col * UNITS
            hit = (wanted >= 0) & (wanted < UNITS)
            unit = jnp.where(hit, wanted, unit)
            asked = jnp.where(hit, 1, asked)
        send_unit.append(unit)
        send_used.append(jnp.where(is_sent(tile, near), asked, 0))

    def place_used(place, near):
        peer = ranked(place if near else place + 2)
        query_col = col
        if near:
            query_col = jnp.clip(jnp.where(from_left, col + 1, col - 1), 0, cols - 1)
        used = jnp.int32(0)
        for slot in range(slots):
            named = far_ref[0, query_col, slot] - peer * UNITS
            used = jnp.where((named >= 0) & (named < UNITS), 1, used)
        return jnp.where(near_here(place) if near else own_here(place), used, 0)

    near_used = [place_used(place, True) for place in range(near_slots)]
    own_used = [place_used(place, False) for place in range(own_slots)]

    def pick_unit(unit_wanted, source):
        wanted = jnp.full((kb, width), unit_wanted, jnp.int32)
        picked = source[0:kb, :].astype(F32)
        for unit in range(1, UNITS):
            block = source[unit * kb : (unit + 1) * kb, :].astype(F32)
            picked = jnp.where(wanted == unit, block, picked)
        return picked.astype(BF16)

    loads[4].wait()
    for index in range(len(far_kinds)):
        far_pack[index, 1] = pick_unit(send_unit[index], vals)

    loads[6].wait()
    loads[7].wait()
    gain_q = gain_q_ref[...].astype(F32).reshape(1, width)
    gain_k = gain_k_ref[...].astype(F32).reshape(1, width)
    rates = lax.rsqrt(x_finish(0) / full_width + EPS)
    rate_columns = to_columns(rates)
    q_rate = rate_columns[:, 0:1]
    k_rate = rate_columns[:, 1:2]
    kn[...] = (k_raw[...].astype(F32) * k_rate * gain_k).astype(BF16)

    def far_start(early):
        for index, (tile, near) in enumerate(far_kinds):
            soon = jnp.logical_or(near, (col - tile) * (col - tile) == 4)

            @pl.when(is_sent(tile, near) & (soon if early else jnp.logical_not(soon)))
            def _(index=index, tile=tile, near=near):
                far_pack[index, 0] = pick_unit(send_unit[index], kn)
                far_copy(index, tile, near).start()

    far_start(True)
    qn[...] = (q_raw[...].astype(F32) * q_rate * gain_q).astype(BF16)
    for side in sides:

        @pl.when(exists[side])
        def _(side=side):
            for head in range(heads):
                nbr_copy(side, 2 + head).start()

    far_start(False)

    def attend(keys, values, queries, upstream, delta_row, lse_row, used=None):
        weight = jnp.exp(dot(keys, queries, LAST) * score_scale - lse_row)
        if used is not None:
            weight = jnp.where(used, weight, 0.0)
        dweight = dot(values, upstream, LAST)
        dscore = (weight * (dweight - delta_row)).astype(BF16)
        weight_low = weight.astype(BF16)
        dq_part = dot(dscore, keys, FIRST)
        dk_parts, dv_parts = [], []
        for start in range(0, queries.shape[0], tokens):
            block = slice(start, start + tokens)
            dk_part = dot(dscore[:, block], queries[block], PLAIN) * score_scale
            dk_parts.append(dk_part.astype(BF16))
            dv_parts.append(dot(weight_low[:, block], upstream[block], PLAIN).astype(BF16))
        return dq_part, dk_parts, dv_parts

    for head, lanes in enumerate(head_lanes):
        dq_part, (dk_part,), (dv_part,) = attend(
            kn[:, lanes],
            vals[:, lanes],
            qn[:, lanes],
            ups[:, lanes],
            stats[0, head : head + 1, :],
            stats[1, head : head + 1, :],
        )
        dq_acc[:, lanes] = dq_part
        total[0, :, lanes] = dk_part.astype(F32)
        total[1, :, lanes] = dv_part.astype(F32)

    def own_pass(place):
        far_wait(place, False)
        used = jnp.full((kb, tokens), own_used[place], jnp.int32) > 0
        for head, lanes in enumerate(head_lanes):
            dq_part, (dk_part,), (dv_part,) = attend(
                own_in[place, 0, :, lanes],
                own_in[place, 1, :, lanes],
                qn[:, lanes],
                ups[:, lanes],
                stats[0, head : head + 1, :],
                stats[1, head : head + 1, :],
                used,
            )
            dq_acc[:, lanes] += dq_part
            own_out[place, 0, :, lanes] = dk_part
            own_out[place, 1, :, lanes] = dv_part
        fret_copy(place, False, 0).start()

    def stat_row(which, head):
        return jnp.concatenate([nbr_stats[side, which, head : head + 1, :] for side in sides], axis=1)

    for place in range(own_slots)[:1]:

        @pl.when(own_here(place))
        def _(place=place):
            own_pass(place)

    for place in range(near_slots):

        @pl.when(near_here(place))
        def _(place=place):
            far_wait(place, True)

    near_mask = (
        jnp.concatenate([jnp.full((kb, tokens), flag, jnp.int32) for flag in near_used], axis=0) > 0
    )
    for head, lanes in enumerate(head_lanes):
        for side in sides:

            @pl.when(exists[side])
            def _(side=side, head=head):
                for message in (0, 1, 2) if head == 0 else (2 + head,):
                    nbr_wait(side, message)

        dq_part, dk_parts, dv_parts = attend(
            kn[:, lanes],
            vals[:, lanes],
            nbr_q[:, :, lanes].reshape(len(sides) * tokens, hw),
            nbr_u[:, :, lanes].reshape(len(sides) * tokens, hw),
            stat_row(0, head),
            stat_row(1, head),
        )
        ret_acc[:, :, lanes] = dq_part.reshape(len(sides), tokens, hw)
        for which, terms in enumerate((dk_parts, dv_parts)):
            acc = total[which, :, lanes]
            for term in terms:
                acc = acc + term.astype(F32)
            total[which, :, lanes] = acc
        dq_part, (dk_part,), (dv_part,) = attend(
            near_in[:, 0, :, lanes].reshape(near_slots * kb, hw),
            near_in[:, 1, :, lanes].reshape(near_slots * kb, hw),
            nbr_q[first, :, lanes],
            nbr_u[first, :, lanes],
            nbr_stats[first, 0, head : head + 1, :],
            nbr_stats[first, 1, head : head + 1, :],
            near_mask,
        )
        ret_acc[first, :, lanes] += dq_part
        near_out[:, 0, :, lanes] = dk_part.reshape(near_slots, kb, hw)
        near_out[:, 1, :, lanes] = dv_part.reshape(near_slots, kb, hw)

        if head + 1 in (split, heads):
            ret_start_all(head // split)

    for place in range(near_slots):

        @pl.when(near_here(place))
        def _(place=place):
            fret_copy(place, True, 0).start()

    for place in range(own_slots)[1:]:

        @pl.when(own_here(place))
        def _(place=place):
            own_pass(place)

    for place in range(near_slots):

        @pl.when(near_here(place))
        def _(place=place):
            fret_copy(place, True, 1).start()

    for place in range(own_slots):

        @pl.when(own_here(place))
        def _(place=place):
            fret_copy(place, False, 1).start()

    for side in sides:

        @pl.when(exists[side])
        def _(side=side):
            ret_wait(side)

    scale_rows = jnp.zeros((8, tokens), F32)
    for side in sides:
        for group in range(len(groups)):
            scale_rows = scale_rows + ret_scale_in[side, group]
    scales = to_columns(scale_rows)
    dq_groups = []
    for group, lanes in enumerate(groups):
        dq_sum = dq_acc[:, lanes]
        for side in sides:
            place = side * len(groups) + group
            coded = ret_in[side, :, lanes].astype(jnp.int32).astype(F32)
            dq_sum = dq_sum + coded * scales[:, place : place + 1]
        dq_groups.append(dq_sum)
    dq_sum = jnp.concatenate(dq_groups, axis=1)
    dq_norm = (dq_sum * score_scale).astype(BF16).astype(F32)
    query_wide = q_raw[...].astype(F32)
    weighted = gain_q * dq_norm
    x_start(1, lane_columns([(0, row_sums(weighted * query_wide))])[0:8])

    def add_far(which):
        for index, (tile, near) in enumerate(far_kinds):

            @pl.when(is_sent(tile, near))
            def _(index=index):
                fret_wait(index, which)

        blocks = []
        for unit in range(UNITS):
            acc = total[which, unit * kb : (unit + 1) * kb, :]
            for index in range(len(far_kinds)):
                picked = jnp.where(send_unit[index] == unit, send_used[index], 0)
                spread = jnp.full((kb, width), picked, jnp.int32) > 0
                acc = acc + jnp.where(spread, fret_in[index, which].astype(F32), 0.0)
            blocks.append(acc)
        return jnp.concatenate(blocks, axis=0).astype(BF16)

    dk_norm = add_far(0).astype(F32)
    key_wide = k_raw[...].astype(F32)
    key_weighted = gain_k * dk_norm
    x_start(2, lane_columns([(1, row_sums(key_weighted * key_wide))])[0:8])

    q_factor = rates * rates * rates * x_finish(1) / full_width
    q_factor = to_columns(q_factor)[:, 0:1]
    dq_out[0, 0] = (q_rate * weighted - query_wide * q_factor).astype(BF16)

    dv_out[0, 0] = add_far(1)
    for side in sides:

        @pl.when(exists[side])
        def _(side=side):
            for message in messages:
                nbr_copy(side, message).wait_send()
            for group in range(len(groups)):
                for which in range(2):
                    ret_copy(side, group, which).wait_send()

    for index, (tile, near) in enumerate(far_kinds):

        @pl.when(is_sent(tile, near))
        def _(index=index, tile=tile, near=near):
            far_copy(index, tile, near).wait_send()

    for place in range(near_slots):

        @pl.when(near_here(place))
        def _(place=place):
            for which in range(2):
                fret_copy(place, True, which).wait_send()

    for place in range(own_slots):

        @pl.when(own_here(place))
        def _(place=place):
            for which in range(2):
                fret_copy(place, False, which).wait_send()

    k_factor = rates * rates * rates * x_finish(2) / full_width
    k_factor = to_columns(k_factor)[:, 1:2]
    dk_out[0, 0] = (k_rate * key_weighted - key_wide * k_factor).astype(BF16)


def copy_kernel(dq_in, dk_in, dv_in, dq_out, dk_out, dv_out, sem):
    pairs = ((dq_in, dq_out), (dk_in, dk_out), (dv_in, dv_out))
    copies = [
        pltpu.make_async_copy(source, target, sem.at[index])
        for index, (source, target) in enumerate(pairs)
    ]
    for copy in copies:
        copy.start()
    for copy in copies:
        copy.wait()


def body(sizes, q_raw, k_raw, values, upstream, outputs, logsumexp, gain_q, gain_k, far_list):
    rows, cols, parts = sizes
    tokens, width = q_raw.shape[2:]
    heads = logsumexp.shape[2]
    lse = logsumexp.transpose(0, 2, 1, 3)
    kb = tokens // UNITS
    stat_rows = -(-heads // 8) * 8
    sides = 2 + (1 if rows == 2 else 2 if rows > 2 else 0)
    near_slots = max((cols - 1) // 2, 1)
    own_slots = max(cols - 2, 1)
    kinds = max(2 * cols, 1)
    shape = jax.ShapeDtypeStruct(q_raw.shape, BF16)
    vmem = pl.BlockSpec(memory_space=pltpu.VMEM)
    anywhere = pl.BlockSpec(memory_space=pltpu.HBM)
    tile = pltpu.VMEM((tokens, width), BF16)
    near_units = pltpu.VMEM((near_slots, 2, kb, width), BF16)
    own_units = pltpu.VMEM((own_slots, 2, kb, width), BF16)
    dma = pltpu.SemaphoreType.DMA
    grads = pl.pallas_call(
        functools.partial(kernel, sizes),
        out_shape=(pltpu.VMEM(q_raw.shape, BF16),) * 3,
        in_specs=[anywhere] * 9,
        out_specs=(vmem,) * 3,
        scratch_shapes=[
            tile,
            tile,
            tile,
            tile,
            tile,
            tile,
            tile,
            pltpu.VMEM(lse.shape[1:], F32),
            pltpu.VMEM(gain_q.shape, BF16),
            pltpu.VMEM(gain_k.shape, BF16),
            pltpu.SMEM(far_list.shape, jnp.int32),
            pltpu.VMEM((2, stat_rows, tokens), F32),
            pltpu.VMEM((sides, 2, stat_rows, tokens), F32),
            pltpu.VMEM((tokens, width), F32),
            pltpu.VMEM((sides, tokens, width), BF16),
            pltpu.VMEM((sides, tokens, width), BF16),
            pltpu.VMEM((kinds, 2, kb, width), BF16),
            near_units,
            near_units,
            own_units,
            own_units,
            pltpu.VMEM((sides, tokens, width), F32),
            pltpu.VMEM((sides, tokens, width), jnp.int16),
            pltpu.VMEM((sides, tokens, width), jnp.int16),
            pltpu.VMEM((sides, 2, 8, tokens), F32),
            pltpu.VMEM((sides, 2, 8, tokens), F32),
            pltpu.VMEM((kinds, 2, kb, width), BF16),
            pltpu.VMEM((2, tokens, width), F32),
            pltpu.VMEM((3, parts, 8, 128), F32),
            dma((9,)),
            dma((sides, 2 + heads)),
            dma((sides, 2 + heads)),
            dma((kinds,)),
            dma((near_slots,)),
            dma((own_slots,)),
            dma((sides, 2, 2)),
            dma((sides, 2, 2)),
            dma((near_slots, 2)),
            dma((own_slots, 2)),
            dma((kinds, 2)),
            dma((3, parts)),
            dma((3, parts)),
        ],
        compiler_params=pltpu.CompilerParams(collective_id=0, has_side_effects=True),
    )(q_raw, k_raw, values, upstream, outputs, lse, gain_q, gain_k, far_list)
    return pl.pallas_call(
        copy_kernel,
        out_shape=(shape, shape, shape),
        in_specs=[vmem] * 3,
        out_specs=(anywhere,) * 3,
        scratch_shapes=[dma((3,))],
        compiler_params=pltpu.CompilerParams(vmem_limit_bytes=4 << 20),
    )(*grads)


def solution(mesh):
    sizes = (mesh.shape["ha"], mesh.shape["wa"], mesh.shape["hd"])
    tile = P("ha", "wa", None, "hd")
    return jax.shard_map(
        functools.partial(body, sizes),
        mesh=mesh,
        in_specs=(tile,) * 5 + (P("ha", "wa", "hd", None), P("hd"), P("hd"), P("ha", None, None)),
        out_specs=(tile,) * 3,
        check_vma=False,
    )
```

```python
import functools
import math

import jax
import jax.numpy as jnp
from jax import lax
from jax.experimental import pallas as pl
from jax.experimental.pallas import tpu as pltpu
from jax.sharding import PartitionSpec as P

UNITS = 4
EPS = 1e-06
MESH = pl.DeviceIdType.MESH
LAST = (((1,), (1,)), ((), ()))
FIRST = (((0,), (0,)), ((), ()))
PLAIN = (((1,), (0,)), ((), ()))
LEFT, RIGHT = 0, 1
CODE_MAX = 32767.0
F32 = jnp.float32
BF16 = jnp.bfloat16


def dot(a, b, dims):
    return lax.dot_general(a, b, dims, preferred_element_type=F32)


def kernel(
    sizes,
    q_hbm,
    k_hbm,
    v_hbm,
    u_hbm,
    o_hbm,
    lse_hbm,
    gain_q_hbm,
    gain_k_hbm,
    far_hbm,
    dq_out,
    dk_out,
    dv_out,
    q_raw,
    k_raw,
    vals,
    ups,
    outs,
    qn,
    kn,
    lse_ref,
    gain_q_ref,
    gain_k_ref,
    far_ref,
    stats,
    nbr_stats,
    dq_acc,
    nbr_q,
    nbr_u,
    far_pack,
    near_in,
    near_out,
    own_in,
    own_out,
    ret_acc,
    ret_out,
    ret_in,
    ret_scale,
    ret_scale_in,
    fret_in,
    total,
    xbuf,
    load_sem,
    nbr_send,
    nbr_recv,
    far_send,
    near_recv,
    own_recv,
    ret_send,
    ret_recv,
    near_send,
    own_send,
    fret_recv,
    x_send,
    x_recv,
):
    rows, cols, parts = sizes
    row = lax.axis_index("ha")
    col = lax.axis_index("wa")
    me = lax.axis_index("hd")
    tokens, width = q_raw.shape
    heads = lse_hbm.shape[1]
    hw = width // heads
    kb = tokens // UNITS
    full_width = width * parts
    slots = far_ref.shape[2]
    near_slots = near_in.shape[0]
    own_slots = own_in.shape[0]
    score_scale = 1.0 / math.sqrt(hw)
    head_lanes = [slice(head * hw, (head + 1) * hw) for head in range(heads)]
    split = (heads + 1) // 2
    groups = [slice(0, split * hw), slice(split * hw, width)] if heads > 1 else [slice(0, width)]

    barrier = pltpu.get_barrier_semaphore()
    hd_ids = [{"hd": lax.rem(me + off, parts)} for off in range(1, parts)]
    for target in hd_ids:
        pl.semaphore_signal(barrier, inc=1, device_id=target, device_id_type=MESH)

    exists = [col > 0, col < cols - 1]
    ids = [{"wa": col - 1}, {"wa": col + 1}]
    facing = [RIGHT, LEFT]
    if rows == 2:
        exists.append(True)
        ids.append({"ha": 1 - row})
        facing.append(2)
        pl.semaphore_signal(barrier, inc=1, device_id=ids[2], device_id_type=MESH)
    elif rows > 2:
        exists += [row > 0, row < rows - 1]
        ids += [{"ha": row - 1}, {"ha": row + 1}]
        facing += [3, 2]
        for side in (2, 3):

            @pl.when(exists[side])
            def _(side=side):
                pl.semaphore_signal(barrier, inc=1, device_id=ids[side], device_id_type=MESH)

    sides = range(len(ids))
    upright = range(2, len(ids))
    for off in range(1, cols):
        pl.semaphore_signal(
            barrier, inc=1, device_id={"wa": lax.rem(col + off, cols)}, device_id_type=MESH
        )

    loads = []
    for index, (source, target) in enumerate(
        (
            (u_hbm.at[0, 0], ups),
            (k_hbm.at[0, 0], k_raw),
            (q_hbm.at[0, 0], q_raw),
            (o_hbm.at[0, 0], outs),
            (v_hbm.at[0, 0], vals),
            (lse_hbm.at[0], lse_ref),
            (gain_q_hbm, gain_q_ref),
            (gain_k_hbm, gain_k_ref),
            (far_hbm, far_ref),
        )
    ):
        copy = pltpu.make_async_copy(source, target, load_sem.at[index])
        copy.start()
        loads.append(copy)

    inner = (col > 0) & (col < cols - 1)

    def lane_columns(columns):
        lane = lax.broadcasted_iota(jnp.int32, (tokens, 128), 1)
        mat = jnp.zeros((tokens, 128), F32)
        for place, column in columns:
            mat = jnp.where(lane == place, column, mat)
        return mat.T

    def row_sums(block):
        acc = block[:, :hw]
        for lanes in head_lanes[1:]:
            acc = acc + block[:, lanes]
        return jnp.sum(acc, axis=1, keepdims=True)

    def to_columns(rows8):
        return jnp.concatenate([rows8] * (tokens // 8), axis=0).T

    def x_copy(which, off):
        return pltpu.make_async_remote_copy(
            src_ref=xbuf.at[which, me],
            dst_ref=xbuf.at[which, me],
            send_sem=x_send.at[which, off],
            recv_sem=x_recv.at[which, off],
            device_id=hd_ids[off - 1],
            device_id_type=MESH,
        )

    def x_start(which, rows8):
        xbuf[which, me] = rows8
        for off in range(1, parts):
            x_copy(which, off).start()

    def x_finish(which):
        for off in range(1, parts):
            x_copy(which, off).wait()
        acc = xbuf[which, 0]
        for part in range(1, parts):
            acc = acc + xbuf[which, part]
        return acc

    def side_id(side):
        if isinstance(side, int):
            return ids[side]
        return {"wa": jnp.where(side == RIGHT, col + 1, col - 1)}

    def face(side):
        return facing[side] if isinstance(side, int) else 1 - side

    def nbr_refs(side, message):
        if message == 0:
            return ups, nbr_u.at[side]
        if message == 1:
            return stats, nbr_stats.at[side]
        lanes = head_lanes[message - 2]
        return qn.at[:, lanes], nbr_q.at[side, :, lanes]

    messages = range(2 + heads)

    def nbr_copy(side, message):
        return pltpu.make_async_remote_copy(
            src_ref=nbr_refs(side, message)[0],
            dst_ref=nbr_refs(face(side), message)[1],
            send_sem=nbr_send.at[side, message],
            recv_sem=nbr_recv.at[face(side), message],
            device_id=ids[side],
            device_id_type=MESH,
        )

    def nbr_wait(side, message):
        pltpu.make_async_remote_copy(
            src_ref=nbr_refs(side, message)[0],
            dst_ref=nbr_refs(side, message)[1],
            send_sem=nbr_send.at[side, message],
            recv_sem=nbr_recv.at[side, message],
            device_id=ids[side],
            device_id_type=MESH,
        ).wait_recv()

    def nearer_left(tile):
        return 2 * tile < cols - 1

    from_left = nearer_left(col)
    behind = jnp.where(from_left, col, cols - 1 - col)
    first = jnp.where(from_left, RIGHT, LEFT)
    second = 1 - first
    has_first = jnp.where(from_left, col < cols - 1, col > 0)
    has_second = jnp.where(from_left, col > 0, col < cols - 1)

    def keeps_right(tile):
        return 2 * (tile + 1) < cols - 1

    def keeps_left(tile):
        return 2 * (tile - 1) > cols - 2

    has_own = keeps_right(col) | keeps_left(col)
    near_tiles = range(1, cols - 1)
    own_tiles = [tile for tile in range(cols) if keeps_right(tile) or keeps_left(tile)]

    def far_copy(index, tile, near):
        rank = col if nearer_left(tile) else cols - 1 - col
        landing, recv = (near_in, near_recv) if near else (own_in, own_recv)
        place = rank if near else rank - 2
        return pltpu.make_async_remote_copy(
            src_ref=far_pack.at[index],
            dst_ref=landing.at[place],
            send_sem=far_send.at[index],
            recv_sem=recv.at[place],
            device_id={"wa": tile},
            device_id_type=MESH,
        )

    def is_near(tile):
        return col < tile if nearer_left(tile) else col > tile

    def is_own(tile):
        return col > tile + 1 if keeps_right(tile) else col < tile - 1

    far_kinds = [(tile, True) for tile in near_tiles] + [(tile, False) for tile in own_tiles]

    def is_sent(tile, near):
        return is_near(tile) if near else is_own(tile)

    def near_here(place):
        return inner & (place < behind)

    def own_here(place):
        return has_own & (place >= behind)

    def ranked(rank):
        return jnp.where(from_left, rank, cols - 1 - rank)

    def far_wait(place, near):
        landing, recv = (near_in, near_recv) if near else (own_in, own_recv)
        pltpu.make_async_remote_copy(
            src_ref=far_pack.at[0],
            dst_ref=landing.at[place],
            send_sem=far_send.at[0],
            recv_sem=recv.at[place],
            device_id={"wa": ranked(place if near else place + 2)},
            device_id_type=MESH,
        ).wait_recv()

    def slot_of(near):
        if near:
            return col - 1
        after = col - cols + len(own_tiles)
        return len(near_tiles) + jnp.where(from_left, col, after)

    def fret_copy(place, near, which):
        source, send = (near_out, near_send) if near else (own_out, own_send)
        return pltpu.make_async_remote_copy(
            src_ref=source.at[place, which],
            dst_ref=fret_in.at[slot_of(near), which],
            send_sem=send.at[place, which],
            recv_sem=fret_recv.at[slot_of(near), which],
            device_id={"wa": ranked(place if near else place + 2)},
            device_id_type=MESH,
        )

    def fret_wait(index, which):
        pltpu.make_async_remote_copy(
            src_ref=fret_in.at[index, which],
            dst_ref=fret_in.at[index, which],
            send_sem=near_send.at[0, which],
            recv_sem=fret_recv.at[index, which],
            device_id={"wa": far_kinds[index][0]},
            device_id_type=MESH,
        ).wait_recv()

    def ret_refs(side, group, which):
        if which == 0:
            return ret_out.at[side, :, groups[group]], ret_in.at[side, :, groups[group]]
        return ret_scale.at[side, group], ret_scale_in.at[side, group]

    def ret_copy(side, group, which):
        return pltpu.make_async_remote_copy(
            src_ref=ret_refs(side, group, which)[0],
            dst_ref=ret_refs(face(side), group, which)[1],
            send_sem=ret_send.at[side, group, which],
            recv_sem=ret_recv.at[face(side), group, which],
            device_id=side_id(side),
            device_id_type=MESH,
        )

    def ret_start(side, group):
        part = ret_acc[side, :, groups[group]]
        largest = jnp.abs(part[:, :hw])
        for start in range(hw, part.shape[1], hw):
            largest = jnp.maximum(largest, jnp.abs(part[:, start : start + hw]))
        largest = jnp.maximum(jnp.max(largest, axis=1, keepdims=True), 1e-30)
        coded = jnp.round(part * (CODE_MAX / largest))
        ret_out[side, :, groups[group]] = coded.astype(jnp.int32).astype(jnp.int16)
        ret_copy(side, group, 0).start()
        place = face(side) * len(groups) + group
        ret_scale[side, group] = lane_columns([(place, largest / CODE_MAX)])[0:8]
        ret_copy(side, group, 1).start()

    def ret_wait(side):
        for group in range(len(groups)):
            for which in range(2):
                pltpu.make_async_remote_copy(
                    src_ref=ret_refs(side, group, which)[0],
                    dst_ref=ret_refs(side, group, which)[1],
                    send_sem=ret_send.at[side, group, which],
                    recv_sem=ret_recv.at[side, group, which],
                    device_id=ids[side],
                    device_id_type=MESH,
                ).wait_recv()

    def ret_start_all(group):
        @pl.when(has_first)
        def _():
            ret_start(first, group)

        for side in upright:

            @pl.when(exists[side])
            def _(side=side):
                ret_start(side, group)

        @pl.when(has_second)
        def _():
            ret_start(second, group)

    greeted = parts - 1 + cols - 1
    if rows == 2:
        greeted = greeted + 1
    elif rows > 2:
        greeted = greeted + jnp.minimum(row, 1) + jnp.minimum(rows - 1 - row, 1)
    loads[0].wait()
    pl.semaphore_wait(barrier, greeted)
    for side in sides:

        @pl.when(exists[side])
        def _(side=side):
            nbr_copy(side, 0).start()

    loads[1].wait()
    key_wide = k_raw[...].astype(F32)
    key_squares = row_sums(key_wide * key_wide)
    loads[2].wait()
    query_wide = q_raw[...].astype(F32)
    query_squares = row_sums(query_wide * query_wide)
    x_start(0, lane_columns([(0, query_squares), (1, key_squares)])[0:8])

    loads[3].wait()
    loads[5].wait()
    delta_columns = []
    for head, lanes in enumerate(head_lanes):
        product = ups[:, lanes].astype(F32) * outs[:, lanes].astype(F32)
        delta_columns.append((head, jnp.sum(product, axis=1, keepdims=True)))
    stats[0] = lane_columns(delta_columns)[0 : stats.shape[1]]
    for head in range(heads):
        stats[1, head : head + 1, :] = lse_ref[head]
    for side in sides:

        @pl.when(exists[side])
        def _(side=side):
            nbr_copy(side, 1).start()

        @pl.when(jnp.logical_not(exists[side]))
        def _(side=side):
            nbr_u[side] = jnp.zeros(nbr_u.shape[1:], BF16)
            nbr_q[side] = jnp.zeros(nbr_q.shape[1:], BF16)
            nbr_stats[side] = jnp.zeros(nbr_stats.shape[1:], F32)
            ret_in[side] = jnp.zeros(ret_in.shape[1:], jnp.int16)
            ret_scale_in[side] = jnp.zeros(ret_scale_in.shape[1:], F32)

    for place in range(near_slots):

        @pl.when(jnp.logical_not(near_here(place)))
        def _(place=place):
            near_in[place] = jnp.zeros(near_in.shape[1:], BF16)

    for place in range(own_slots):

        @pl.when(jnp.logical_not(own_here(place)))
        def _(place=place):
            own_in[place] = jnp.zeros(own_in.shape[1:], BF16)

    loads[8].wait()
    send_unit = []
    send_used = []
    for tile, near in far_kinds:
        query_col = tile if not near else tile + 1 if nearer_left(tile) else tile - 1
        unit = jnp.int32(0)
        asked = jnp.int32(0)
        for slot in range(slots):
            wanted = far_ref[0, query_col, slot] - col * UNITS
            hit = (wanted >= 0) & (wanted < UNITS)
            unit = jnp.where(hit, wanted, unit)
            asked = jnp.where(hit, 1, asked)
        send_unit.append(unit)
        send_used.append(jnp.where(is_sent(tile, near), asked, 0))

    def place_used(place, near):
        peer = ranked(place if near else place + 2)
        query_col = col
        if near:
            query_col = jnp.clip(jnp.where(from_left, col + 1, col - 1), 0, cols - 1)
        used = jnp.int32(0)
        for slot in range(slots):
            named = far_ref[0, query_col, slot] - peer * UNITS
            used = jnp.where((named >= 0) & (named < UNITS), 1, used)
        return jnp.where(near_here(place) if near else own_here(place), used, 0)

    near_used = [place_used(place, True) for place in range(near_slots)]
    own_used = [place_used(place, False) for place in range(own_slots)]

    def pick_unit(unit_wanted, source):
        wanted = jnp.full((kb, width), unit_wanted, jnp.int32)
        picked = source[0:kb, :].astype(F32)
        for unit in range(1, UNITS):
            block = source[unit * kb : (unit + 1) * kb, :].astype(F32)
            picked = jnp.where(wanted == unit, block, picked)
        return picked.astype(BF16)

    loads[4].wait()
    for index in range(len(far_kinds)):
        far_pack[index, 1] = pick_unit(send_unit[index], vals)

    loads[6].wait()
    loads[7].wait()
    gain_q = gain_q_ref[...].astype(F32).reshape(1, width)
    gain_k = gain_k_ref[...].astype(F32).reshape(1, width)
    rates = lax.rsqrt(x_finish(0) / full_width + EPS)
    rate_columns = to_columns(rates)
    q_rate = rate_columns[:, 0:1]
    k_rate = rate_columns[:, 1:2]
    kn[...] = (k_raw[...].astype(F32) * k_rate * gain_k).astype(BF16)

    def is_timed(tile, near, early):
        if near:
            return is_sent(tile, near) if early else False
        gap = (col - tile) * (col - tile)
        return is_sent(tile, near) & (gap == 4 if early else gap > 4)

    def far_start(early):
        for index, (tile, near) in enumerate(far_kinds):
            @pl.when(is_timed(tile, near, early))
            def _(index=index, tile=tile, near=near):
                far_pack[index, 0] = pick_unit(send_unit[index], kn)
                far_copy(index, tile, near).start()

    far_start(True)
    qn[...] = (q_raw[...].astype(F32) * q_rate * gain_q).astype(BF16)
    for side in sides:

        @pl.when(exists[side])
        def _(side=side):
            for head in range(split):
                nbr_copy(side, 2 + head).start()

    far_start(False)
    for side in sides:

        @pl.when(exists[side])
        def _(side=side):
            for head in range(split, heads):
                nbr_copy(side, 2 + head).start()

    def attend(keys, values, queries, upstream, delta_row, lse_row, used=None):
        weight = jnp.exp(dot(keys, queries, LAST) * score_scale - lse_row)
        if used is not None:
            weight = jnp.where(used, weight, 0.0)
        dweight = dot(values, upstream, LAST)
        dscore = (weight * (dweight - delta_row)).astype(BF16)
        weight_low = weight.astype(BF16)
        dq_part = dot(dscore, keys, FIRST)
        dk_parts, dv_parts = [], []
        for start in range(0, queries.shape[0], tokens):
            block = slice(start, start + tokens)
            dk_part = dot(dscore[:, block], queries[block], PLAIN) * score_scale
            dk_parts.append(dk_part.astype(BF16))
            dv_parts.append(dot(weight_low[:, block], upstream[block], PLAIN).astype(BF16))
        return dq_part, dk_parts, dv_parts

    for head, lanes in enumerate(head_lanes):
        dq_part, (dk_part,), (dv_part,) = attend(
            kn[:, lanes],
            vals[:, lanes],
            qn[:, lanes],
            ups[:, lanes],
            stats[0, head : head + 1, :],
            stats[1, head : head + 1, :],
        )
        dq_acc[:, lanes] = dq_part
        total[0, :, lanes] = dk_part.astype(F32)
        total[1, :, lanes] = dv_part.astype(F32)

    def own_pass(place):
        far_wait(place, False)
        used = jnp.full((kb, tokens), own_used[place], jnp.int32) > 0
        for head, lanes in enumerate(head_lanes):
            dq_part, (dk_part,), (dv_part,) = attend(
                own_in[place, 0, :, lanes],
                own_in[place, 1, :, lanes],
                qn[:, lanes],
                ups[:, lanes],
                stats[0, head : head + 1, :],
                stats[1, head : head + 1, :],
                used,
            )
            dq_acc[:, lanes] += dq_part
            own_out[place, 0, :, lanes] = dk_part
            own_out[place, 1, :, lanes] = dv_part
        fret_copy(place, False, 0).start()

    def stat_row(which, head):
        return jnp.concatenate([nbr_stats[side, which, head : head + 1, :] for side in sides], axis=1)

    for place in range(own_slots)[:1]:

        @pl.when(own_here(place))
        def _(place=place):
            own_pass(place)

    for place in range(near_slots):

        @pl.when(near_here(place))
        def _(place=place):
            far_wait(place, True)

    near_mask = (
        jnp.concatenate([jnp.full((kb, tokens), flag, jnp.int32) for flag in near_used], axis=0) > 0
    )
    for head, lanes in enumerate(head_lanes):
        for side in sides:

            @pl.when(exists[side])
            def _(side=side, head=head):
                for message in (0, 1, 2) if head == 0 else (2 + head,):
                    nbr_wait(side, message)

        dq_part, dk_parts, dv_parts = attend(
            kn[:, lanes],
            vals[:, lanes],
            nbr_q[:, :, lanes].reshape(len(sides) * tokens, hw),
            nbr_u[:, :, lanes].reshape(len(sides) * tokens, hw),
            stat_row(0, head),
            stat_row(1, head),
        )
        ret_acc[:, :, lanes] = dq_part.reshape(len(sides), tokens, hw)
        for which, terms in enumerate((dk_parts, dv_parts)):
            acc = total[which, :, lanes]
            for term in terms:
                acc = acc + term.astype(F32)
            total[which, :, lanes] = acc
        dq_part, (dk_part,), (dv_part,) = attend(
            near_in[:, 0, :, lanes].reshape(near_slots * kb, hw),
            near_in[:, 1, :, lanes].reshape(near_slots * kb, hw),
            nbr_q[first, :, lanes],
            nbr_u[first, :, lanes],
            nbr_stats[first, 0, head : head + 1, :],
            nbr_stats[first, 1, head : head + 1, :],
            near_mask,
        )
        ret_acc[first, :, lanes] += dq_part
        near_out[:, 0, :, lanes] = dk_part.reshape(near_slots, kb, hw)
        near_out[:, 1, :, lanes] = dv_part.reshape(near_slots, kb, hw)

        if head + 1 in (split, heads):
            ret_start_all(head // split)

    for place in range(near_slots):

        @pl.when(near_here(place))
        def _(place=place):
            fret_copy(place, True, 0).start()

    for place in range(own_slots)[1:]:

        @pl.when(own_here(place))
        def _(place=place):
            own_pass(place)

    for place in range(near_slots):

        @pl.when(near_here(place))
        def _(place=place):
            fret_copy(place, True, 1).start()

    for place in range(own_slots):

        @pl.when(own_here(place))
        def _(place=place):
            fret_copy(place, False, 1).start()

    def add_early(which):
        for index, (tile, near) in enumerate(far_kinds):

            @pl.when(is_timed(tile, near, True))
            def _(index=index):
                fret_wait(index, which)
                for unit in range(UNITS):
                    picked = jnp.where(send_unit[index] == unit, send_used[index], 0)
                    spread = jnp.full((kb, width), picked, jnp.int32) > 0
                    total[which, unit * kb : (unit + 1) * kb, :] += jnp.where(
                        spread, fret_in[index, which].astype(F32), 0.0
                    )

    def add_late(which):
        late = [index for index, (_, near) in enumerate(far_kinds) if not near]
        for index in late:

            @pl.when(is_timed(*far_kinds[index], False))
            def _(index=index):
                fret_wait(index, which)

        pieces = []
        for unit in range(UNITS):
            acc = total[which, unit * kb : (unit + 1) * kb, :]
            for index in late:
                timed = is_timed(*far_kinds[index], False) & (send_unit[index] == unit)
                picked = jnp.where(timed, send_used[index], 0)
                spread = jnp.full((kb, width), picked, jnp.int32) > 0
                acc = acc + jnp.where(spread, fret_in[index, which].astype(F32), 0.0)
            pieces.append(acc)
        return jnp.concatenate(pieces, axis=0).astype(BF16)

    add_early(0)

    for side in sides:

        @pl.when(exists[side])
        def _(side=side):
            ret_wait(side)

    scale_rows = jnp.zeros((8, tokens), F32)
    for side in sides:
        for group in range(len(groups)):
            scale_rows = scale_rows + ret_scale_in[side, group]
    scales = to_columns(scale_rows)
    dq_groups = []
    for group, lanes in enumerate(groups):
        dq_sum = dq_acc[:, lanes]
        for side in sides:
            place = side * len(groups) + group
            coded = ret_in[side, :, lanes].astype(jnp.int32).astype(F32)
            dq_sum = dq_sum + coded * scales[:, place : place + 1]
        dq_groups.append(dq_sum)
    dq_sum = jnp.concatenate(dq_groups, axis=1)
    dq_norm = (dq_sum * score_scale).astype(BF16).astype(F32)
    query_wide = q_raw[...].astype(F32)
    weighted = gain_q * dq_norm
    x_start(1, lane_columns([(0, row_sums(weighted * query_wide))])[0:8])

    dk_norm = add_late(0).astype(F32)
    key_wide = k_raw[...].astype(F32)
    key_weighted = gain_k * dk_norm
    x_start(2, lane_columns([(1, row_sums(key_weighted * key_wide))])[0:8])

    q_factor = rates * rates * rates * x_finish(1) / full_width
    q_factor = to_columns(q_factor)[:, 0:1]
    dq_out[0, 0] = (q_rate * weighted - query_wide * q_factor).astype(BF16)

    add_early(1)
    dv_out[0, 0] = add_late(1)
    for side in sides:

        @pl.when(exists[side])
        def _(side=side):
            for message in messages:
                nbr_copy(side, message).wait_send()
            for group in range(len(groups)):
                for which in range(2):
                    ret_copy(side, group, which).wait_send()

    for index, (tile, near) in enumerate(far_kinds):

        @pl.when(is_sent(tile, near))
        def _(index=index, tile=tile, near=near):
            far_copy(index, tile, near).wait_send()

    for place in range(near_slots):

        @pl.when(near_here(place))
        def _(place=place):
            for which in range(2):
                fret_copy(place, True, which).wait_send()

    for place in range(own_slots):

        @pl.when(own_here(place))
        def _(place=place):
            for which in range(2):
                fret_copy(place, False, which).wait_send()

    k_factor = rates * rates * rates * x_finish(2) / full_width
    k_factor = to_columns(k_factor)[:, 1:2]
    dk_out[0, 0] = (k_rate * key_weighted - key_wide * k_factor).astype(BF16)


def copy_kernel(dq_in, dk_in, dv_in, dq_out, dk_out, dv_out, sem):
    pairs = ((dq_in, dq_out), (dk_in, dk_out), (dv_in, dv_out))
    copies = [
        pltpu.make_async_copy(source, target, sem.at[index])
        for index, (source, target) in enumerate(pairs)
    ]
    for copy in copies:
        copy.start()
    for copy in copies:
        copy.wait()


def body(sizes, q_raw, k_raw, values, upstream, outputs, logsumexp, gain_q, gain_k, far_list):
    rows, cols, parts = sizes
    tokens, width = q_raw.shape[2:]
    heads = logsumexp.shape[2]
    lse = logsumexp.transpose(0, 2, 1, 3)
    kb = tokens // UNITS
    stat_rows = -(-heads // 8) * 8
    sides = 2 + (1 if rows == 2 else 2 if rows > 2 else 0)
    near_slots = max((cols - 1) // 2, 1)
    own_slots = max(cols - 2, 1)
    kinds = max(2 * cols, 1)
    shape = jax.ShapeDtypeStruct(q_raw.shape, BF16)
    vmem = pl.BlockSpec(memory_space=pltpu.VMEM)
    anywhere = pl.BlockSpec(memory_space=pltpu.HBM)
    tile = pltpu.VMEM((tokens, width), BF16)
    near_units = pltpu.VMEM((near_slots, 2, kb, width), BF16)
    own_units = pltpu.VMEM((own_slots, 2, kb, width), BF16)
    dma = pltpu.SemaphoreType.DMA
    grads = pl.pallas_call(
        functools.partial(kernel, sizes),
        out_shape=(pltpu.VMEM(q_raw.shape, BF16),) * 3,
        in_specs=[anywhere] * 9,
        out_specs=(vmem,) * 3,
        scratch_shapes=[
            tile,
            tile,
            tile,
            tile,
            tile,
            tile,
            tile,
            pltpu.VMEM(lse.shape[1:], F32),
            pltpu.VMEM(gain_q.shape, BF16),
            pltpu.VMEM(gain_k.shape, BF16),
            pltpu.SMEM(far_list.shape, jnp.int32),
            pltpu.VMEM((2, stat_rows, tokens), F32),
            pltpu.VMEM((sides, 2, stat_rows, tokens), F32),
            pltpu.VMEM((tokens, width), F32),
            pltpu.VMEM((sides, tokens, width), BF16),
            pltpu.VMEM((sides, tokens, width), BF16),
            pltpu.VMEM((kinds, 2, kb, width), BF16),
            near_units,
            near_units,
            own_units,
            own_units,
            pltpu.VMEM((sides, tokens, width), F32),
            pltpu.VMEM((sides, tokens, width), jnp.int16),
            pltpu.VMEM((sides, tokens, width), jnp.int16),
            pltpu.VMEM((sides, 2, 8, tokens), F32),
            pltpu.VMEM((sides, 2, 8, tokens), F32),
            pltpu.VMEM((kinds, 2, kb, width), BF16),
            pltpu.VMEM((2, tokens, width), F32),
            pltpu.VMEM((3, parts, 8, 128), F32),
            dma((9,)),
            dma((sides, 2 + heads)),
            dma((sides, 2 + heads)),
            dma((kinds,)),
            dma((near_slots,)),
            dma((own_slots,)),
            dma((sides, 2, 2)),
            dma((sides, 2, 2)),
            dma((near_slots, 2)),
            dma((own_slots, 2)),
            dma((kinds, 2)),
            dma((3, parts)),
            dma((3, parts)),
        ],
        compiler_params=pltpu.CompilerParams(collective_id=0, has_side_effects=True),
    )(q_raw, k_raw, values, upstream, outputs, lse, gain_q, gain_k, far_list)
    return pl.pallas_call(
        copy_kernel,
        out_shape=(shape, shape, shape),
        in_specs=[vmem] * 3,
        out_specs=(anywhere,) * 3,
        scratch_shapes=[dma((3,))],
        compiler_params=pltpu.CompilerParams(vmem_limit_bytes=4 << 20),
    )(*grads)


def solution(mesh):
    sizes = (mesh.shape["ha"], mesh.shape["wa"], mesh.shape["hd"])
    tile = P("ha", "wa", None, "hd")
    return jax.shard_map(
        functools.partial(body, sizes),
        mesh=mesh,
        in_specs=(tile,) * 5 + (P("ha", "wa", "hd", None), P("hd"), P("hd"), P("ha", None, None)),
        out_specs=(tile,) * 3,
        check_vma=False,
    )
```

```python
import functools
import math

import jax
import jax.numpy as jnp
from jax import lax
from jax.experimental import pallas as pl
from jax.experimental.pallas import tpu as pltpu
from jax.sharding import PartitionSpec as P

UNITS = 4
EPS = 1e-06
MESH = pl.DeviceIdType.MESH
LAST = (((1,), (1,)), ((), ()))
FIRST = (((0,), (0,)), ((), ()))
PLAIN = (((1,), (0,)), ((), ()))
LEFT, RIGHT = 0, 1
CODE_MAX = 32767.0
F32 = jnp.float32
BF16 = jnp.bfloat16


def dot(a, b, dims):
    return lax.dot_general(a, b, dims, preferred_element_type=F32)


def kernel(
    sizes,
    q_hbm,
    k_hbm,
    v_hbm,
    u_hbm,
    o_hbm,
    lse_hbm,
    gain_q_hbm,
    gain_k_hbm,
    far_hbm,
    dq_out,
    dk_out,
    dv_out,
    q_raw,
    k_raw,
    vals,
    ups,
    outs,
    qn,
    kn,
    lse_ref,
    gain_q_ref,
    gain_k_ref,
    far_ref,
    stats,
    nbr_stats,
    dq_acc,
    nbr_q,
    nbr_u,
    far_pack,
    near_in,
    near_out,
    own_in,
    own_out,
    own_work,
    ret_acc,
    ret_out,
    ret_in,
    ret_scale,
    ret_scale_in,
    fret_in,
    total,
    xbuf,
    load_sem,
    nbr_send,
    nbr_recv,
    far_send,
    near_recv,
    own_recv,
    ret_send,
    ret_recv,
    near_send,
    own_send,
    fret_recv,
    x_send,
    x_recv,
):
    rows, cols, parts = sizes
    row = lax.axis_index("ha")
    col = lax.axis_index("wa")
    me = lax.axis_index("hd")
    tokens, width = q_raw.shape
    heads = lse_hbm.shape[1]
    hw = width // heads
    kb = tokens // UNITS
    full_width = width * parts
    slots = far_ref.shape[2]
    near_slots = near_in.shape[0]
    own_slots = own_in.shape[0]
    score_scale = 1.0 / math.sqrt(hw)
    head_lanes = [slice(head * hw, (head + 1) * hw) for head in range(heads)]
    split = (heads + 1) // 2
    groups = [slice(0, split * hw), slice(split * hw, width)] if heads > 1 else [slice(0, width)]

    barrier = pltpu.get_barrier_semaphore()
    hd_ids = [{"hd": lax.rem(me + off, parts)} for off in range(1, parts)]
    for target in hd_ids:
        pl.semaphore_signal(barrier, inc=1, device_id=target, device_id_type=MESH)

    exists = [col > 0, col < cols - 1]
    ids = [{"wa": col - 1}, {"wa": col + 1}]
    facing = [RIGHT, LEFT]
    if rows == 2:
        exists.append(True)
        ids.append({"ha": 1 - row})
        facing.append(2)
        pl.semaphore_signal(barrier, inc=1, device_id=ids[2], device_id_type=MESH)
    elif rows > 2:
        exists += [row > 0, row < rows - 1]
        ids += [{"ha": row - 1}, {"ha": row + 1}]
        facing += [3, 2]
        for side in (2, 3):

            @pl.when(exists[side])
            def _(side=side):
                pl.semaphore_signal(barrier, inc=1, device_id=ids[side], device_id_type=MESH)

    sides = range(len(ids))
    upright = range(2, len(ids))
    for off in range(1, cols):
        pl.semaphore_signal(
            barrier, inc=1, device_id={"wa": lax.rem(col + off, cols)}, device_id_type=MESH
        )

    loads = []
    for index, (source, target) in enumerate(
        (
            (u_hbm.at[0, 0], ups),
            (k_hbm.at[0, 0], k_raw),
            (q_hbm.at[0, 0], q_raw),
            (o_hbm.at[0, 0], outs),
            (v_hbm.at[0, 0], vals),
            (lse_hbm.at[0], lse_ref),
            (gain_q_hbm, gain_q_ref),
            (gain_k_hbm, gain_k_ref),
            (far_hbm, far_ref),
        )
    ):
        copy = pltpu.make_async_copy(source, target, load_sem.at[index])
        copy.start()
        loads.append(copy)

    inner = (col > 0) & (col < cols - 1)

    def lane_columns(columns):
        lane = lax.broadcasted_iota(jnp.int32, (tokens, 128), 1)
        mat = jnp.zeros((tokens, 128), F32)
        for place, column in columns:
            mat = jnp.where(lane == place, column, mat)
        return mat.T

    def row_sums(block):
        acc = block[:, :hw]
        for lanes in head_lanes[1:]:
            acc = acc + block[:, lanes]
        return jnp.sum(acc, axis=1, keepdims=True)

    def to_columns(rows8):
        return jnp.concatenate([rows8] * (tokens // rows8.shape[0]), axis=0).T

    def to_column(row1):
        return jnp.broadcast_to(row1, (128, tokens)).T[:, 0:1]

    def x_copy(which, off):
        return pltpu.make_async_remote_copy(
            src_ref=xbuf.at[which, me, pl.ds(0, x_rows[which])],
            dst_ref=xbuf.at[which, me, pl.ds(0, x_rows[which])],
            send_sem=x_send.at[which, off],
            recv_sem=x_recv.at[which, off],
            device_id=hd_ids[off - 1],
            device_id_type=MESH,
        )

    x_rows = (2, 1, 1)

    def x_start(which, sums):
        xbuf[which, me, 0 : x_rows[which]] = sums
        for off in range(1, parts):
            x_copy(which, off).start()

    def x_finish(which):
        for off in range(1, parts):
            x_copy(which, off).wait()
        acc = xbuf[which, 0, 0 : x_rows[which]]
        for part in range(1, parts):
            acc = acc + xbuf[which, part, 0 : x_rows[which]]
        return acc

    def side_id(side):
        if isinstance(side, int):
            return ids[side]
        return {"wa": jnp.where(side == RIGHT, col + 1, col - 1)}

    def face(side):
        return facing[side] if isinstance(side, int) else 1 - side

    def nbr_refs(side, message):
        if message == 0:
            return ups, nbr_u.at[side]
        if message == 1:
            return stats, nbr_stats.at[side]
        lanes = head_lanes[message - 2]
        return qn.at[:, lanes], nbr_q.at[side, :, lanes]

    messages = range(2 + heads)

    def nbr_copy(side, message):
        return pltpu.make_async_remote_copy(
            src_ref=nbr_refs(side, message)[0],
            dst_ref=nbr_refs(face(side), message)[1],
            send_sem=nbr_send.at[side, message],
            recv_sem=nbr_recv.at[face(side), message],
            device_id=ids[side],
            device_id_type=MESH,
        )

    def nbr_wait(side, message):
        pltpu.make_async_remote_copy(
            src_ref=nbr_refs(side, message)[0],
            dst_ref=nbr_refs(side, message)[1],
            send_sem=nbr_send.at[side, message],
            recv_sem=nbr_recv.at[side, message],
            device_id=ids[side],
            device_id_type=MESH,
        ).wait_recv()

    def nearer_left(tile):
        return 2 * tile < cols - 1

    from_left = nearer_left(col)
    behind = jnp.where(from_left, col, cols - 1 - col)
    first = jnp.where(from_left, RIGHT, LEFT)
    second = 1 - first
    has_first = jnp.where(from_left, col < cols - 1, col > 0)
    has_second = jnp.where(from_left, col > 0, col < cols - 1)

    def keeps_right(tile):
        return 2 * (tile + 1) < cols - 1

    def keeps_left(tile):
        return 2 * (tile - 1) > cols - 2

    has_own = keeps_right(col) | keeps_left(col)
    near_tiles = range(1, cols - 1)
    own_tiles = [tile for tile in range(cols) if keeps_right(tile) or keeps_left(tile)]

    def far_copy(index, tile, near):
        rank = col if nearer_left(tile) else cols - 1 - col
        landing, recv = (near_in, near_recv) if near else (own_in, own_recv)
        place = rank if near else rank - 2
        return pltpu.make_async_remote_copy(
            src_ref=far_pack.at[index],
            dst_ref=landing.at[place],
            send_sem=far_send.at[index],
            recv_sem=recv.at[place],
            device_id={"wa": tile},
            device_id_type=MESH,
        )

    def is_near(tile):
        return col < tile if nearer_left(tile) else col > tile

    def is_own(tile):
        return col > tile + 1 if keeps_right(tile) else col < tile - 1

    far_kinds = [(tile, True) for tile in near_tiles] + [(tile, False) for tile in own_tiles]

    def is_sent(tile, near):
        return is_near(tile) if near else is_own(tile)

    def near_here(place):
        return inner & (place < behind)

    def own_here(place):
        return has_own & (place >= behind)

    def ranked(rank):
        return jnp.where(from_left, rank, cols - 1 - rank)

    def far_wait(place, near):
        landing, recv = (near_in, near_recv) if near else (own_in, own_recv)
        pltpu.make_async_remote_copy(
            src_ref=far_pack.at[0],
            dst_ref=landing.at[place],
            send_sem=far_send.at[0],
            recv_sem=recv.at[place],
            device_id={"wa": ranked(place if near else place + 2)},
            device_id_type=MESH,
        ).wait_recv()

    def slot_of(near):
        if near:
            return col - 1
        after = col - cols + len(own_tiles)
        return len(near_tiles) + jnp.where(from_left, col, after)

    def fret_copy(place, near, which):
        source, send = (near_out, near_send) if near else (own_out, own_send)
        return pltpu.make_async_remote_copy(
            src_ref=source.at[place, which],
            dst_ref=fret_in.at[slot_of(near), which],
            send_sem=send.at[place, which],
            recv_sem=fret_recv.at[slot_of(near), which],
            device_id={"wa": ranked(place if near else place + 2)},
            device_id_type=MESH,
        )

    def fret_wait(index, which):
        pltpu.make_async_remote_copy(
            src_ref=fret_in.at[index, which],
            dst_ref=fret_in.at[index, which],
            send_sem=near_send.at[0, which],
            recv_sem=fret_recv.at[index, which],
            device_id={"wa": far_kinds[index][0]},
            device_id_type=MESH,
        ).wait_recv()

    def ret_refs(side, group, which):
        if which == 0:
            return ret_out.at[side, :, groups[group]], ret_in.at[side, :, groups[group]]
        return ret_scale.at[side, group], ret_scale_in.at[side, group]

    def ret_copy(side, group, which):
        return pltpu.make_async_remote_copy(
            src_ref=ret_refs(side, group, which)[0],
            dst_ref=ret_refs(face(side), group, which)[1],
            send_sem=ret_send.at[side, group, which],
            recv_sem=ret_recv.at[face(side), group, which],
            device_id=side_id(side),
            device_id_type=MESH,
        )

    def ret_start(side, group):
        part = ret_acc[side, :, groups[group]]
        largest = jnp.abs(part[:, :hw])
        for start in range(hw, part.shape[1], hw):
            largest = jnp.maximum(largest, jnp.abs(part[:, start : start + hw]))
        largest = jnp.maximum(jnp.max(largest, axis=1, keepdims=True), 1e-30)
        coded = jnp.round(part * (CODE_MAX / largest))
        ret_out[side, :, groups[group]] = coded.astype(jnp.int32).astype(jnp.int16)
        ret_copy(side, group, 0).start()
        place = face(side) * len(groups) + group
        ret_scale[side, group] = lane_columns([(place, largest / CODE_MAX)])[0:8]
        ret_copy(side, group, 1).start()

    def ret_wait(side):
        for group in range(len(groups)):
            for which in range(2):
                pltpu.make_async_remote_copy(
                    src_ref=ret_refs(side, group, which)[0],
                    dst_ref=ret_refs(side, group, which)[1],
                    send_sem=ret_send.at[side, group, which],
                    recv_sem=ret_recv.at[side, group, which],
                    device_id=ids[side],
                    device_id_type=MESH,
                ).wait_recv()

    def ret_start_all(group):
        @pl.when(has_first)
        def _():
            ret_start(first, group)

        for side in upright:

            @pl.when(exists[side])
            def _(side=side):
                ret_start(side, group)

        @pl.when(has_second)
        def _():
            ret_start(second, group)

    greeted = parts - 1 + cols - 1
    if rows == 2:
        greeted = greeted + 1
    elif rows > 2:
        greeted = greeted + jnp.minimum(row, 1) + jnp.minimum(rows - 1 - row, 1)
    loads[0].wait()
    pl.semaphore_wait(barrier, greeted)
    for side in sides:

        @pl.when(exists[side])
        def _(side=side):
            nbr_copy(side, 0).start()

    loads[1].wait()
    key_wide = k_raw[...].astype(F32)
    key_squares = row_sums(key_wide * key_wide)
    loads[2].wait()
    query_wide = q_raw[...].astype(F32)
    query_squares = row_sums(query_wide * query_wide)
    x_start(0, lane_columns([(0, query_squares), (1, key_squares)])[0:2])

    loads[3].wait()
    loads[5].wait()
    delta_columns = []
    for head, lanes in enumerate(head_lanes):
        product = ups[:, lanes].astype(F32) * outs[:, lanes].astype(F32)
        delta_columns.append((head, jnp.sum(product, axis=1, keepdims=True)))
    stats[0] = lane_columns(delta_columns)[0 : stats.shape[1]]
    for head in range(heads):
        stats[1, head : head + 1, :] = lse_ref[head]
    for side in sides:

        @pl.when(exists[side])
        def _(side=side):
            nbr_copy(side, 1).start()

        @pl.when(jnp.logical_not(exists[side]))
        def _(side=side):
            nbr_u[side] = jnp.zeros(nbr_u.shape[1:], BF16)
            nbr_q[side] = jnp.zeros(nbr_q.shape[1:], BF16)
            nbr_stats[side] = jnp.zeros(nbr_stats.shape[1:], F32)
            ret_in[side] = jnp.zeros(ret_in.shape[1:], jnp.int16)
            ret_scale_in[side] = jnp.zeros(ret_scale_in.shape[1:], F32)

    for place in range(near_slots):

        @pl.when(jnp.logical_not(near_here(place)))
        def _(place=place):
            near_in[place] = jnp.zeros(near_in.shape[1:], BF16)

    for place in range(own_slots):

        @pl.when(jnp.logical_not(own_here(place)))
        def _(place=place):
            own_in[place] = jnp.zeros(own_in.shape[1:], BF16)

    loads[8].wait()
    send_unit = []
    send_used = []
    for tile, near in far_kinds:
        query_col = tile if not near else tile + 1 if nearer_left(tile) else tile - 1
        unit = jnp.int32(0)
        asked = jnp.int32(0)
        for slot in range(slots):
            wanted = far_ref[0, query_col, slot] - col * UNITS
            hit = (wanted >= 0) & (wanted < UNITS)
            unit = jnp.where(hit, wanted, unit)
            asked = jnp.where(hit, 1, asked)
        send_unit.append(unit)
        send_used.append(jnp.where(is_sent(tile, near), asked, 0))

    def place_used(place, near):
        peer = ranked(place if near else place + 2)
        query_col = col
        if near:
            query_col = jnp.clip(jnp.where(from_left, col + 1, col - 1), 0, cols - 1)
        used = jnp.int32(0)
        for slot in range(slots):
            named = far_ref[0, query_col, slot] - peer * UNITS
            used = jnp.where((named >= 0) & (named < UNITS), 1, used)
        return jnp.where(near_here(place) if near else own_here(place), used, 0)

    near_used = [place_used(place, True) for place in range(near_slots)]
    own_used = [place_used(place, False) for place in range(own_slots)]

    def pick_unit(unit_wanted, source):
        wanted = jnp.full((kb, width), unit_wanted, jnp.int32)
        picked = source[0:kb, :].astype(F32)
        for unit in range(1, UNITS):
            block = source[unit * kb : (unit + 1) * kb, :].astype(F32)
            picked = jnp.where(wanted == unit, block, picked)
        return picked.astype(BF16)

    loads[4].wait()
    for index in range(len(far_kinds)):
        far_pack[index, 1] = pick_unit(send_unit[index], vals)

    loads[6].wait()
    loads[7].wait()
    gain_q = gain_q_ref[...].astype(F32).reshape(1, width)
    gain_k = gain_k_ref[...].astype(F32).reshape(1, width)
    rates = lax.rsqrt(x_finish(0) / full_width + EPS)
    rate_columns = to_columns(rates)
    q_rate = rate_columns[:, 0:1]
    k_rate = rate_columns[:, 1:2]
    kn[...] = (k_raw[...].astype(F32) * k_rate * gain_k).astype(BF16)

    def is_timed(tile, near, early):
        if near:
            return is_sent(tile, near) if early else False
        gap = (col - tile) * (col - tile)
        return is_sent(tile, near) & (gap == 4 if early else gap > 4)

    def far_start(early):
        for index, (tile, near) in enumerate(far_kinds):
            @pl.when(is_timed(tile, near, early))
            def _(index=index, tile=tile, near=near):
                far_pack[index, 0] = pick_unit(send_unit[index], kn)
                far_copy(index, tile, near).start()

    far_start(True)
    qn[...] = (q_raw[...].astype(F32) * q_rate * gain_q).astype(BF16)
    for side in sides:

        @pl.when(exists[side])
        def _(side=side):
            for head in range(split):
                nbr_copy(side, 2 + head).start()

    far_start(False)
    for side in sides:

        @pl.when(exists[side])
        def _(side=side):
            for head in range(split, heads):
                nbr_copy(side, 2 + head).start()

    def attend(keys, values, queries, upstream, delta_row, lse_row, used=None):
        weight = jnp.exp(dot(keys, queries, LAST) * score_scale - lse_row)
        if used is not None:
            weight = jnp.where(used, weight, 0.0)
        dweight = dot(values, upstream, LAST)
        dscore = (weight * (dweight - delta_row)).astype(BF16)
        weight_low = weight.astype(BF16)
        dq_part = dot(dscore, keys, FIRST)
        dk_parts, dv_parts = [], []
        for start in range(0, queries.shape[0], tokens):
            block = slice(start, start + tokens)
            dk_part = dot(dscore[:, block], queries[block], PLAIN) * score_scale
            dk_parts.append(dk_part.astype(BF16))
            dv_parts.append(dot(weight_low[:, block], upstream[block], PLAIN).astype(BF16))
        return dq_part, dk_parts, dv_parts

    for head, lanes in enumerate(head_lanes):
        dq_part, (dk_part,), (dv_part,) = attend(
            kn[:, lanes],
            vals[:, lanes],
            qn[:, lanes],
            ups[:, lanes],
            stats[0, head : head + 1, :],
            stats[1, head : head + 1, :],
        )
        dq_acc[:, lanes] = dq_part
        total[0, :, lanes] = dk_part.astype(F32)
        total[1, :, lanes] = dv_part.astype(F32)

    def own_scores(place):
        far_wait(place, False)
        used = jnp.full((kb, tokens), own_used[place], jnp.int32) > 0
        for head, lanes in enumerate(head_lanes):
            scores = dot(own_in[place, 0, :, lanes], qn[:, lanes], LAST) * score_scale
            weight = jnp.where(used, jnp.exp(scores - stats[1, head : head + 1, :]), 0.0)
            dweight = dot(own_in[place, 1, :, lanes], ups[:, lanes], LAST)
            dscore = (weight * (dweight - stats[0, head : head + 1, :])).astype(BF16)
            own_work[place, 0, head] = dscore
            own_work[place, 1, head] = weight.astype(BF16)
            own_out[place, 0, :, lanes] = (dot(dscore, qn[:, lanes], PLAIN) * score_scale).astype(BF16)
        fret_copy(place, False, 0).start()

    def own_rest(place):
        for head, lanes in enumerate(head_lanes):
            own_out[place, 1, :, lanes] = dot(own_work[place, 1, head], ups[:, lanes], PLAIN).astype(BF16)
            dq_acc[:, lanes] += dot(own_work[place, 0, head], own_in[place, 0, :, lanes], FIRST)

    def own_each(step, places):
        for place in places:

            @pl.when(own_here(place))
            def _(place=place):
                step(place)

    early_places, late_places = range(own_slots)[:1], range(own_slots)[1:]

    def stat_row(which, head):
        return jnp.concatenate([nbr_stats[side, which, head : head + 1, :] for side in sides], axis=1)

    own_each(own_scores, early_places)
    own_each(own_rest, early_places)
    for place in range(near_slots):

        @pl.when(near_here(place))
        def _(place=place):
            far_wait(place, True)

    near_mask = (
        jnp.concatenate([jnp.full((kb, tokens), flag, jnp.int32) for flag in near_used], axis=0) > 0
    )
    for head, lanes in enumerate(head_lanes):
        for side in sides:

            @pl.when(exists[side])
            def _(side=side, head=head):
                for message in (0, 1, 2) if head == 0 else (2 + head,):
                    nbr_wait(side, message)

        dq_part, dk_parts, dv_parts = attend(
            kn[:, lanes],
            vals[:, lanes],
            nbr_q[:, :, lanes].reshape(len(sides) * tokens, hw),
            nbr_u[:, :, lanes].reshape(len(sides) * tokens, hw),
            stat_row(0, head),
            stat_row(1, head),
        )
        ret_acc[:, :, lanes] = dq_part.reshape(len(sides), tokens, hw)
        for which, terms in enumerate((dk_parts, dv_parts)):
            acc = total[which, :, lanes]
            for term in terms:
                acc = acc + term.astype(F32)
            total[which, :, lanes] = acc
        dq_part, (dk_part,), (dv_part,) = attend(
            near_in[:, 0, :, lanes].reshape(near_slots * kb, hw),
            near_in[:, 1, :, lanes].reshape(near_slots * kb, hw),
            nbr_q[first, :, lanes],
            nbr_u[first, :, lanes],
            nbr_stats[first, 0, head : head + 1, :],
            nbr_stats[first, 1, head : head + 1, :],
            near_mask,
        )
        ret_acc[first, :, lanes] += dq_part
        near_out[:, 0, :, lanes] = dk_part.reshape(near_slots, kb, hw)
        near_out[:, 1, :, lanes] = dv_part.reshape(near_slots, kb, hw)

        if head + 1 == heads:
            own_each(own_scores, late_places)
        if head + 1 in (split, heads):
            ret_start_all(head // split)

    for place in range(near_slots):

        @pl.when(near_here(place))
        def _(place=place):
            fret_copy(place, True, 0).start()

    own_each(own_rest, late_places)
    for place in range(near_slots):

        @pl.when(near_here(place))
        def _(place=place):
            fret_copy(place, True, 1).start()

    for place in range(own_slots):

        @pl.when(own_here(place))
        def _(place=place):
            fret_copy(place, False, 1).start()

    def add_early(which):
        for index, (tile, near) in enumerate(far_kinds):

            @pl.when(is_timed(tile, near, True))
            def _(index=index):
                fret_wait(index, which)
                for unit in range(UNITS):
                    picked = jnp.where(send_unit[index] == unit, send_used[index], 0)
                    spread = jnp.full((kb, width), picked, jnp.int32) > 0
                    total[which, unit * kb : (unit + 1) * kb, :] += jnp.where(
                        spread, fret_in[index, which].astype(F32), 0.0
                    )

    def add_late(which):
        late = [index for index, (_, near) in enumerate(far_kinds) if not near]
        for index in late:

            @pl.when(is_timed(*far_kinds[index], False))
            def _(index=index):
                fret_wait(index, which)

        pieces = []
        for unit in range(UNITS):
            acc = total[which, unit * kb : (unit + 1) * kb, :]
            for index in late:
                timed = is_timed(*far_kinds[index], False) & (send_unit[index] == unit)
                picked = jnp.where(timed, send_used[index], 0)
                spread = jnp.full((kb, width), picked, jnp.int32) > 0
                acc = acc + jnp.where(spread, fret_in[index, which].astype(F32), 0.0)
            pieces.append(acc)
        return jnp.concatenate(pieces, axis=0).astype(BF16)

    add_early(0)

    for side in sides:

        @pl.when(exists[side])
        def _(side=side):
            ret_wait(side)

    scale_rows = jnp.zeros((8, tokens), F32)
    for side in sides:
        for group in range(len(groups)):
            scale_rows = scale_rows + ret_scale_in[side, group]
    scales = to_columns(scale_rows)
    dq_groups = []
    for group, lanes in enumerate(groups):
        dq_sum = dq_acc[:, lanes]
        for side in sides:
            place = side * len(groups) + group
            coded = ret_in[side, :, lanes].astype(jnp.int32).astype(F32)
            dq_sum = dq_sum + coded * scales[:, place : place + 1]
        dq_groups.append(dq_sum)
    dq_sum = jnp.concatenate(dq_groups, axis=1)
    dq_norm = (dq_sum * score_scale).astype(BF16).astype(F32)
    query_wide = q_raw[...].astype(F32)
    weighted = gain_q * dq_norm
    x_start(1, lane_columns([(0, row_sums(weighted * query_wide))])[0:1])

    dk_norm = add_late(0).astype(F32)
    key_wide = k_raw[...].astype(F32)
    key_weighted = gain_k * dk_norm
    x_start(2, lane_columns([(0, row_sums(key_weighted * key_wide))])[0:1])

    q_factor = to_column(rates[0:1] * rates[0:1] * rates[0:1] * x_finish(1) / full_width)
    dq_out[0, 0] = (q_rate * weighted - query_wide * q_factor).astype(BF16)

    add_early(1)
    dv_out[0, 0] = add_late(1)
    for side in sides:

        @pl.when(exists[side])
        def _(side=side):
            for message in messages:
                nbr_copy(side, message).wait_send()
            for group in range(len(groups)):
                for which in range(2):
                    ret_copy(side, group, which).wait_send()

    for index, (tile, near) in enumerate(far_kinds):

        @pl.when(is_sent(tile, near))
        def _(index=index, tile=tile, near=near):
            far_copy(index, tile, near).wait_send()

    for place in range(near_slots):

        @pl.when(near_here(place))
        def _(place=place):
            for which in range(2):
                fret_copy(place, True, which).wait_send()

    for place in range(own_slots):

        @pl.when(own_here(place))
        def _(place=place):
            for which in range(2):
                fret_copy(place, False, which).wait_send()

    k_factor = to_column(rates[1:2] * rates[1:2] * rates[1:2] * x_finish(2) / full_width)
    dk_out[0, 0] = (k_rate * key_weighted - key_wide * k_factor).astype(BF16)


def copy_kernel(dq_in, dk_in, dv_in, dq_out, dk_out, dv_out, sem):
    pairs = ((dq_in, dq_out), (dk_in, dk_out), (dv_in, dv_out))
    copies = [
        pltpu.make_async_copy(source, target, sem.at[index])
        for index, (source, target) in enumerate(pairs)
    ]
    for copy in copies:
        copy.start()
    for copy in copies:
        copy.wait()


def body(sizes, q_raw, k_raw, values, upstream, outputs, logsumexp, gain_q, gain_k, far_list):
    rows, cols, parts = sizes
    tokens, width = q_raw.shape[2:]
    heads = logsumexp.shape[2]
    lse = logsumexp.transpose(0, 2, 1, 3)
    kb = tokens // UNITS
    stat_rows = -(-heads // 8) * 8
    sides = 2 + (1 if rows == 2 else 2 if rows > 2 else 0)
    near_slots = max((cols - 1) // 2, 1)
    own_slots = max(cols - 2, 1)
    kinds = max(2 * cols, 1)
    shape = jax.ShapeDtypeStruct(q_raw.shape, BF16)
    vmem = pl.BlockSpec(memory_space=pltpu.VMEM)
    anywhere = pl.BlockSpec(memory_space=pltpu.HBM)
    tile = pltpu.VMEM((tokens, width), BF16)
    near_units = pltpu.VMEM((near_slots, 2, kb, width), BF16)
    own_units = pltpu.VMEM((own_slots, 2, kb, width), BF16)
    dma = pltpu.SemaphoreType.DMA
    grads = pl.pallas_call(
        functools.partial(kernel, sizes),
        out_shape=(pltpu.VMEM(q_raw.shape, BF16),) * 3,
        in_specs=[anywhere] * 9,
        out_specs=(vmem,) * 3,
        scratch_shapes=[
            tile,
            tile,
            tile,
            tile,
            tile,
            tile,
            tile,
            pltpu.VMEM(lse.shape[1:], F32),
            pltpu.VMEM(gain_q.shape, BF16),
            pltpu.VMEM(gain_k.shape, BF16),
            pltpu.SMEM(far_list.shape, jnp.int32),
            pltpu.VMEM((2, stat_rows, tokens), F32),
            pltpu.VMEM((sides, 2, stat_rows, tokens), F32),
            pltpu.VMEM((tokens, width), F32),
            pltpu.VMEM((sides, tokens, width), BF16),
            pltpu.VMEM((sides, tokens, width), BF16),
            pltpu.VMEM((kinds, 2, kb, width), BF16),
            near_units,
            near_units,
            own_units,
            own_units,
            pltpu.VMEM((own_slots, 2, heads, kb, tokens), BF16),
            pltpu.VMEM((sides, tokens, width), F32),
            pltpu.VMEM((sides, tokens, width), jnp.int16),
            pltpu.VMEM((sides, tokens, width), jnp.int16),
            pltpu.VMEM((sides, 2, 8, tokens), F32),
            pltpu.VMEM((sides, 2, 8, tokens), F32),
            pltpu.VMEM((kinds, 2, kb, width), BF16),
            pltpu.VMEM((2, tokens, width), F32),
            pltpu.VMEM((3, parts, 8, 128), F32),
            dma((9,)),
            dma((sides, 2 + heads)),
            dma((sides, 2 + heads)),
            dma((kinds,)),
            dma((near_slots,)),
            dma((own_slots,)),
            dma((sides, 2, 2)),
            dma((sides, 2, 2)),
            dma((near_slots, 2)),
            dma((own_slots, 2)),
            dma((kinds, 2)),
            dma((3, parts)),
            dma((3, parts)),
        ],
        compiler_params=pltpu.CompilerParams(collective_id=0, has_side_effects=True),
    )(q_raw, k_raw, values, upstream, outputs, lse, gain_q, gain_k, far_list)
    return pl.pallas_call(
        copy_kernel,
        out_shape=(shape, shape, shape),
        in_specs=[vmem] * 3,
        out_specs=(anywhere,) * 3,
        scratch_shapes=[dma((3,))],
        compiler_params=pltpu.CompilerParams(vmem_limit_bytes=4 << 20),
    )(*grads)


def solution(mesh):
    sizes = (mesh.shape["ha"], mesh.shape["wa"], mesh.shape["hd"])
    tile = P("ha", "wa", None, "hd")
    return jax.shard_map(
        functools.partial(body, sizes),
        mesh=mesh,
        in_specs=(tile,) * 5 + (P("ha", "wa", "hd", None), P("hd"), P("hd"), P("ha", None, None)),
        out_specs=(tile,) * 3,
        check_vma=False,
    )
```

```python
import functools
import math

import jax
import jax.numpy as jnp
from jax import lax
from jax.experimental import pallas as pl
from jax.experimental.pallas import tpu as pltpu
from jax.sharding import PartitionSpec as P

UNITS = 4
EPS = 1e-06
MESH = pl.DeviceIdType.MESH
LAST = (((1,), (1,)), ((), ()))
FIRST = (((0,), (0,)), ((), ()))
PLAIN = (((1,), (0,)), ((), ()))
LEFT, RIGHT = 0, 1
CODE_MAX = 32767.0
F32 = jnp.float32
BF16 = jnp.bfloat16


def dot(a, b, dims):
    return lax.dot_general(a, b, dims, preferred_element_type=F32)


def kernel(
    sizes,
    q_hbm,
    k_hbm,
    v_hbm,
    u_hbm,
    o_hbm,
    lse_hbm,
    gain_q_hbm,
    gain_k_hbm,
    far_hbm,
    dq_out,
    dk_out,
    dv_out,
    q_raw,
    k_raw,
    vals,
    ups,
    outs,
    qn,
    kn,
    lse_ref,
    gain_q_ref,
    gain_k_ref,
    far_ref,
    stats,
    nbr_stats,
    dq_acc,
    nbr_q,
    nbr_u,
    far_pack,
    near_in,
    near_out,
    own_in,
    own_out,
    own_work,
    ret_acc,
    ret_out,
    ret_in,
    ret_scale,
    ret_scale_in,
    fret_in,
    total,
    xbuf,
    load_sem,
    nbr_send,
    nbr_recv,
    far_send,
    near_recv,
    own_recv,
    ret_send,
    ret_recv,
    near_send,
    own_send,
    fret_recv,
    x_send,
    x_recv,
):
    rows, cols, parts = sizes
    row = lax.axis_index("ha")
    col = lax.axis_index("wa")
    me = lax.axis_index("hd")
    tokens, width = q_raw.shape
    heads = lse_hbm.shape[1]
    hw = width // heads
    kb = tokens // UNITS
    full_width = width * parts
    slots = far_ref.shape[2]
    near_slots = near_in.shape[0]
    own_slots = own_in.shape[0]
    score_scale = 1.0 / math.sqrt(hw)
    head_lanes = [slice(head * hw, (head + 1) * hw) for head in range(heads)]
    split = (heads + 1) // 2
    groups = [slice(0, split * hw), slice(split * hw, width)] if heads > 1 else [slice(0, width)]

    barrier = pltpu.get_barrier_semaphore()
    hd_ids = [{"hd": lax.rem(me + off, parts)} for off in range(1, parts)]
    for target in hd_ids:
        pl.semaphore_signal(barrier, inc=1, device_id=target, device_id_type=MESH)

    exists = [col > 0, col < cols - 1]
    ids = [{"wa": col - 1}, {"wa": col + 1}]
    facing = [RIGHT, LEFT]
    if rows == 2:
        exists.append(True)
        ids.append({"ha": 1 - row})
        facing.append(2)
        pl.semaphore_signal(barrier, inc=1, device_id=ids[2], device_id_type=MESH)
    elif rows > 2:
        exists += [row > 0, row < rows - 1]
        ids += [{"ha": row - 1}, {"ha": row + 1}]
        facing += [3, 2]
        for side in (2, 3):

            @pl.when(exists[side])
            def _(side=side):
                pl.semaphore_signal(barrier, inc=1, device_id=ids[side], device_id_type=MESH)

    sides = range(len(ids))
    upright = range(2, len(ids))
    for off in range(1, cols):
        pl.semaphore_signal(
            barrier, inc=1, device_id={"wa": lax.rem(col + off, cols)}, device_id_type=MESH
        )

    loads = []
    for index, (source, target) in enumerate(
        (
            (u_hbm.at[0, 0], ups),
            (k_hbm.at[0, 0], k_raw),
            (q_hbm.at[0, 0], q_raw),
            (o_hbm.at[0, 0], outs),
            (v_hbm.at[0, 0], vals),
            (lse_hbm.at[0], lse_ref),
            (gain_q_hbm, gain_q_ref),
            (gain_k_hbm, gain_k_ref),
            (far_hbm, far_ref),
        )
    ):
        copy = pltpu.make_async_copy(source, target, load_sem.at[index])
        copy.start()
        loads.append(copy)

    inner = (col > 0) & (col < cols - 1)

    def lane_columns(columns):
        lane = lax.broadcasted_iota(jnp.int32, (tokens, 128), 1)
        mat = jnp.zeros((tokens, 128), F32)
        for place, column in columns:
            mat = jnp.where(lane == place, column, mat)
        return mat.T

    def row_sums(block):
        acc = block[:, :hw]
        for lanes in head_lanes[1:]:
            acc = acc + block[:, lanes]
        return jnp.sum(acc, axis=1, keepdims=True)

    def to_columns(rows8):
        return jnp.concatenate([rows8] * (tokens // rows8.shape[0]), axis=0).T

    def to_column(row1):
        return jnp.broadcast_to(row1, (128, tokens)).T[:, 0:1]

    def x_copy(which, off):
        return pltpu.make_async_remote_copy(
            src_ref=xbuf.at[which, me, pl.ds(0, x_rows[which])],
            dst_ref=xbuf.at[which, me, pl.ds(0, x_rows[which])],
            send_sem=x_send.at[which, off],
            recv_sem=x_recv.at[which, off],
            device_id=hd_ids[off - 1],
            device_id_type=MESH,
        )

    x_rows = (2, 1, 1)

    def x_start(which, sums):
        xbuf[which, me, 0 : x_rows[which]] = sums
        for off in range(1, parts):
            x_copy(which, off).start()

    def x_finish(which):
        for off in range(1, parts):
            x_copy(which, off).wait()
        acc = xbuf[which, 0, 0 : x_rows[which]]
        for part in range(1, parts):
            acc = acc + xbuf[which, part, 0 : x_rows[which]]
        return acc

    def side_id(side):
        if isinstance(side, int):
            return ids[side]
        return {"wa": jnp.where(side == RIGHT, col + 1, col - 1)}

    def face(side):
        return facing[side] if isinstance(side, int) else 1 - side

    def nbr_refs(side, message):
        if message == 0:
            return ups, nbr_u.at[side]
        if message == 1:
            return stats, nbr_stats.at[side]
        lanes = head_lanes[message - 2]
        return qn.at[:, lanes], nbr_q.at[side, :, lanes]

    messages = range(2 + heads)

    def nbr_copy(side, message):
        return pltpu.make_async_remote_copy(
            src_ref=nbr_refs(side, message)[0],
            dst_ref=nbr_refs(face(side), message)[1],
            send_sem=nbr_send.at[side, message],
            recv_sem=nbr_recv.at[face(side), message],
            device_id=ids[side],
            device_id_type=MESH,
        )

    def nbr_wait(side, message):
        pltpu.make_async_remote_copy(
            src_ref=nbr_refs(side, message)[0],
            dst_ref=nbr_refs(side, message)[1],
            send_sem=nbr_send.at[side, message],
            recv_sem=nbr_recv.at[side, message],
            device_id=ids[side],
            device_id_type=MESH,
        ).wait_recv()

    def nearer_left(tile):
        return 2 * tile < cols - 1

    from_left = nearer_left(col)
    behind = jnp.where(from_left, col, cols - 1 - col)
    first = jnp.where(from_left, RIGHT, LEFT)
    second = 1 - first
    has_first = jnp.where(from_left, col < cols - 1, col > 0)
    has_second = jnp.where(from_left, col > 0, col < cols - 1)

    def keeps_right(tile):
        return 2 * (tile + 1) < cols - 1

    def keeps_left(tile):
        return 2 * (tile - 1) > cols - 2

    has_own = keeps_right(col) | keeps_left(col)
    near_tiles = range(1, cols - 1)
    own_tiles = [tile for tile in range(cols) if keeps_right(tile) or keeps_left(tile)]

    def far_copy(index, tile, near):
        rank = col if nearer_left(tile) else cols - 1 - col
        landing, recv = (near_in, near_recv) if near else (own_in, own_recv)
        place = rank if near else rank - 2
        return pltpu.make_async_remote_copy(
            src_ref=far_pack.at[index],
            dst_ref=landing.at[place],
            send_sem=far_send.at[index],
            recv_sem=recv.at[place],
            device_id={"wa": tile},
            device_id_type=MESH,
        )

    def is_near(tile):
        return col < tile if nearer_left(tile) else col > tile

    def is_own(tile):
        return col > tile + 1 if keeps_right(tile) else col < tile - 1

    far_kinds = [(tile, True) for tile in near_tiles] + [(tile, False) for tile in own_tiles]

    def is_sent(tile, near):
        return is_near(tile) if near else is_own(tile)

    def near_here(place):
        return inner & (place < behind)

    def own_here(place):
        return has_own & (place >= behind)

    def ranked(rank):
        return jnp.where(from_left, rank, cols - 1 - rank)

    def far_wait(place, near):
        landing, recv = (near_in, near_recv) if near else (own_in, own_recv)
        pltpu.make_async_remote_copy(
            src_ref=far_pack.at[0],
            dst_ref=landing.at[place],
            send_sem=far_send.at[0],
            recv_sem=recv.at[place],
            device_id={"wa": ranked(place if near else place + 2)},
            device_id_type=MESH,
        ).wait_recv()

    def slot_of(near):
        if near:
            return col - 1
        after = col - cols + len(own_tiles)
        return len(near_tiles) + jnp.where(from_left, col, after)

    def fret_copy(place, near, which):
        source, send = (near_out, near_send) if near else (own_out, own_send)
        return pltpu.make_async_remote_copy(
            src_ref=source.at[place, which],
            dst_ref=fret_in.at[slot_of(near), which],
            send_sem=send.at[place, which],
            recv_sem=fret_recv.at[slot_of(near), which],
            device_id={"wa": ranked(place if near else place + 2)},
            device_id_type=MESH,
        )

    def fret_wait(index, which):
        pltpu.make_async_remote_copy(
            src_ref=fret_in.at[index, which],
            dst_ref=fret_in.at[index, which],
            send_sem=near_send.at[0, which],
            recv_sem=fret_recv.at[index, which],
            device_id={"wa": far_kinds[index][0]},
            device_id_type=MESH,
        ).wait_recv()

    def ret_refs(side, group, which):
        if which == 0:
            return ret_out.at[side, :, groups[group]], ret_in.at[side, :, groups[group]]
        return ret_scale.at[side, group], ret_scale_in.at[side, group]

    def ret_copy(side, group, which):
        return pltpu.make_async_remote_copy(
            src_ref=ret_refs(side, group, which)[0],
            dst_ref=ret_refs(face(side), group, which)[1],
            send_sem=ret_send.at[side, group, which],
            recv_sem=ret_recv.at[face(side), group, which],
            device_id=side_id(side),
            device_id_type=MESH,
        )

    def ret_start(side, group):
        part = ret_acc[side, :, groups[group]]
        largest = jnp.abs(part[:, :hw])
        for start in range(hw, part.shape[1], hw):
            largest = jnp.maximum(largest, jnp.abs(part[:, start : start + hw]))
        largest = jnp.maximum(jnp.max(largest, axis=1, keepdims=True), 1e-30)
        coded = jnp.round(part * (CODE_MAX / largest))
        ret_out[side, :, groups[group]] = coded.astype(jnp.int32).astype(jnp.int16)
        ret_copy(side, group, 0).start()
        place = face(side) * len(groups) + group
        ret_scale[side, group] = lane_columns([(place, largest / CODE_MAX)])[0:8]
        ret_copy(side, group, 1).start()

    def ret_wait(side):
        for group in range(len(groups)):
            for which in range(2):
                pltpu.make_async_remote_copy(
                    src_ref=ret_refs(side, group, which)[0],
                    dst_ref=ret_refs(side, group, which)[1],
                    send_sem=ret_send.at[side, group, which],
                    recv_sem=ret_recv.at[side, group, which],
                    device_id=ids[side],
                    device_id_type=MESH,
                ).wait_recv()

    def ret_start_all(group):
        @pl.when(has_first)
        def _():
            ret_start(first, group)

        for side in upright:

            @pl.when(exists[side])
            def _(side=side):
                ret_start(side, group)

        @pl.when(has_second)
        def _():
            ret_start(second, group)

    greeted = parts - 1 + cols - 1
    if rows == 2:
        greeted = greeted + 1
    elif rows > 2:
        greeted = greeted + jnp.minimum(row, 1) + jnp.minimum(rows - 1 - row, 1)
    loads[0].wait()
    pl.semaphore_wait(barrier, greeted)
    for side in sides:

        @pl.when(exists[side])
        def _(side=side):
            nbr_copy(side, 0).start()

    loads[1].wait()
    key_wide = k_raw[...].astype(F32)
    key_squares = row_sums(key_wide * key_wide)
    loads[2].wait()
    query_wide = q_raw[...].astype(F32)
    query_squares = row_sums(query_wide * query_wide)
    x_start(0, lane_columns([(0, query_squares), (1, key_squares)])[0:2])

    loads[3].wait()
    loads[5].wait()
    delta_columns = []
    for head, lanes in enumerate(head_lanes):
        product = ups[:, lanes].astype(F32) * outs[:, lanes].astype(F32)
        delta_columns.append((head, jnp.sum(product, axis=1, keepdims=True)))
    stats[0] = lane_columns(delta_columns)[0 : stats.shape[1]]
    for head in range(heads):
        stats[1, head : head + 1, :] = lse_ref[head]
    for side in sides:

        @pl.when(exists[side])
        def _(side=side):
            nbr_copy(side, 1).start()

        @pl.when(jnp.logical_not(exists[side]))
        def _(side=side):
            nbr_u[side] = jnp.zeros(nbr_u.shape[1:], BF16)
            nbr_q[side] = jnp.zeros(nbr_q.shape[1:], BF16)
            nbr_stats[side] = jnp.zeros(nbr_stats.shape[1:], F32)
            ret_in[side] = jnp.zeros(ret_in.shape[1:], jnp.int16)
            ret_scale_in[side] = jnp.zeros(ret_scale_in.shape[1:], F32)

    for place in range(near_slots):

        @pl.when(jnp.logical_not(near_here(place)))
        def _(place=place):
            near_in[place] = jnp.zeros(near_in.shape[1:], BF16)

    for place in range(own_slots):

        @pl.when(jnp.logical_not(own_here(place)))
        def _(place=place):
            own_in[place] = jnp.zeros(own_in.shape[1:], BF16)

    loads[8].wait()
    send_unit = []
    send_used = []
    for tile, near in far_kinds:
        query_col = tile if not near else tile + 1 if nearer_left(tile) else tile - 1
        unit = jnp.int32(0)
        asked = jnp.int32(0)
        for slot in range(slots):
            wanted = far_ref[0, query_col, slot] - col * UNITS
            hit = (wanted >= 0) & (wanted < UNITS)
            unit = jnp.where(hit, wanted, unit)
            asked = jnp.where(hit, 1, asked)
        send_unit.append(unit)
        send_used.append(jnp.where(is_sent(tile, near), asked, 0))

    def place_used(place, near):
        peer = ranked(place if near else place + 2)
        query_col = col
        if near:
            query_col = jnp.clip(jnp.where(from_left, col + 1, col - 1), 0, cols - 1)
        used = jnp.int32(0)
        for slot in range(slots):
            named = far_ref[0, query_col, slot] - peer * UNITS
            used = jnp.where((named >= 0) & (named < UNITS), 1, used)
        return jnp.where(near_here(place) if near else own_here(place), used, 0)

    near_used = [place_used(place, True) for place in range(near_slots)]
    own_used = [place_used(place, False) for place in range(own_slots)]

    def pick_unit(unit_wanted, source):
        wanted = jnp.full((kb, width), unit_wanted, jnp.int32)
        picked = source[0:kb, :].astype(F32)
        for unit in range(1, UNITS):
            block = source[unit * kb : (unit + 1) * kb, :].astype(F32)
            picked = jnp.where(wanted == unit, block, picked)
        return picked.astype(BF16)

    loads[4].wait()
    for index in range(len(far_kinds)):
        far_pack[index, 1] = pick_unit(send_unit[index], vals)

    loads[6].wait()
    loads[7].wait()
    gain_q = gain_q_ref[...].astype(F32).reshape(1, width)
    gain_k = gain_k_ref[...].astype(F32).reshape(1, width)
    rates = lax.rsqrt(x_finish(0) / full_width + EPS)
    rate_columns = to_columns(rates)
    q_rate = rate_columns[:, 0:1]
    k_rate = rate_columns[:, 1:2]
    kn[...] = (k_raw[...].astype(F32) * k_rate * gain_k).astype(BF16)

    def is_timed(tile, near, early):
        if near:
            return is_sent(tile, near) if early else False
        gap = (col - tile) * (col - tile)
        return is_sent(tile, near) & (gap == 4 if early else gap > 4)

    def far_start(early):
        for index, (tile, near) in enumerate(far_kinds):
            @pl.when(is_timed(tile, near, early))
            def _(index=index, tile=tile, near=near):
                far_pack[index, 0] = pick_unit(send_unit[index], kn)
                far_copy(index, tile, near).start()

    far_start(True)
    qn[...] = (q_raw[...].astype(F32) * q_rate * gain_q).astype(BF16)
    for side in sides:

        @pl.when(exists[side])
        def _(side=side):
            for head in range(split):
                nbr_copy(side, 2 + head).start()

    far_start(False)
    for side in sides:

        @pl.when(exists[side])
        def _(side=side):
            for head in range(split, heads):
                nbr_copy(side, 2 + head).start()

    def attend(keys, values, queries, upstream, delta_row, lse_row, used=None):
        weight = jnp.exp(dot(keys, queries, LAST) * score_scale - lse_row)
        if used is not None:
            weight = jnp.where(used, weight, 0.0)
        dweight = dot(values, upstream, LAST)
        dscore = (weight * (dweight - delta_row)).astype(BF16)
        weight_low = weight.astype(BF16)
        dq_part = dot(dscore, keys, FIRST)
        dk_parts, dv_parts = [], []
        for start in range(0, queries.shape[0], tokens):
            block = slice(start, start + tokens)
            dk_part = dot(dscore[:, block], queries[block], PLAIN) * score_scale
            dk_parts.append(dk_part.astype(BF16))
            dv_parts.append(dot(weight_low[:, block], upstream[block], PLAIN).astype(BF16))
        return dq_part, dk_parts, dv_parts

    for head, lanes in enumerate(head_lanes):
        dq_part, (dk_part,), (dv_part,) = attend(
            kn[:, lanes],
            vals[:, lanes],
            qn[:, lanes],
            ups[:, lanes],
            stats[0, head : head + 1, :],
            stats[1, head : head + 1, :],
        )
        dq_acc[:, lanes] = dq_part
        total[0, :, lanes] = dk_part.astype(F32)
        total[1, :, lanes] = dv_part.astype(F32)

    def own_scores(place):
        far_wait(place, False)
        used = jnp.full((kb, tokens), own_used[place], jnp.int32) > 0
        for head, lanes in enumerate(head_lanes):
            scores = dot(own_in[place, 0, :, lanes], qn[:, lanes], LAST) * score_scale
            weight = jnp.where(used, jnp.exp(scores - stats[1, head : head + 1, :]), 0.0)
            dweight = dot(own_in[place, 1, :, lanes], ups[:, lanes], LAST)
            dscore = (weight * (dweight - stats[0, head : head + 1, :])).astype(BF16)
            own_work[place, 0, head] = dscore
            own_work[place, 1, head] = weight.astype(BF16)
            own_out[place, 0, :, lanes] = (dot(dscore, qn[:, lanes], PLAIN) * score_scale).astype(BF16)
        fret_copy(place, False, 0).start()

    def own_rest(place):
        for head, lanes in enumerate(head_lanes):
            own_out[place, 1, :, lanes] = dot(own_work[place, 1, head], ups[:, lanes], PLAIN).astype(BF16)
            dq_acc[:, lanes] += dot(own_work[place, 0, head], own_in[place, 0, :, lanes], FIRST)

    def own_each(step, places):
        for place in places:

            @pl.when(own_here(place))
            def _(place=place):
                step(place)

    early_places, late_places = range(own_slots)[:1], range(own_slots)[1:]

    def stat_row(which, head):
        return jnp.concatenate([nbr_stats[side, which, head : head + 1, :] for side in sides], axis=1)

    own_each(own_scores, early_places)
    own_each(own_rest, early_places)
    for place in range(near_slots):

        @pl.when(near_here(place))
        def _(place=place):
            far_wait(place, True)

    near_rows = [
        jnp.concatenate(
            [jnp.full((kb, tokens), jnp.where(first == side, flag, 0), jnp.int32) for side in sides],
            axis=1,
        )
        for flag in near_used
    ]
    all_rows = jnp.ones((tokens, len(sides) * tokens), jnp.int32)
    side_mask = jnp.concatenate([all_rows] + near_rows, axis=0) > 0

    def with_near(own, which, lanes):
        near = near_in[:, which, :, lanes].reshape(near_slots * kb, hw)
        return jnp.concatenate([own[:, lanes], near], axis=0)

    for head, lanes in enumerate(head_lanes):
        for side in sides:

            @pl.when(exists[side])
            def _(side=side, head=head):
                for message in (0, 1, 2) if head == 0 else (2 + head,):
                    nbr_wait(side, message)

        dq_part, dk_parts, dv_parts = attend(
            with_near(kn, 0, lanes),
            with_near(vals, 1, lanes),
            nbr_q[:, :, lanes].reshape(len(sides) * tokens, hw),
            nbr_u[:, :, lanes].reshape(len(sides) * tokens, hw),
            stat_row(0, head),
            stat_row(1, head),
            side_mask,
        )
        ret_acc[:, :, lanes] = dq_part.reshape(len(sides), tokens, hw)
        for which, terms in enumerate((dk_parts, dv_parts)):
            acc = total[which, :, lanes]
            for term in terms:
                acc = acc + term[:tokens].astype(F32)
            total[which, :, lanes] = acc
            far_acc = terms[0][tokens:].astype(F32)
            for term in terms[1:]:
                far_acc = far_acc + term[tokens:].astype(F32)
            near_out[:, which, :, lanes] = far_acc.astype(BF16).reshape(near_slots, kb, hw)
        if head + 1 in (split, heads):
            ret_start_all(head // split)

    for place in range(near_slots):

        @pl.when(near_here(place))
        def _(place=place):
            fret_copy(place, True, 0).start()

    own_each(own_scores, late_places)
    own_each(own_rest, late_places)
    for place in range(near_slots):

        @pl.when(near_here(place))
        def _(place=place):
            fret_copy(place, True, 1).start()

    for place in range(own_slots):

        @pl.when(own_here(place))
        def _(place=place):
            fret_copy(place, False, 1).start()

    def add_early(which):
        for index, (tile, near) in enumerate(far_kinds):

            @pl.when(is_timed(tile, near, True))
            def _(index=index):
                fret_wait(index, which)
                for unit in range(UNITS):
                    picked = jnp.where(send_unit[index] == unit, send_used[index], 0)
                    spread = jnp.full((kb, width), picked, jnp.int32) > 0
                    total[which, unit * kb : (unit + 1) * kb, :] += jnp.where(
                        spread, fret_in[index, which].astype(F32), 0.0
                    )

    def add_late(which):
        late = [index for index, (_, near) in enumerate(far_kinds) if not near]
        for index in late:

            @pl.when(is_timed(*far_kinds[index], False))
            def _(index=index):
                fret_wait(index, which)

        pieces = []
        for unit in range(UNITS):
            acc = total[which, unit * kb : (unit + 1) * kb, :]
            for index in late:
                timed = is_timed(*far_kinds[index], False) & (send_unit[index] == unit)
                picked = jnp.where(timed, send_used[index], 0)
                spread = jnp.full((kb, width), picked, jnp.int32) > 0
                acc = acc + jnp.where(spread, fret_in[index, which].astype(F32), 0.0)
            pieces.append(acc)
        return jnp.concatenate(pieces, axis=0).astype(BF16)

    add_early(0)

    for side in sides:

        @pl.when(exists[side])
        def _(side=side):
            ret_wait(side)

    scale_rows = jnp.zeros((8, tokens), F32)
    for side in sides:
        for group in range(len(groups)):
            scale_rows = scale_rows + ret_scale_in[side, group]
    scales = to_columns(scale_rows)
    dq_groups = []
    for group, lanes in enumerate(groups):
        dq_sum = dq_acc[:, lanes]
        for side in sides:
            place = side * len(groups) + group
            coded = ret_in[side, :, lanes].astype(jnp.int32).astype(F32)
            dq_sum = dq_sum + coded * scales[:, place : place + 1]
        dq_groups.append(dq_sum)
    dq_sum = jnp.concatenate(dq_groups, axis=1)
    dq_norm = (dq_sum * score_scale).astype(BF16).astype(F32)
    query_wide = q_raw[...].astype(F32)
    weighted = gain_q * dq_norm
    x_start(1, lane_columns([(0, row_sums(weighted * query_wide))])[0:1])

    dk_norm = add_late(0).astype(F32)
    key_wide = k_raw[...].astype(F32)
    key_weighted = gain_k * dk_norm
    x_start(2, lane_columns([(0, row_sums(key_weighted * key_wide))])[0:1])

    q_factor = to_column(rates[0:1] * rates[0:1] * rates[0:1] * x_finish(1) / full_width)
    dq_out[0, 0] = (q_rate * weighted - query_wide * q_factor).astype(BF16)

    add_early(1)
    dv_out[0, 0] = add_late(1)
    for side in sides:

        @pl.when(exists[side])
        def _(side=side):
            for message in messages:
                nbr_copy(side, message).wait_send()
            for group in range(len(groups)):
                for which in range(2):
                    ret_copy(side, group, which).wait_send()

    for index, (tile, near) in enumerate(far_kinds):

        @pl.when(is_sent(tile, near))
        def _(index=index, tile=tile, near=near):
            far_copy(index, tile, near).wait_send()

    for place in range(near_slots):

        @pl.when(near_here(place))
        def _(place=place):
            for which in range(2):
                fret_copy(place, True, which).wait_send()

    for place in range(own_slots):

        @pl.when(own_here(place))
        def _(place=place):
            for which in range(2):
                fret_copy(place, False, which).wait_send()

    k_factor = to_column(rates[1:2] * rates[1:2] * rates[1:2] * x_finish(2) / full_width)
    dk_out[0, 0] = (k_rate * key_weighted - key_wide * k_factor).astype(BF16)


def copy_kernel(dq_in, dk_in, dv_in, dq_out, dk_out, dv_out, sem):
    pairs = ((dq_in, dq_out), (dk_in, dk_out), (dv_in, dv_out))
    copies = [
        pltpu.make_async_copy(source, target, sem.at[index])
        for index, (source, target) in enumerate(pairs)
    ]
    for copy in copies:
        copy.start()
    for copy in copies:
        copy.wait()


def body(sizes, q_raw, k_raw, values, upstream, outputs, logsumexp, gain_q, gain_k, far_list):
    rows, cols, parts = sizes
    tokens, width = q_raw.shape[2:]
    heads = logsumexp.shape[2]
    lse = logsumexp.transpose(0, 2, 1, 3)
    kb = tokens // UNITS
    stat_rows = -(-heads // 8) * 8
    sides = 2 + (1 if rows == 2 else 2 if rows > 2 else 0)
    near_slots = max((cols - 1) // 2, 1)
    own_slots = max(cols - 2, 1)
    kinds = max(2 * cols, 1)
    shape = jax.ShapeDtypeStruct(q_raw.shape, BF16)
    vmem = pl.BlockSpec(memory_space=pltpu.VMEM)
    anywhere = pl.BlockSpec(memory_space=pltpu.HBM)
    tile = pltpu.VMEM((tokens, width), BF16)
    near_units = pltpu.VMEM((near_slots, 2, kb, width), BF16)
    own_units = pltpu.VMEM((own_slots, 2, kb, width), BF16)
    dma = pltpu.SemaphoreType.DMA
    grads = pl.pallas_call(
        functools.partial(kernel, sizes),
        out_shape=(pltpu.VMEM(q_raw.shape, BF16),) * 3,
        in_specs=[anywhere] * 9,
        out_specs=(vmem,) * 3,
        scratch_shapes=[
            tile,
            tile,
            tile,
            tile,
            tile,
            tile,
            tile,
            pltpu.VMEM(lse.shape[1:], F32),
            pltpu.VMEM(gain_q.shape, BF16),
            pltpu.VMEM(gain_k.shape, BF16),
            pltpu.SMEM(far_list.shape, jnp.int32),
            pltpu.VMEM((2, stat_rows, tokens), F32),
            pltpu.VMEM((sides, 2, stat_rows, tokens), F32),
            pltpu.VMEM((tokens, width), F32),
            pltpu.VMEM((sides, tokens, width), BF16),
            pltpu.VMEM((sides, tokens, width), BF16),
            pltpu.VMEM((kinds, 2, kb, width), BF16),
            near_units,
            near_units,
            own_units,
            own_units,
            pltpu.VMEM((own_slots, 2, heads, kb, tokens), BF16),
            pltpu.VMEM((sides, tokens, width), F32),
            pltpu.VMEM((sides, tokens, width), jnp.int16),
            pltpu.VMEM((sides, tokens, width), jnp.int16),
            pltpu.VMEM((sides, 2, 8, tokens), F32),
            pltpu.VMEM((sides, 2, 8, tokens), F32),
            pltpu.VMEM((kinds, 2, kb, width), BF16),
            pltpu.VMEM((2, tokens, width), F32),
            pltpu.VMEM((3, parts, 8, 128), F32),
            dma((9,)),
            dma((sides, 2 + heads)),
            dma((sides, 2 + heads)),
            dma((kinds,)),
            dma((near_slots,)),
            dma((own_slots,)),
            dma((sides, 2, 2)),
            dma((sides, 2, 2)),
            dma((near_slots, 2)),
            dma((own_slots, 2)),
            dma((kinds, 2)),
            dma((3, parts)),
            dma((3, parts)),
        ],
        compiler_params=pltpu.CompilerParams(collective_id=0, has_side_effects=True),
    )(q_raw, k_raw, values, upstream, outputs, lse, gain_q, gain_k, far_list)
    return pl.pallas_call(
        copy_kernel,
        out_shape=(shape, shape, shape),
        in_specs=[vmem] * 3,
        out_specs=(anywhere,) * 3,
        scratch_shapes=[dma((3,))],
        compiler_params=pltpu.CompilerParams(vmem_limit_bytes=4 << 20),
    )(*grads)


def solution(mesh):
    sizes = (mesh.shape["ha"], mesh.shape["wa"], mesh.shape["hd"])
    tile = P("ha", "wa", None, "hd")
    return jax.shard_map(
        functools.partial(body, sizes),
        mesh=mesh,
        in_specs=(tile,) * 5 + (P("ha", "wa", "hd", None), P("hd"), P("hd"), P("ha", None, None)),
        out_specs=(tile,) * 3,
        check_vma=False,
    )
```

```python
import functools
import math

import jax
import jax.numpy as jnp
from jax import lax
from jax.experimental import pallas as pl
from jax.experimental.pallas import tpu as pltpu
from jax.sharding import PartitionSpec as P

UNITS = 4
EPS = 1e-06
MESH = pl.DeviceIdType.MESH
LAST = (((1,), (1,)), ((), ()))
FIRST = (((0,), (0,)), ((), ()))
PLAIN = (((1,), (0,)), ((), ()))
LEFT, RIGHT = 0, 1
CODE_MAX = 32767.0
F32 = jnp.float32
BF16 = jnp.bfloat16


def dot(a, b, dims):
    return lax.dot_general(a, b, dims, preferred_element_type=F32)


def kernel(
    sizes,
    q_hbm,
    k_hbm,
    v_hbm,
    u_hbm,
    o_hbm,
    lse_hbm,
    gain_q_hbm,
    gain_k_hbm,
    far_hbm,
    dq_out,
    dk_out,
    dv_out,
    q_raw,
    k_raw,
    vals,
    ups,
    outs,
    qn,
    kn,
    lse_ref,
    gain_q_ref,
    gain_k_ref,
    far_ref,
    stats,
    nbr_stats,
    dq_acc,
    nbr_q,
    nbr_u,
    far_pack,
    near_in,
    near_out,
    own_in,
    own_out,
    own_work,
    ret_acc,
    ret_out,
    ret_in,
    ret_scale,
    ret_scale_in,
    fret_in,
    total,
    xbuf,
    load_sem,
    nbr_send,
    nbr_recv,
    far_send,
    near_recv,
    own_recv,
    ret_send,
    ret_recv,
    near_send,
    own_send,
    fret_recv,
    x_send,
    x_recv,
):
    rows, cols, parts = sizes
    row = lax.axis_index("ha")
    col = lax.axis_index("wa")
    me = lax.axis_index("hd")
    tokens, width = q_raw.shape
    heads = lse_hbm.shape[1]
    hw = width // heads
    kb = tokens // UNITS
    full_width = width * parts
    slots = far_ref.shape[2]
    near_slots = near_in.shape[0]
    own_slots = own_in.shape[0]
    score_scale = 1.0 / math.sqrt(hw)
    head_lanes = [slice(head * hw, (head + 1) * hw) for head in range(heads)]
    split = (heads + 1) // 2
    groups = [slice(0, split * hw), slice(split * hw, width)] if heads > 1 else [slice(0, width)]

    barrier = pltpu.get_barrier_semaphore()
    hd_ids = [{"hd": lax.rem(me + off, parts)} for off in range(1, parts)]
    for target in hd_ids:
        pl.semaphore_signal(barrier, inc=1, device_id=target, device_id_type=MESH)

    exists = [col > 0, col < cols - 1]
    ids = [{"wa": col - 1}, {"wa": col + 1}]
    facing = [RIGHT, LEFT]
    if rows == 2:
        exists.append(True)
        ids.append({"ha": 1 - row})
        facing.append(2)
        pl.semaphore_signal(barrier, inc=1, device_id=ids[2], device_id_type=MESH)
    elif rows > 2:
        exists += [row > 0, row < rows - 1]
        ids += [{"ha": row - 1}, {"ha": row + 1}]
        facing += [3, 2]
        for side in (2, 3):

            @pl.when(exists[side])
            def _(side=side):
                pl.semaphore_signal(barrier, inc=1, device_id=ids[side], device_id_type=MESH)

    sides = range(len(ids))
    upright = range(2, len(ids))
    for off in range(1, cols):
        pl.semaphore_signal(
            barrier, inc=1, device_id={"wa": lax.rem(col + off, cols)}, device_id_type=MESH
        )

    loads = []
    for index, (source, target) in enumerate(
        (
            (u_hbm.at[0, 0], ups),
            (k_hbm.at[0, 0], k_raw),
            (q_hbm.at[0, 0], q_raw),
            (o_hbm.at[0, 0], outs),
            (v_hbm.at[0, 0], vals),
            (lse_hbm.at[0], lse_ref),
            (gain_q_hbm, gain_q_ref),
            (gain_k_hbm, gain_k_ref),
            (far_hbm, far_ref),
        )
    ):
        copy = pltpu.make_async_copy(source, target, load_sem.at[index])
        copy.start()
        loads.append(copy)

    inner = (col > 0) & (col < cols - 1)

    def lane_columns(columns):
        lane = lax.broadcasted_iota(jnp.int32, (tokens, 128), 1)
        mat = jnp.zeros((tokens, 128), F32)
        for place, column in columns:
            mat = jnp.where(lane == place, column, mat)
        return mat.T

    def row_sums(block):
        acc = block[:, :hw]
        for lanes in head_lanes[1:]:
            acc = acc + block[:, lanes]
        return jnp.sum(acc, axis=1, keepdims=True)

    def to_columns(rows8):
        return jnp.concatenate([rows8] * (tokens // rows8.shape[0]), axis=0).T

    def to_column(row1):
        return jnp.broadcast_to(row1, (128, tokens)).T[:, 0:1]

    def x_copy(which, off):
        return pltpu.make_async_remote_copy(
            src_ref=xbuf.at[which, me, pl.ds(0, x_rows[which])],
            dst_ref=xbuf.at[which, me, pl.ds(0, x_rows[which])],
            send_sem=x_send.at[which, off],
            recv_sem=x_recv.at[which, off],
            device_id=hd_ids[off - 1],
            device_id_type=MESH,
        )

    x_rows = (2, 1, 1)

    def x_start(which, sums):
        xbuf[which, me, 0 : x_rows[which]] = sums
        for off in range(1, parts):
            x_copy(which, off).start()

    def x_finish(which):
        for off in range(1, parts):
            x_copy(which, off).wait()
        acc = xbuf[which, 0, 0 : x_rows[which]]
        for part in range(1, parts):
            acc = acc + xbuf[which, part, 0 : x_rows[which]]
        return acc

    def side_id(side):
        if isinstance(side, int):
            return ids[side]
        return {"wa": jnp.where(side == RIGHT, col + 1, col - 1)}

    def face(side):
        return facing[side] if isinstance(side, int) else 1 - side

    def nbr_refs(side, message):
        if message == 0:
            return ups, nbr_u.at[side]
        if message == 1:
            return stats, nbr_stats.at[side]
        lanes = head_lanes[message - 2]
        return qn.at[:, lanes], nbr_q.at[side, :, lanes]

    messages = range(2 + heads)

    def nbr_copy(side, message):
        return pltpu.make_async_remote_copy(
            src_ref=nbr_refs(side, message)[0],
            dst_ref=nbr_refs(face(side), message)[1],
            send_sem=nbr_send.at[side, message],
            recv_sem=nbr_recv.at[face(side), message],
            device_id=ids[side],
            device_id_type=MESH,
        )

    def nbr_wait(side, message):
        pltpu.make_async_remote_copy(
            src_ref=nbr_refs(side, message)[0],
            dst_ref=nbr_refs(side, message)[1],
            send_sem=nbr_send.at[side, message],
            recv_sem=nbr_recv.at[side, message],
            device_id=ids[side],
            device_id_type=MESH,
        ).wait_recv()

    def nearer_left(tile):
        return 2 * tile < cols - 1

    from_left = nearer_left(col)
    behind = jnp.where(from_left, col, cols - 1 - col)
    first = jnp.where(from_left, RIGHT, LEFT)
    second = 1 - first
    has_first = jnp.where(from_left, col < cols - 1, col > 0)
    has_second = jnp.where(from_left, col > 0, col < cols - 1)

    def keeps_right(tile):
        return 2 * (tile + 1) < cols - 1

    def keeps_left(tile):
        return 2 * (tile - 1) > cols - 2

    has_own = keeps_right(col) | keeps_left(col)
    near_tiles = range(1, cols - 1)
    own_tiles = [tile for tile in range(cols) if keeps_right(tile) or keeps_left(tile)]

    def far_copy(index, tile, near):
        rank = col if nearer_left(tile) else cols - 1 - col
        landing, recv = (near_in, near_recv) if near else (own_in, own_recv)
        place = rank if near else rank - 2
        return pltpu.make_async_remote_copy(
            src_ref=far_pack.at[index],
            dst_ref=landing.at[place],
            send_sem=far_send.at[index],
            recv_sem=recv.at[place],
            device_id={"wa": tile},
            device_id_type=MESH,
        )

    def is_near(tile):
        return col < tile if nearer_left(tile) else col > tile

    def is_own(tile):
        return col > tile + 1 if keeps_right(tile) else col < tile - 1

    far_kinds = [(tile, True) for tile in near_tiles] + [(tile, False) for tile in own_tiles]

    def is_sent(tile, near):
        return is_near(tile) if near else is_own(tile)

    def near_here(place):
        return inner & (place < behind)

    def own_here(place):
        return has_own & (place >= behind)

    def ranked(rank):
        return jnp.where(from_left, rank, cols - 1 - rank)

    def far_wait(place, near):
        landing, recv = (near_in, near_recv) if near else (own_in, own_recv)
        pltpu.make_async_remote_copy(
            src_ref=far_pack.at[0],
            dst_ref=landing.at[place],
            send_sem=far_send.at[0],
            recv_sem=recv.at[place],
            device_id={"wa": ranked(place if near else place + 2)},
            device_id_type=MESH,
        ).wait_recv()

    def slot_of(near):
        if near:
            return col - 1
        after = col - cols + len(own_tiles)
        return len(near_tiles) + jnp.where(from_left, col, after)

    def fret_copy(place, near, which):
        source, send = (near_out, near_send) if near else (own_out, own_send)
        return pltpu.make_async_remote_copy(
            src_ref=source.at[place, which],
            dst_ref=fret_in.at[slot_of(near), which],
            send_sem=send.at[place, which],
            recv_sem=fret_recv.at[slot_of(near), which],
            device_id={"wa": ranked(place if near else place + 2)},
            device_id_type=MESH,
        )

    def fret_wait(index, which):
        pltpu.make_async_remote_copy(
            src_ref=fret_in.at[index, which],
            dst_ref=fret_in.at[index, which],
            send_sem=near_send.at[0, which],
            recv_sem=fret_recv.at[index, which],
            device_id={"wa": far_kinds[index][0]},
            device_id_type=MESH,
        ).wait_recv()

    def ret_refs(side, group, which):
        if which == 0:
            return ret_out.at[side, :, groups[group]], ret_in.at[side, :, groups[group]]
        return ret_scale.at[side, group], ret_scale_in.at[side, group]

    def ret_copy(side, group, which):
        return pltpu.make_async_remote_copy(
            src_ref=ret_refs(side, group, which)[0],
            dst_ref=ret_refs(face(side), group, which)[1],
            send_sem=ret_send.at[side, group, which],
            recv_sem=ret_recv.at[face(side), group, which],
            device_id=side_id(side),
            device_id_type=MESH,
        )

    def ret_start(side, group):
        part = ret_acc[side, :, groups[group]]
        largest = jnp.abs(part[:, :hw])
        for start in range(hw, part.shape[1], hw):
            largest = jnp.maximum(largest, jnp.abs(part[:, start : start + hw]))
        largest = jnp.maximum(jnp.max(largest, axis=1, keepdims=True), 1e-30)
        coded = jnp.round(part * (CODE_MAX / largest))
        ret_out[side, :, groups[group]] = coded.astype(jnp.int32).astype(jnp.int16)
        ret_copy(side, group, 0).start()
        place = face(side) * len(groups) + group
        ret_scale[side, group] = lane_columns([(place, largest / CODE_MAX)])[0:8]
        ret_copy(side, group, 1).start()

    def ret_wait(side):
        for group in range(len(groups)):
            for which in range(2):
                pltpu.make_async_remote_copy(
                    src_ref=ret_refs(side, group, which)[0],
                    dst_ref=ret_refs(side, group, which)[1],
                    send_sem=ret_send.at[side, group, which],
                    recv_sem=ret_recv.at[side, group, which],
                    device_id=ids[side],
                    device_id_type=MESH,
                ).wait_recv()

    def ret_start_all(group):
        @pl.when(has_first)
        def _():
            ret_start(first, group)

        @pl.when(has_second)
        def _():
            ret_start(second, group)

        for side in upright:

            @pl.when(exists[side])
            def _(side=side):
                ret_start(side, group)

    greeted = parts - 1 + cols - 1
    if rows == 2:
        greeted = greeted + 1
    elif rows > 2:
        greeted = greeted + jnp.minimum(row, 1) + jnp.minimum(rows - 1 - row, 1)
    loads[0].wait()
    pl.semaphore_wait(barrier, greeted)
    for side in sides:

        @pl.when(exists[side])
        def _(side=side):
            nbr_copy(side, 0).start()

    loads[1].wait()
    key_wide = k_raw[...].astype(F32)
    key_squares = row_sums(key_wide * key_wide)
    loads[2].wait()
    query_wide = q_raw[...].astype(F32)
    query_squares = row_sums(query_wide * query_wide)
    x_start(0, lane_columns([(0, query_squares), (1, key_squares)])[0:2])

    loads[3].wait()
    loads[5].wait()
    delta_columns = []
    for head, lanes in enumerate(head_lanes):
        product = ups[:, lanes].astype(F32) * outs[:, lanes].astype(F32)
        delta_columns.append((head, jnp.sum(product, axis=1, keepdims=True)))
    stats[0] = lane_columns(delta_columns)[0 : stats.shape[1]]
    for head in range(heads):
        stats[1, head : head + 1, :] = lse_ref[head]
    for side in sides:

        @pl.when(exists[side])
        def _(side=side):
            nbr_copy(side, 1).start()

        @pl.when(jnp.logical_not(exists[side]))
        def _(side=side):
            nbr_u[side] = jnp.zeros(nbr_u.shape[1:], BF16)
            nbr_q[side] = jnp.zeros(nbr_q.shape[1:], BF16)
            nbr_stats[side] = jnp.zeros(nbr_stats.shape[1:], F32)
            ret_in[side] = jnp.zeros(ret_in.shape[1:], jnp.int16)
            ret_scale_in[side] = jnp.zeros(ret_scale_in.shape[1:], F32)

    for place in range(near_slots):

        @pl.when(jnp.logical_not(near_here(place)))
        def _(place=place):
            near_in[place] = jnp.zeros(near_in.shape[1:], BF16)

    for place in range(own_slots):

        @pl.when(jnp.logical_not(own_here(place)))
        def _(place=place):
            own_in[place] = jnp.zeros(own_in.shape[1:], BF16)

    loads[8].wait()
    send_unit = []
    send_used = []
    for tile, near in far_kinds:
        query_col = tile if not near else tile + 1 if nearer_left(tile) else tile - 1
        unit = jnp.int32(0)
        asked = jnp.int32(0)
        for slot in range(slots):
            wanted = far_ref[0, query_col, slot] - col * UNITS
            hit = (wanted >= 0) & (wanted < UNITS)
            unit = jnp.where(hit, wanted, unit)
            asked = jnp.where(hit, 1, asked)
        send_unit.append(unit)
        send_used.append(jnp.where(is_sent(tile, near), asked, 0))

    def place_used(place, near):
        peer = ranked(place if near else place + 2)
        query_col = col
        if near:
            query_col = jnp.clip(jnp.where(from_left, col + 1, col - 1), 0, cols - 1)
        used = jnp.int32(0)
        for slot in range(slots):
            named = far_ref[0, query_col, slot] - peer * UNITS
            used = jnp.where((named >= 0) & (named < UNITS), 1, used)
        return jnp.where(near_here(place) if near else own_here(place), used, 0)

    near_used = [place_used(place, True) for place in range(near_slots)]
    own_used = [place_used(place, False) for place in range(own_slots)]

    def pick_unit(unit_wanted, source):
        wanted = jnp.full((kb, width), unit_wanted, jnp.int32)
        picked = source[0:kb, :].astype(F32)
        for unit in range(1, UNITS):
            block = source[unit * kb : (unit + 1) * kb, :].astype(F32)
            picked = jnp.where(wanted == unit, block, picked)
        return picked.astype(BF16)

    loads[4].wait()
    for index in range(len(far_kinds)):
        far_pack[index, 1] = pick_unit(send_unit[index], vals)

    loads[6].wait()
    loads[7].wait()
    gain_q = gain_q_ref[...].astype(F32).reshape(1, width)
    gain_k = gain_k_ref[...].astype(F32).reshape(1, width)
    rates = lax.rsqrt(x_finish(0) / full_width + EPS)
    rate_columns = to_columns(rates)
    q_rate = rate_columns[:, 0:1]
    k_rate = rate_columns[:, 1:2]
    kn[...] = (k_raw[...].astype(F32) * k_rate * gain_k).astype(BF16)

    def is_timed(tile, near, early):
        if near:
            return is_sent(tile, near) if early else False
        gap = (col - tile) * (col - tile)
        return is_sent(tile, near) & (gap == 4 if early else gap > 4)

    def far_start(early):
        for index, (tile, near) in enumerate(far_kinds):
            @pl.when(is_timed(tile, near, early))
            def _(index=index, tile=tile, near=near):
                far_pack[index, 0] = pick_unit(send_unit[index], kn)
                far_copy(index, tile, near).start()

    far_start(True)
    qn[...] = (q_raw[...].astype(F32) * q_rate * gain_q).astype(BF16)
    for side in sides:

        @pl.when(exists[side])
        def _(side=side):
            for head in range(split):
                nbr_copy(side, 2 + head).start()

    far_start(False)
    for side in sides:

        @pl.when(exists[side])
        def _(side=side):
            for head in range(split, heads):
                nbr_copy(side, 2 + head).start()

    def attend(keys, values, queries, upstream, delta_row, lse_row, used=None):
        weight = jnp.exp(dot(keys, queries, LAST) * score_scale - lse_row)
        if used is not None:
            weight = jnp.where(used, weight, 0.0)
        dweight = dot(values, upstream, LAST)
        dscore = (weight * (dweight - delta_row)).astype(BF16)
        weight_low = weight.astype(BF16)
        dq_part = dot(dscore, keys, FIRST)
        dk_parts, dv_parts = [], []
        for start in range(0, queries.shape[0], tokens):
            block = slice(start, start + tokens)
            dk_part = dot(dscore[:, block], queries[block], PLAIN) * score_scale
            dk_parts.append(dk_part.astype(BF16))
            dv_parts.append(dot(weight_low[:, block], upstream[block], PLAIN).astype(BF16))
        return dq_part, dk_parts, dv_parts

    for head, lanes in enumerate(head_lanes):
        dq_part, (dk_part,), (dv_part,) = attend(
            kn[:, lanes],
            vals[:, lanes],
            qn[:, lanes],
            ups[:, lanes],
            stats[0, head : head + 1, :],
            stats[1, head : head + 1, :],
        )
        dq_acc[:, lanes] = dq_part
        total[0, :, lanes] = dk_part.astype(F32)
        total[1, :, lanes] = dv_part.astype(F32)

    def own_scores(place):
        far_wait(place, False)
        used = jnp.full((kb, tokens), own_used[place], jnp.int32) > 0
        for head, lanes in enumerate(head_lanes):
            scores = dot(own_in[place, 0, :, lanes], qn[:, lanes], LAST) * score_scale
            weight = jnp.where(used, jnp.exp(scores - stats[1, head : head + 1, :]), 0.0)
            dweight = dot(own_in[place, 1, :, lanes], ups[:, lanes], LAST)
            dscore = (weight * (dweight - stats[0, head : head + 1, :])).astype(BF16)
            own_work[place, 0, head] = dscore
            own_work[place, 1, head] = weight.astype(BF16)
            own_out[place, 0, :, lanes] = (dot(dscore, qn[:, lanes], PLAIN) * score_scale).astype(BF16)
        fret_copy(place, False, 0).start()

    def own_rest(place):
        for head, lanes in enumerate(head_lanes):
            own_out[place, 1, :, lanes] = dot(own_work[place, 1, head], ups[:, lanes], PLAIN).astype(BF16)
            dq_acc[:, lanes] += dot(own_work[place, 0, head], own_in[place, 0, :, lanes], FIRST)

    def own_each(step, places):
        for place in places:

            @pl.when(own_here(place))
            def _(place=place):
                step(place)

    early_places, late_places = range(own_slots)[:1], range(own_slots)[1:]

    def stat_row(which, head):
        return jnp.concatenate([nbr_stats[side, which, head : head + 1, :] for side in sides], axis=1)

    own_each(own_scores, early_places)
    own_each(own_rest, early_places)
    for place in range(near_slots):

        @pl.when(near_here(place))
        def _(place=place):
            far_wait(place, True)

    near_rows = [
        jnp.concatenate(
            [jnp.full((kb, tokens), jnp.where(first == side, flag, 0), jnp.int32) for side in sides],
            axis=1,
        )
        for flag in near_used
    ]
    all_rows = jnp.ones((tokens, len(sides) * tokens), jnp.int32)
    side_mask = jnp.concatenate([all_rows] + near_rows, axis=0) > 0

    def with_near(own, which, lanes):
        near = near_in[:, which, :, lanes].reshape(near_slots * kb, hw)
        return jnp.concatenate([own[:, lanes], near], axis=0)

    for head, lanes in enumerate(head_lanes):
        for side in sides:

            @pl.when(exists[side])
            def _(side=side, head=head):
                for message in (0, 1, 2) if head == 0 else (2 + head,):
                    nbr_wait(side, message)

        dq_part, dk_parts, dv_parts = attend(
            with_near(kn, 0, lanes),
            with_near(vals, 1, lanes),
            nbr_q[:, :, lanes].reshape(len(sides) * tokens, hw),
            nbr_u[:, :, lanes].reshape(len(sides) * tokens, hw),
            stat_row(0, head),
            stat_row(1, head),
            side_mask,
        )
        ret_acc[:, :, lanes] = dq_part.reshape(len(sides), tokens, hw)
        for which, terms in enumerate((dk_parts, dv_parts)):
            acc = total[which, :, lanes]
            for term in terms:
                acc = acc + term[:tokens].astype(F32)
            total[which, :, lanes] = acc
            far_acc = terms[0][tokens:].astype(F32)
            for term in terms[1:]:
                far_acc = far_acc + term[tokens:].astype(F32)
            near_out[:, which, :, lanes] = far_acc.astype(BF16).reshape(near_slots, kb, hw)
        if head + 1 in (split, heads):
            ret_start_all(head // split)

    for place in range(near_slots):

        @pl.when(near_here(place))
        def _(place=place):
            fret_copy(place, True, 0).start()

    own_each(own_scores, late_places)
    own_each(own_rest, late_places)
    for place in range(near_slots):

        @pl.when(near_here(place))
        def _(place=place):
            fret_copy(place, True, 1).start()

    for place in range(own_slots):

        @pl.when(own_here(place))
        def _(place=place):
            fret_copy(place, False, 1).start()

    def add_early(which):
        for index, (tile, near) in enumerate(far_kinds):

            @pl.when(is_timed(tile, near, True))
            def _(index=index):
                fret_wait(index, which)
                for unit in range(UNITS):
                    picked = jnp.where(send_unit[index] == unit, send_used[index], 0)
                    spread = jnp.full((kb, width), picked, jnp.int32) > 0
                    total[which, unit * kb : (unit + 1) * kb, :] += jnp.where(
                        spread, fret_in[index, which].astype(F32), 0.0
                    )

    def add_late(which):
        late = [index for index, (_, near) in enumerate(far_kinds) if not near]
        for index in late:

            @pl.when(is_timed(*far_kinds[index], False))
            def _(index=index):
                fret_wait(index, which)

        pieces = []
        for unit in range(UNITS):
            acc = total[which, unit * kb : (unit + 1) * kb, :]
            for index in late:
                timed = is_timed(*far_kinds[index], False) & (send_unit[index] == unit)
                picked = jnp.where(timed, send_used[index], 0)
                spread = jnp.full((kb, width), picked, jnp.int32) > 0
                acc = acc + jnp.where(spread, fret_in[index, which].astype(F32), 0.0)
            pieces.append(acc)
        return jnp.concatenate(pieces, axis=0).astype(BF16)

    add_early(0)

    for side in sides:

        @pl.when(exists[side])
        def _(side=side):
            ret_wait(side)

    scale_rows = jnp.zeros((8, tokens), F32)
    for side in sides:
        for group in range(len(groups)):
            scale_rows = scale_rows + ret_scale_in[side, group]
    scales = to_columns(scale_rows)
    dq_groups = []
    for group, lanes in enumerate(groups):
        dq_sum = dq_acc[:, lanes]
        for side in sides:
            place = side * len(groups) + group
            coded = ret_in[side, :, lanes].astype(jnp.int32).astype(F32)
            dq_sum = dq_sum + coded * scales[:, place : place + 1]
        dq_groups.append(dq_sum)
    dq_sum = jnp.concatenate(dq_groups, axis=1)
    dq_norm = (dq_sum * score_scale).astype(BF16).astype(F32)
    query_wide = q_raw[...].astype(F32)
    weighted = gain_q * dq_norm
    x_start(1, lane_columns([(0, row_sums(weighted * query_wide))])[0:1])

    dk_norm = add_late(0).astype(F32)
    key_wide = k_raw[...].astype(F32)
    key_weighted = gain_k * dk_norm
    x_start(2, lane_columns([(0, row_sums(key_weighted * key_wide))])[0:1])

    q_factor = to_column(rates[0:1] * rates[0:1] * rates[0:1] * x_finish(1) / full_width)
    dq_out[0, 0] = (q_rate * weighted - query_wide * q_factor).astype(BF16)

    add_early(1)
    dv_out[0, 0] = add_late(1)
    for side in sides:

        @pl.when(exists[side])
        def _(side=side):
            for message in messages:
                nbr_copy(side, message).wait_send()
            for group in range(len(groups)):
                for which in range(2):
                    ret_copy(side, group, which).wait_send()

    for index, (tile, near) in enumerate(far_kinds):

        @pl.when(is_sent(tile, near))
        def _(index=index, tile=tile, near=near):
            far_copy(index, tile, near).wait_send()

    for place in range(near_slots):

        @pl.when(near_here(place))
        def _(place=place):
            for which in range(2):
                fret_copy(place, True, which).wait_send()

    for place in range(own_slots):

        @pl.when(own_here(place))
        def _(place=place):
            for which in range(2):
                fret_copy(place, False, which).wait_send()

    k_factor = to_column(rates[1:2] * rates[1:2] * rates[1:2] * x_finish(2) / full_width)
    dk_out[0, 0] = (k_rate * key_weighted - key_wide * k_factor).astype(BF16)


def copy_kernel(dq_in, dk_in, dv_in, dq_out, dk_out, dv_out, sem):
    pairs = ((dq_in, dq_out), (dk_in, dk_out), (dv_in, dv_out))
    copies = [
        pltpu.make_async_copy(source, target, sem.at[index])
        for index, (source, target) in enumerate(pairs)
    ]
    for copy in copies:
        copy.start()
    for copy in copies:
        copy.wait()


def body(sizes, q_raw, k_raw, values, upstream, outputs, logsumexp, gain_q, gain_k, far_list):
    rows, cols, parts = sizes
    tokens, width = q_raw.shape[2:]
    heads = logsumexp.shape[2]
    lse = logsumexp.transpose(0, 2, 1, 3)
    kb = tokens // UNITS
    stat_rows = -(-heads // 8) * 8
    sides = 2 + (1 if rows == 2 else 2 if rows > 2 else 0)
    near_slots = max((cols - 1) // 2, 1)
    own_slots = max(cols - 2, 1)
    kinds = max(2 * cols, 1)
    shape = jax.ShapeDtypeStruct(q_raw.shape, BF16)
    vmem = pl.BlockSpec(memory_space=pltpu.VMEM)
    anywhere = pl.BlockSpec(memory_space=pltpu.HBM)
    tile = pltpu.VMEM((tokens, width), BF16)
    near_units = pltpu.VMEM((near_slots, 2, kb, width), BF16)
    own_units = pltpu.VMEM((own_slots, 2, kb, width), BF16)
    dma = pltpu.SemaphoreType.DMA
    grads = pl.pallas_call(
        functools.partial(kernel, sizes),
        out_shape=(pltpu.VMEM(q_raw.shape, BF16),) * 3,
        in_specs=[anywhere] * 9,
        out_specs=(vmem,) * 3,
        scratch_shapes=[
            tile,
            tile,
            tile,
            tile,
            tile,
            tile,
            tile,
            pltpu.VMEM(lse.shape[1:], F32),
            pltpu.VMEM(gain_q.shape, BF16),
            pltpu.VMEM(gain_k.shape, BF16),
            pltpu.SMEM(far_list.shape, jnp.int32),
            pltpu.VMEM((2, stat_rows, tokens), F32),
            pltpu.VMEM((sides, 2, stat_rows, tokens), F32),
            pltpu.VMEM((tokens, width), F32),
            pltpu.VMEM((sides, tokens, width), BF16),
            pltpu.VMEM((sides, tokens, width), BF16),
            pltpu.VMEM((kinds, 2, kb, width), BF16),
            near_units,
            near_units,
            own_units,
            own_units,
            pltpu.VMEM((own_slots, 2, heads, kb, tokens), BF16),
            pltpu.VMEM((sides, tokens, width), F32),
            pltpu.VMEM((sides, tokens, width), jnp.int16),
            pltpu.VMEM((sides, tokens, width), jnp.int16),
            pltpu.VMEM((sides, 2, 8, tokens), F32),
            pltpu.VMEM((sides, 2, 8, tokens), F32),
            pltpu.VMEM((kinds, 2, kb, width), BF16),
            pltpu.VMEM((2, tokens, width), F32),
            pltpu.VMEM((3, parts, 8, 128), F32),
            dma((9,)),
            dma((sides, 2 + heads)),
            dma((sides, 2 + heads)),
            dma((kinds,)),
            dma((near_slots,)),
            dma((own_slots,)),
            dma((sides, 2, 2)),
            dma((sides, 2, 2)),
            dma((near_slots, 2)),
            dma((own_slots, 2)),
            dma((kinds, 2)),
            dma((3, parts)),
            dma((3, parts)),
        ],
        compiler_params=pltpu.CompilerParams(collective_id=0, has_side_effects=True),
    )(q_raw, k_raw, values, upstream, outputs, lse, gain_q, gain_k, far_list)
    return pl.pallas_call(
        copy_kernel,
        out_shape=(shape, shape, shape),
        in_specs=[vmem] * 3,
        out_specs=(anywhere,) * 3,
        scratch_shapes=[dma((3,))],
        compiler_params=pltpu.CompilerParams(vmem_limit_bytes=4 << 20),
    )(*grads)


def solution(mesh):
    sizes = (mesh.shape["ha"], mesh.shape["wa"], mesh.shape["hd"])
    tile = P("ha", "wa", None, "hd")
    return jax.shard_map(
        functools.partial(body, sizes),
        mesh=mesh,
        in_specs=(tile,) * 5 + (P("ha", "wa", "hd", None), P("hd"), P("hd"), P("ha", None, None)),
        out_specs=(tile,) * 3,
        check_vma=False,
    )
```

```python
import functools
import math

import jax
import jax.numpy as jnp
from jax import lax
from jax.experimental import pallas as pl
from jax.experimental.pallas import tpu as pltpu
from jax.sharding import PartitionSpec as P

UNITS = 4
EPS = 1e-06
MESH = pl.DeviceIdType.MESH
LAST = (((1,), (1,)), ((), ()))
FIRST = (((0,), (0,)), ((), ()))
PLAIN = (((1,), (0,)), ((), ()))
LEFT, RIGHT = 0, 1
CODE_MAX = 32767.0
F32 = jnp.float32
BF16 = jnp.bfloat16


def dot(a, b, dims):
    return lax.dot_general(a, b, dims, preferred_element_type=F32)


def kernel(
    sizes,
    q_hbm,
    k_hbm,
    v_hbm,
    u_hbm,
    o_hbm,
    lse_hbm,
    gain_q_hbm,
    gain_k_hbm,
    far_hbm,
    dq_out,
    dk_out,
    dv_out,
    q_raw,
    k_raw,
    vals,
    ups,
    outs,
    qn,
    kn,
    lse_ref,
    gain_q_ref,
    gain_k_ref,
    far_ref,
    stats,
    nbr_stats,
    dq_acc,
    nbr_q,
    nbr_u,
    far_pack,
    near_in,
    near_out,
    own_in,
    own_out,
    own_work,
    ret_acc,
    ret_out,
    ret_in,
    ret_scale,
    ret_scale_in,
    fret_in,
    total,
    xbuf,
    load_sem,
    nbr_send,
    nbr_recv,
    far_send,
    near_recv,
    own_recv,
    ret_send,
    ret_recv,
    near_send,
    own_send,
    fret_recv,
    x_send,
    x_recv,
):
    rows, cols, parts = sizes
    row = lax.axis_index("ha")
    col = lax.axis_index("wa")
    me = lax.axis_index("hd")
    tokens, width = q_raw.shape
    heads = lse_hbm.shape[1]
    hw = width // heads
    kb = tokens // UNITS
    full_width = width * parts
    slots = far_ref.shape[2]
    near_slots = near_in.shape[0]
    own_slots = own_in.shape[0]
    score_scale = 1.0 / math.sqrt(hw)
    head_lanes = [slice(head * hw, (head + 1) * hw) for head in range(heads)]
    split = (heads + 1) // 2
    groups = [slice(0, split * hw), slice(split * hw, width)] if heads > 1 else [slice(0, width)]

    barrier = pltpu.get_barrier_semaphore()
    hd_ids = [{"hd": lax.rem(me + off, parts)} for off in range(1, parts)]
    for target in hd_ids:
        pl.semaphore_signal(barrier, inc=1, device_id=target, device_id_type=MESH)

    exists = [col > 0, col < cols - 1]
    ids = [{"wa": col - 1}, {"wa": col + 1}]
    facing = [RIGHT, LEFT]
    if rows == 2:
        exists.append(True)
        ids.append({"ha": 1 - row})
        facing.append(2)
        pl.semaphore_signal(barrier, inc=1, device_id=ids[2], device_id_type=MESH)
    elif rows > 2:
        exists += [row > 0, row < rows - 1]
        ids += [{"ha": row - 1}, {"ha": row + 1}]
        facing += [3, 2]
        for side in (2, 3):

            @pl.when(exists[side])
            def _(side=side):
                pl.semaphore_signal(barrier, inc=1, device_id=ids[side], device_id_type=MESH)

    sides = range(len(ids))
    upright = range(2, len(ids))
    for off in range(1, cols):
        pl.semaphore_signal(
            barrier, inc=1, device_id={"wa": lax.rem(col + off, cols)}, device_id_type=MESH
        )

    loads = []
    for index, (source, target) in enumerate(
        (
            (u_hbm.at[0, 0], ups),
            (k_hbm.at[0, 0], k_raw),
            (q_hbm.at[0, 0], q_raw),
            (o_hbm.at[0, 0], outs),
            (v_hbm.at[0, 0], vals),
            (lse_hbm.at[0], lse_ref),
            (gain_q_hbm, gain_q_ref),
            (gain_k_hbm, gain_k_ref),
            (far_hbm, far_ref),
        )
    ):
        copy = pltpu.make_async_copy(source, target, load_sem.at[index])
        copy.start()
        loads.append(copy)

    inner = (col > 0) & (col < cols - 1)

    def lane_columns(columns):
        lane = lax.broadcasted_iota(jnp.int32, (tokens, 128), 1)
        mat = jnp.zeros((tokens, 128), F32)
        for place, column in columns:
            mat = jnp.where(lane == place, column, mat)
        return mat.T

    def row_sums(block):
        acc = block[:, :hw]
        for lanes in head_lanes[1:]:
            acc = acc + block[:, lanes]
        return jnp.sum(acc, axis=1, keepdims=True)

    def to_columns(rows8):
        return jnp.concatenate([rows8] * (tokens // rows8.shape[0]), axis=0).T

    def to_column(row1):
        return jnp.broadcast_to(row1, (128, tokens)).T[:, 0:1]

    def x_copy(which, off):
        return pltpu.make_async_remote_copy(
            src_ref=xbuf.at[which, me, pl.ds(0, x_rows[which])],
            dst_ref=xbuf.at[which, me, pl.ds(0, x_rows[which])],
            send_sem=x_send.at[which, off],
            recv_sem=x_recv.at[which, off],
            device_id=hd_ids[off - 1],
            device_id_type=MESH,
        )

    x_rows = (2, 1, 1)

    def x_start(which, sums):
        xbuf[which, me, 0 : x_rows[which]] = sums
        for off in range(1, parts):
            x_copy(which, off).start()

    def x_finish(which):
        for off in range(1, parts):
            x_copy(which, off).wait()
        acc = xbuf[which, 0, 0 : x_rows[which]]
        for part in range(1, parts):
            acc = acc + xbuf[which, part, 0 : x_rows[which]]
        return acc

    def side_id(side):
        if isinstance(side, int):
            return ids[side]
        return {"wa": jnp.where(side == RIGHT, col + 1, col - 1)}

    def face(side):
        return facing[side] if isinstance(side, int) else 1 - side

    def nbr_refs(side, message):
        if message == 0:
            return ups, nbr_u.at[side]
        if message == 1:
            return stats, nbr_stats.at[side]
        lanes = head_lanes[message - 2]
        return qn.at[:, lanes], nbr_q.at[side, :, lanes]

    messages = range(2 + heads)

    def nbr_copy(side, message):
        return pltpu.make_async_remote_copy(
            src_ref=nbr_refs(side, message)[0],
            dst_ref=nbr_refs(face(side), message)[1],
            send_sem=nbr_send.at[side, message],
            recv_sem=nbr_recv.at[face(side), message],
            device_id=ids[side],
            device_id_type=MESH,
        )

    def nbr_wait(side, message):
        pltpu.make_async_remote_copy(
            src_ref=nbr_refs(side, message)[0],
            dst_ref=nbr_refs(side, message)[1],
            send_sem=nbr_send.at[side, message],
            recv_sem=nbr_recv.at[side, message],
            device_id=ids[side],
            device_id_type=MESH,
        ).wait_recv()

    def nearer_left(tile):
        return 2 * tile < cols - 1

    from_left = nearer_left(col)
    behind = jnp.where(from_left, col, cols - 1 - col)
    first = jnp.where(from_left, RIGHT, LEFT)
    second = 1 - first
    has_first = jnp.where(from_left, col < cols - 1, col > 0)
    has_second = jnp.where(from_left, col > 0, col < cols - 1)

    def keeps_right(tile):
        return 2 * (tile + 1) < cols - 1

    def keeps_left(tile):
        return 2 * (tile - 1) > cols - 2

    has_own = keeps_right(col) | keeps_left(col)
    near_tiles = range(1, cols - 1)
    own_tiles = [tile for tile in range(cols) if keeps_right(tile) or keeps_left(tile)]

    def far_copy(index, tile, near):
        rank = col if nearer_left(tile) else cols - 1 - col
        landing, recv = (near_in, near_recv) if near else (own_in, own_recv)
        place = rank if near else rank - 2
        return pltpu.make_async_remote_copy(
            src_ref=far_pack.at[index],
            dst_ref=landing.at[place],
            send_sem=far_send.at[index],
            recv_sem=recv.at[place],
            device_id={"wa": tile},
            device_id_type=MESH,
        )

    def is_near(tile):
        return col < tile if nearer_left(tile) else col > tile

    def is_own(tile):
        return col > tile + 1 if keeps_right(tile) else col < tile - 1

    far_kinds = [(tile, True) for tile in near_tiles] + [(tile, False) for tile in own_tiles]

    def is_sent(tile, near):
        return is_near(tile) if near else is_own(tile)

    def near_here(place):
        return inner & (place < behind)

    def own_here(place):
        return has_own & (place >= behind)

    def ranked(rank):
        return jnp.where(from_left, rank, cols - 1 - rank)

    def far_wait(place, near):
        landing, recv = (near_in, near_recv) if near else (own_in, own_recv)
        pltpu.make_async_remote_copy(
            src_ref=far_pack.at[0],
            dst_ref=landing.at[place],
            send_sem=far_send.at[0],
            recv_sem=recv.at[place],
            device_id={"wa": ranked(place if near else place + 2)},
            device_id_type=MESH,
        ).wait_recv()

    def slot_of(near):
        if near:
            return col - 1
        after = col - cols + len(own_tiles)
        return len(near_tiles) + jnp.where(from_left, col, after)

    def fret_copy(place, near, which):
        source, send = (near_out, near_send) if near else (own_out, own_send)
        return pltpu.make_async_remote_copy(
            src_ref=source.at[place, which],
            dst_ref=fret_in.at[slot_of(near), which],
            send_sem=send.at[place, which],
            recv_sem=fret_recv.at[slot_of(near), which],
            device_id={"wa": ranked(place if near else place + 2)},
            device_id_type=MESH,
        )

    def fret_wait(index, which):
        pltpu.make_async_remote_copy(
            src_ref=fret_in.at[index, which],
            dst_ref=fret_in.at[index, which],
            send_sem=near_send.at[0, which],
            recv_sem=fret_recv.at[index, which],
            device_id={"wa": far_kinds[index][0]},
            device_id_type=MESH,
        ).wait_recv()

    def ret_refs(side, group, which):
        if which == 0:
            return ret_out.at[side, :, groups[group]], ret_in.at[side, :, groups[group]]
        return ret_scale.at[side, group], ret_scale_in.at[side, group]

    def ret_copy(side, group, which):
        return pltpu.make_async_remote_copy(
            src_ref=ret_refs(side, group, which)[0],
            dst_ref=ret_refs(face(side), group, which)[1],
            send_sem=ret_send.at[side, group, which],
            recv_sem=ret_recv.at[face(side), group, which],
            device_id=side_id(side),
            device_id_type=MESH,
        )

    def ret_start(side, group):
        part = ret_acc[side, :, groups[group]]
        largest = jnp.abs(part[:, :hw])
        for start in range(hw, part.shape[1], hw):
            largest = jnp.maximum(largest, jnp.abs(part[:, start : start + hw]))
        largest = jnp.maximum(jnp.max(largest, axis=1, keepdims=True), 1e-30)
        coded = jnp.round(part * (CODE_MAX / largest))
        ret_out[side, :, groups[group]] = coded.astype(jnp.int32).astype(jnp.int16)
        ret_copy(side, group, 0).start()
        place = face(side) * len(groups) + group
        ret_scale[side, group] = lane_columns([(place, largest / CODE_MAX)])[0:8]
        ret_copy(side, group, 1).start()

    def ret_wait(side):
        for group in range(len(groups)):
            for which in range(2):
                pltpu.make_async_remote_copy(
                    src_ref=ret_refs(side, group, which)[0],
                    dst_ref=ret_refs(side, group, which)[1],
                    send_sem=ret_send.at[side, group, which],
                    recv_sem=ret_recv.at[side, group, which],
                    device_id=ids[side],
                    device_id_type=MESH,
                ).wait_recv()

    def ret_start_all(group):
        @pl.when(has_first)
        def _():
            ret_start(first, group)

        @pl.when(has_second)
        def _():
            ret_start(second, group)

        for side in upright:

            @pl.when(exists[side])
            def _(side=side):
                ret_start(side, group)

    greeted = parts - 1 + cols - 1
    if rows == 2:
        greeted = greeted + 1
    elif rows > 2:
        greeted = greeted + jnp.minimum(row, 1) + jnp.minimum(rows - 1 - row, 1)
    loads[0].wait()
    pl.semaphore_wait(barrier, greeted)
    for side in sides:

        @pl.when(exists[side])
        def _(side=side):
            nbr_copy(side, 0).start()

    loads[1].wait()
    key_wide = k_raw[...].astype(F32)
    key_squares = row_sums(key_wide * key_wide)
    loads[2].wait()
    query_wide = q_raw[...].astype(F32)
    query_squares = row_sums(query_wide * query_wide)
    x_start(0, lane_columns([(0, query_squares), (1, key_squares)])[0:2])

    loads[3].wait()
    loads[5].wait()
    delta_columns = []
    for head, lanes in enumerate(head_lanes):
        product = ups[:, lanes].astype(F32) * outs[:, lanes].astype(F32)
        delta_columns.append((head, jnp.sum(product, axis=1, keepdims=True)))
    stats[0] = lane_columns(delta_columns)[0 : stats.shape[1]]
    for head in range(heads):
        stats[1, head : head + 1, :] = lse_ref[head]
    for side in sides:

        @pl.when(exists[side])
        def _(side=side):
            nbr_copy(side, 1).start()

        @pl.when(jnp.logical_not(exists[side]))
        def _(side=side):
            nbr_u[side] = jnp.zeros(nbr_u.shape[1:], BF16)
            nbr_q[side] = jnp.zeros(nbr_q.shape[1:], BF16)
            nbr_stats[side] = jnp.zeros(nbr_stats.shape[1:], F32)
            ret_in[side] = jnp.zeros(ret_in.shape[1:], jnp.int16)
            ret_scale_in[side] = jnp.zeros(ret_scale_in.shape[1:], F32)

    for place in range(near_slots):

        @pl.when(jnp.logical_not(near_here(place)))
        def _(place=place):
            near_in[place] = jnp.zeros(near_in.shape[1:], BF16)

    for place in range(own_slots):

        @pl.when(jnp.logical_not(own_here(place)))
        def _(place=place):
            own_in[place] = jnp.zeros(own_in.shape[1:], BF16)

    loads[8].wait()
    send_unit = []
    send_used = []
    for tile, near in far_kinds:
        query_col = tile if not near else tile + 1 if nearer_left(tile) else tile - 1
        unit = jnp.int32(0)
        asked = jnp.int32(0)
        for slot in range(slots):
            wanted = far_ref[0, query_col, slot] - col * UNITS
            hit = (wanted >= 0) & (wanted < UNITS)
            unit = jnp.where(hit, wanted, unit)
            asked = jnp.where(hit, 1, asked)
        send_unit.append(unit)
        send_used.append(jnp.where(is_sent(tile, near), asked, 0))

    def place_used(place, near):
        peer = ranked(place if near else place + 2)
        query_col = col
        if near:
            query_col = jnp.clip(jnp.where(from_left, col + 1, col - 1), 0, cols - 1)
        used = jnp.int32(0)
        for slot in range(slots):
            named = far_ref[0, query_col, slot] - peer * UNITS
            used = jnp.where((named >= 0) & (named < UNITS), 1, used)
        return jnp.where(near_here(place) if near else own_here(place), used, 0)

    near_used = [place_used(place, True) for place in range(near_slots)]
    own_used = [place_used(place, False) for place in range(own_slots)]

    def pick_unit(unit_wanted, source):
        wanted = jnp.full((kb, width), unit_wanted, jnp.int32)
        picked = source[0:kb, :].astype(F32)
        for unit in range(1, UNITS):
            block = source[unit * kb : (unit + 1) * kb, :].astype(F32)
            picked = jnp.where(wanted == unit, block, picked)
        return picked.astype(BF16)

    loads[4].wait()
    for index in range(len(far_kinds)):
        far_pack[index, 1] = pick_unit(send_unit[index], vals)

    loads[6].wait()
    loads[7].wait()
    gain_q = gain_q_ref[...].astype(F32).reshape(1, width)
    gain_k = gain_k_ref[...].astype(F32).reshape(1, width)
    rates = lax.rsqrt(x_finish(0) / full_width + EPS)
    rate_columns = to_columns(rates)
    q_rate = rate_columns[:, 0:1]
    k_rate = rate_columns[:, 1:2]
    kn[...] = (k_raw[...].astype(F32) * k_rate * gain_k).astype(BF16)

    def is_timed(tile, near, early):
        if near:
            return is_sent(tile, near) if early else False
        gap = (col - tile) * (col - tile)
        return is_sent(tile, near) & (gap == 4 if early else gap > 4)

    def far_start(early):
        for index, (tile, near) in enumerate(far_kinds):
            @pl.when(is_timed(tile, near, early))
            def _(index=index, tile=tile, near=near):
                far_pack[index, 0] = pick_unit(send_unit[index], kn)
                far_copy(index, tile, near).start()

    far_start(True)
    qn[...] = (q_raw[...].astype(F32) * q_rate * gain_q).astype(BF16)
    for side in sides:

        @pl.when(exists[side])
        def _(side=side):
            for head in range(split):
                nbr_copy(side, 2 + head).start()

    far_start(False)
    for side in sides:

        @pl.when(exists[side])
        def _(side=side):
            for head in range(split, heads):
                nbr_copy(side, 2 + head).start()

    def attend(keys, values, queries, upstream, delta_row, lse_row, used=None):
        weight = jnp.exp(dot(keys, queries, LAST) * score_scale - lse_row)
        if used is not None:
            weight = jnp.where(used, weight, 0.0)
        dweight = dot(values, upstream, LAST)
        dscore = (weight * (dweight - delta_row)).astype(BF16)
        weight_low = weight.astype(BF16)
        dq_part = dot(dscore, keys, FIRST)
        dk_parts, dv_parts = [], []
        for start in range(0, queries.shape[0], tokens):
            block = slice(start, start + tokens)
            dk_part = dot(dscore[:, block], queries[block], PLAIN) * score_scale
            dk_parts.append(dk_part.astype(BF16))
            dv_parts.append(dot(weight_low[:, block], upstream[block], PLAIN).astype(BF16))
        return dq_part, dk_parts, dv_parts

    for head, lanes in enumerate(head_lanes):
        dq_part, (dk_part,), (dv_part,) = attend(
            kn[:, lanes],
            vals[:, lanes],
            qn[:, lanes],
            ups[:, lanes],
            stats[0, head : head + 1, :],
            stats[1, head : head + 1, :],
        )
        dq_acc[:, lanes] = dq_part
        total[0, :, lanes] = dk_part.astype(F32)
        total[1, :, lanes] = dv_part.astype(F32)

    def own_scores(place):
        far_wait(place, False)
        used = jnp.full((kb, tokens), own_used[place], jnp.int32) > 0
        for head, lanes in enumerate(head_lanes):
            scores = dot(own_in[place, 0, :, lanes], qn[:, lanes], LAST) * score_scale
            weight = jnp.where(used, jnp.exp(scores - stats[1, head : head + 1, :]), 0.0)
            dweight = dot(own_in[place, 1, :, lanes], ups[:, lanes], LAST)
            dscore = (weight * (dweight - stats[0, head : head + 1, :])).astype(BF16)
            own_work[place, 0, head] = dscore
            own_work[place, 1, head] = weight.astype(BF16)
            own_out[place, 0, :, lanes] = (dot(dscore, qn[:, lanes], PLAIN) * score_scale).astype(BF16)
        fret_copy(place, False, 0).start()

    def own_rest(place):
        for head, lanes in enumerate(head_lanes):
            own_out[place, 1, :, lanes] = dot(own_work[place, 1, head], ups[:, lanes], PLAIN).astype(BF16)
            dq_acc[:, lanes] += dot(own_work[place, 0, head], own_in[place, 0, :, lanes], FIRST)

    def own_each(step, places):
        for place in places:

            @pl.when(own_here(place))
            def _(place=place):
                step(place)

    early_places, late_places = range(own_slots)[:1], range(own_slots)[1:]

    def stat_row(which, head):
        return jnp.concatenate([nbr_stats[side, which, head : head + 1, :] for side in sides], axis=1)

    own_each(own_scores, early_places)
    own_each(own_rest, early_places)
    for place in range(near_slots):

        @pl.when(near_here(place))
        def _(place=place):
            far_wait(place, True)

    near_rows = [
        jnp.concatenate(
            [jnp.full((kb, tokens), jnp.where(first == side, flag, 0), jnp.int32) for side in sides],
            axis=1,
        )
        for flag in near_used
    ]
    all_rows = jnp.ones((tokens, len(sides) * tokens), jnp.int32)
    side_mask = jnp.concatenate([all_rows] + near_rows, axis=0) > 0

    def with_near(own, which, lanes):
        near = near_in[:, which, :, lanes].reshape(near_slots * kb, hw)
        return jnp.concatenate([own[:, lanes], near], axis=0)

    for head, lanes in enumerate(head_lanes):
        for side in sides:

            @pl.when(exists[side])
            def _(side=side, head=head):
                for message in (0, 1, 2) if head == 0 else (2 + head,):
                    nbr_wait(side, message)

        dq_part, dk_parts, dv_parts = attend(
            with_near(kn, 0, lanes),
            with_near(vals, 1, lanes),
            nbr_q[:, :, lanes].reshape(len(sides) * tokens, hw),
            nbr_u[:, :, lanes].reshape(len(sides) * tokens, hw),
            stat_row(0, head),
            stat_row(1, head),
            side_mask,
        )
        ret_acc[:, :, lanes] = dq_part.reshape(len(sides), tokens, hw)
        for which, terms in enumerate((dk_parts, dv_parts)):
            acc = total[which, :, lanes]
            for term in terms:
                acc = acc + term[:tokens].astype(F32)
            total[which, :, lanes] = acc
            far_acc = terms[0][tokens:].astype(F32)
            for term in terms[1:]:
                far_acc = far_acc + term[tokens:].astype(F32)
            near_out[:, which, :, lanes] = far_acc.astype(BF16).reshape(near_slots, kb, hw)
        if head + 1 in (split, heads):
            ret_start_all(head // split)

    for place in range(near_slots):

        @pl.when(near_here(place))
        def _(place=place):
            fret_copy(place, True, 0).start()

    own_each(own_scores, late_places)
    own_each(own_rest, late_places)
    for place in range(near_slots):

        @pl.when(near_here(place))
        def _(place=place):
            fret_copy(place, True, 1).start()

    for place in range(own_slots):

        @pl.when(own_here(place))
        def _(place=place):
            fret_copy(place, False, 1).start()

    def add_early(which):
        for index, (tile, near) in enumerate(far_kinds):

            @pl.when(is_timed(tile, near, True))
            def _(index=index):
                fret_wait(index, which)
                for unit in range(UNITS):
                    picked = jnp.where(send_unit[index] == unit, send_used[index], 0)
                    spread = jnp.full((kb, width), picked, jnp.int32) > 0
                    total[which, unit * kb : (unit + 1) * kb, :] += jnp.where(
                        spread, fret_in[index, which].astype(F32), 0.0
                    )

    def add_late(which):
        late = [index for index, (_, near) in enumerate(far_kinds) if not near]
        for index in late:

            @pl.when(is_timed(*far_kinds[index], False))
            def _(index=index):
                fret_wait(index, which)

        pieces = []
        for unit in range(UNITS):
            acc = total[which, unit * kb : (unit + 1) * kb, :]
            for index in late:
                timed = is_timed(*far_kinds[index], False) & (send_unit[index] == unit)
                picked = jnp.where(timed, send_used[index], 0)
                spread = jnp.full((kb, width), picked, jnp.int32) > 0
                acc = acc + jnp.where(spread, fret_in[index, which].astype(F32), 0.0)
            pieces.append(acc)
        return jnp.concatenate(pieces, axis=0).astype(BF16)


    for side in sides:

        @pl.when(exists[side])
        def _(side=side):
            ret_wait(side)

    scale_rows = jnp.zeros((8, tokens), F32)
    for side in sides:
        for group in range(len(groups)):
            scale_rows = scale_rows + ret_scale_in[side, group]
    scales = to_columns(scale_rows)
    dq_groups = []
    for group, lanes in enumerate(groups):
        dq_sum = dq_acc[:, lanes]
        for side in sides:
            place = side * len(groups) + group
            coded = ret_in[side, :, lanes].astype(jnp.int32).astype(F32)
            dq_sum = dq_sum + coded * scales[:, place : place + 1]
        dq_groups.append(dq_sum)
    dq_sum = jnp.concatenate(dq_groups, axis=1)
    dq_norm = (dq_sum * score_scale).astype(BF16).astype(F32)
    query_wide = q_raw[...].astype(F32)
    weighted = gain_q * dq_norm
    x_start(1, lane_columns([(0, row_sums(weighted * query_wide))])[0:1])

    add_early(0)
    dk_norm = add_late(0).astype(F32)
    key_wide = k_raw[...].astype(F32)
    key_weighted = gain_k * dk_norm
    x_start(2, lane_columns([(0, row_sums(key_weighted * key_wide))])[0:1])

    q_factor = to_column(rates[0:1] * rates[0:1] * rates[0:1] * x_finish(1) / full_width)
    dq_out[0, 0] = (q_rate * weighted - query_wide * q_factor).astype(BF16)

    add_early(1)
    dv_out[0, 0] = add_late(1)
    for side in sides:

        @pl.when(exists[side])
        def _(side=side):
            for message in messages:
                nbr_copy(side, message).wait_send()
            for group in range(len(groups)):
                for which in range(2):
                    ret_copy(side, group, which).wait_send()

    for index, (tile, near) in enumerate(far_kinds):

        @pl.when(is_sent(tile, near))
        def _(index=index, tile=tile, near=near):
            far_copy(index, tile, near).wait_send()

    for place in range(near_slots):

        @pl.when(near_here(place))
        def _(place=place):
            for which in range(2):
                fret_copy(place, True, which).wait_send()

    for place in range(own_slots):

        @pl.when(own_here(place))
        def _(place=place):
            for which in range(2):
                fret_copy(place, False, which).wait_send()

    k_factor = to_column(rates[1:2] * rates[1:2] * rates[1:2] * x_finish(2) / full_width)
    dk_out[0, 0] = (k_rate * key_weighted - key_wide * k_factor).astype(BF16)


def copy_kernel(dq_in, dk_in, dv_in, dq_out, dk_out, dv_out, sem):
    pairs = ((dq_in, dq_out), (dk_in, dk_out), (dv_in, dv_out))
    copies = [
        pltpu.make_async_copy(source, target, sem.at[index])
        for index, (source, target) in enumerate(pairs)
    ]
    for copy in copies:
        copy.start()
    for copy in copies:
        copy.wait()


def body(sizes, q_raw, k_raw, values, upstream, outputs, logsumexp, gain_q, gain_k, far_list):
    rows, cols, parts = sizes
    tokens, width = q_raw.shape[2:]
    heads = logsumexp.shape[2]
    lse = logsumexp.transpose(0, 2, 1, 3)
    kb = tokens // UNITS
    stat_rows = -(-heads // 8) * 8
    sides = 2 + (1 if rows == 2 else 2 if rows > 2 else 0)
    near_slots = max((cols - 1) // 2, 1)
    own_slots = max(cols - 2, 1)
    kinds = max(2 * cols, 1)
    shape = jax.ShapeDtypeStruct(q_raw.shape, BF16)
    vmem = pl.BlockSpec(memory_space=pltpu.VMEM)
    anywhere = pl.BlockSpec(memory_space=pltpu.HBM)
    tile = pltpu.VMEM((tokens, width), BF16)
    near_units = pltpu.VMEM((near_slots, 2, kb, width), BF16)
    own_units = pltpu.VMEM((own_slots, 2, kb, width), BF16)
    dma = pltpu.SemaphoreType.DMA
    grads = pl.pallas_call(
        functools.partial(kernel, sizes),
        out_shape=(pltpu.VMEM(q_raw.shape, BF16),) * 3,
        in_specs=[anywhere] * 9,
        out_specs=(vmem,) * 3,
        scratch_shapes=[
            tile,
            tile,
            tile,
            tile,
            tile,
            tile,
            tile,
            pltpu.VMEM(lse.shape[1:], F32),
            pltpu.VMEM(gain_q.shape, BF16),
            pltpu.VMEM(gain_k.shape, BF16),
            pltpu.SMEM(far_list.shape, jnp.int32),
            pltpu.VMEM((2, stat_rows, tokens), F32),
            pltpu.VMEM((sides, 2, stat_rows, tokens), F32),
            pltpu.VMEM((tokens, width), F32),
            pltpu.VMEM((sides, tokens, width), BF16),
            pltpu.VMEM((sides, tokens, width), BF16),
            pltpu.VMEM((kinds, 2, kb, width), BF16),
            near_units,
            near_units,
            own_units,
            own_units,
            pltpu.VMEM((own_slots, 2, heads, kb, tokens), BF16),
            pltpu.VMEM((sides, tokens, width), F32),
            pltpu.VMEM((sides, tokens, width), jnp.int16),
            pltpu.VMEM((sides, tokens, width), jnp.int16),
            pltpu.VMEM((sides, 2, 8, tokens), F32),
            pltpu.VMEM((sides, 2, 8, tokens), F32),
            pltpu.VMEM((kinds, 2, kb, width), BF16),
            pltpu.VMEM((2, tokens, width), F32),
            pltpu.VMEM((3, parts, 8, 128), F32),
            dma((9,)),
            dma((sides, 2 + heads)),
            dma((sides, 2 + heads)),
            dma((kinds,)),
            dma((near_slots,)),
            dma((own_slots,)),
            dma((sides, 2, 2)),
            dma((sides, 2, 2)),
            dma((near_slots, 2)),
            dma((own_slots, 2)),
            dma((kinds, 2)),
            dma((3, parts)),
            dma((3, parts)),
        ],
        compiler_params=pltpu.CompilerParams(collective_id=0, has_side_effects=True),
    )(q_raw, k_raw, values, upstream, outputs, lse, gain_q, gain_k, far_list)
    return pl.pallas_call(
        copy_kernel,
        out_shape=(shape, shape, shape),
        in_specs=[vmem] * 3,
        out_specs=(anywhere,) * 3,
        scratch_shapes=[dma((3,))],
        compiler_params=pltpu.CompilerParams(vmem_limit_bytes=4 << 20),
    )(*grads)


def solution(mesh):
    sizes = (mesh.shape["ha"], mesh.shape["wa"], mesh.shape["hd"])
    tile = P("ha", "wa", None, "hd")
    return jax.shard_map(
        functools.partial(body, sizes),
        mesh=mesh,
        in_specs=(tile,) * 5 + (P("ha", "wa", "hd", None), P("hd"), P("hd"), P("ha", None, None)),
        out_specs=(tile,) * 3,
        check_vma=False,
    )
```
